128 devices in a mesh: slab: 32 (over z, x_lo, y), view: 4 (over x_hi, core).
Axes of the slice: x: 4 (x_hi: 2, x_lo: 2; x = x_hi * 2 + x_lo), y: 4, z: 4, core: 2. Of those that a mesh axis runs over, the one named last changes fastest.
Arguments:
- volume: float32 [128, 32, 128], P('slab', 'view'), may hold values from -6 to 6
- measured: float32 [4, 32, 4096], P('view', 'slab'), may hold values from -6 to 6
- dual_gain: float32 [4, 32, 4096], P('view', 'slab'), may hold values from 0.5 to 2
- pattern: int32 [4, 32, 64, 16], P(None, 'slab'), may hold values from 0 to 255
- angle: int32 [4, 32, 64], P(None, 'slab'), may hold values from 0 to 7
- response: bfloat16 [512, 1024], replicated, may hold values from -0.1875 to 0.1875
- w1: bfloat16 [9, 32, 6], replicated, may hold values from -0.875 to 0.875
- bias1: float32 [32], replicated, may hold values from -3 to 3
- w2: bfloat16 [9, 32, 96], replicated, may hold values from -0.21875 to 0.21875
- bias2: float32 [32], replicated, may hold values from -3 to 3
- w3: bfloat16 [9, 1, 96], replicated, may hold values from -0.21875 to 0.21875
- upstream: bfloat16 [128, 32, 128], P('slab', 'view'), may hold values from -6 to 6
Outputs:
- new_volume: float32 [128, 32, 128], P('slab', 'view')
- grad_volume: float32 [128, 32, 128], P('slab', 'view')
- grad_w1: float32 [9, 32, 6], replicated
- grad_bias1: float32 [32], replicated
- grad_w2: float32 [9, 32, 96], replicated
- grad_bias2: float32 [32], replicated
- grad_w3: float32 [9, 1, 96], replicated
The draws below stay inside these ranges and needn't reach their ends.
Inputs may be any that keep to these rules, and one draw needn't show every extreme that they name: `pattern`: tile numbers within the band, numbered as in the first step.
All inputs are finite; a program needn't handle non-finite values.
Results may differ from the reference program's by a relative error of at most 0.025.
Values may be sent and summed in bfloat16 or wider, within the bound.
A program may use at most 192 MiB of HBM per device.

```python
import math
import jax
import jax.numpy as jnp
import numpy as np
from jax import lax

CZ = 4
CY = 8
CX = 128
TILE = 64
CH = 32
K_TILES = 16
ANGLES = 8
DTILE = 64
BAND_TILES = 256
GROUPS = 4
BANDS = 32
DPIX = 4096
NZ = 128
NY = 32
NX = 128
VOXELS = 524288
N_SLAB = 32
N_VIEW = 4


def with_ends(entries, stream_key, least, largest):
    index_at = [jax.random.randint(jax.random.fold_in(stream_key, axis), (), 0, length) for axis, length in enumerate(entries.shape)]
    widest = entries.shape.index(max(entries.shape))
    beside = index_at[:widest] + [(index_at[widest] + 1) % entries.shape[widest]] + index_at[widest + 1:]
    return entries.at[tuple(index_at)].set(least).at[tuple(beside)].set(largest)


def steps_of(own_key, shape, split, low, high):
    loudness, own = 1.0, jax.random.fold_in(own_key, 6)
    for position, blocks in split:
        draws = jnp.exp(jax.random.uniform(jax.random.fold_in(own, position), (blocks,), jnp.float32, low / len(split), high / len(split)))
        loudness = loudness * jnp.repeat(draws, shape[position] // blocks).reshape([-1 if axis == position else 1 for axis in range(len(shape))])
    return loudness


def cumulative_ranks(count, lean):
    weights = [(1 << 20) // math.isqrt(standing ** lean) + 1 for standing in range(1, count + 1)]
    scale = 1 + sum(weights) // (1 << 30)
    return np.cumsum(np.array([max(1, weight // scale) for weight in weights]))


def ranked_ids(own_key, dims, count, lean):
    listing = cumulative_ranks(count, lean)
    lot = jax.random.randint(jax.random.fold_in(own_key, 1), dims, 0, int(listing[count - 1]))
    standing = jnp.searchsorted(jnp.asarray(listing, jnp.int32), lot, side="right")
    return jax.random.permutation(jax.random.fold_in(own_key, 2), count)[standing].astype(jnp.int32)


def bell_draw(own_key, dims, width, limit, cuts=(), held_as=jnp.bfloat16):
    level = steps_of(own_key, dims, cuts, -0.22, 0.18) if cuts else 1.0
    entries = jax.random.normal(own_key, dims, jnp.float32) * width * level
    return jnp.minimum(jnp.maximum(entries, -limit), limit).astype(held_as)


def setup_inputs(seed: int = 0) -> dict:
    seeds = jax.random.split(jax.random.key(seed), 13)
    volume = bell_draw(seeds[0], (NZ, NY, NX), 1.0, 6.0, ((0, 32), (1, 4)), jnp.float32)
    measured = bell_draw(seeds[1], (GROUPS, BANDS, DPIX), 1.0, 6.0, ((0, 4), (1, 32)), jnp.float32)
    dual_gain = jnp.clip(jnp.exp(math.log(2.0) - 1.3862944 * jax.random.uniform(seeds[2], (GROUPS, BANDS, DPIX), jnp.float32) ** steps_of(seeds[2], (GROUPS, BANDS, DPIX), ((0, 4), (1, 32)), -0.2, 0.2)), 0.5, 2.0)
    pattern = with_ends(ranked_ids(seeds[3], (GROUPS, BANDS, DTILE, K_TILES), BAND_TILES, 1), jax.random.fold_in(seeds[3], 3), 0, BAND_TILES - 1).astype(jnp.int32)
    angle = with_ends(jax.random.randint(seeds[4], (GROUPS, BANDS, DTILE), 0, ANGLES), jax.random.fold_in(seeds[4], 1), 0, ANGLES - 1).astype(jnp.int32)
    response = bell_draw(seeds[5], (ANGLES * TILE, K_TILES * TILE), (K_TILES * TILE) ** -0.5, 0.1875)
    w1 = bell_draw(seeds[6], (9, CH, 6), 54 ** -0.5, 0.875)
    bias1 = bell_draw(seeds[7], (CH,), 0.5, 3.0, (), jnp.float32)
    w2 = bell_draw(seeds[8], (9, CH, 3 * CH), (27 * CH) ** -0.5, 0.21875)
    bias2 = bell_draw(seeds[9], (CH,), 0.5, 3.0, (), jnp.float32)
    w3 = bell_draw(seeds[10], (9, 1, 3 * CH), (27 * CH) ** -0.5, 0.21875)
    upstream = bell_draw(seeds[11], (NZ, NY, NX), 1.0, 6.0, ((0, 32), (1, 4)))
    return dict(volume=volume, measured=measured, dual_gain=dual_gain, pattern=pattern, angle=angle, response=response, w1=w1, bias1=bias1, w2=w2, bias2=bias2, w3=w3, upstream=upstream)


def shift_x(source, offset):
    if offset == 0:
        return source
    zero_col = jnp.zeros(source.shape[:-1] + (1,), source.dtype)
    if offset == 1:
        return jnp.concatenate([source[..., 1:], zero_col], axis=-1)
    return jnp.concatenate([zero_col, source[..., :-1]], axis=-1)

def pad_field(field_in):
    return jnp.pad(field_in, ((0, 0), (1, 1), (1, 1), (0, 0)))

def stacked_plane(padded, depth_off, row_off, slab_depth, slab_height):
    slice_cut = padded[:, depth_off:depth_off + slab_depth, row_off:row_off + slab_height, :]
    return jnp.concatenate([shift_x(slice_cut, col_off - 1) for col_off in range(3)], axis=0)

def conv_apply(padded, weight):
    slab_depth = padded.shape[1] - 2
    slab_height = padded.shape[2] - 2
    accumulated = jnp.zeros((weight.shape[1], slab_depth, slab_height, padded.shape[3]), jnp.float32)
    for depth_off in range(3):
        for row_off in range(3):
            stacked = stacked_plane(padded, depth_off, row_off, slab_depth, slab_height).astype(jnp.float32)
            accumulated = accumulated + jnp.einsum('ok,kzyx->ozyx', weight[depth_off * 3 + row_off].astype(jnp.float32), stacked, precision=lax.Precision.HIGHEST)
    return accumulated

def conv_transpose(padded, weight):
    slab_depth = padded.shape[1] - 2
    slab_height = padded.shape[2] - 2
    channels = weight.shape[2] // 3
    accumulated = jnp.zeros((channels, slab_depth, slab_height, padded.shape[3]), jnp.float32)
    for depth_off in range(3):
        for row_off in range(3):
            slice_cut = padded[:, 2 - depth_off:2 - depth_off + slab_depth, 2 - row_off:2 - row_off + slab_height, :].astype(jnp.float32)
            partial_out = jnp.einsum('ok,ozyx->kzyx', weight[depth_off * 3 + row_off].astype(jnp.float32), slice_cut, precision=lax.Precision.HIGHEST)
            for col_off in range(3):
                accumulated = accumulated + shift_x(partial_out[col_off * channels:(col_off + 1) * channels], 1 - col_off)
    return accumulated

def weight_grad(grad_out, padded):
    slab_depth = padded.shape[1] - 2
    slab_height = padded.shape[2] - 2
    grad_f32 = grad_out.astype(jnp.float32)
    pieces = []
    for depth_off in range(3):
        for row_off in range(3):
            stacked = stacked_plane(padded, depth_off, row_off, slab_depth, slab_height).astype(jnp.float32)
            pieces.append(jnp.einsum('ozyx,kzyx->ok', grad_f32, stacked, precision=lax.Precision.HIGHEST))
    return jnp.stack(pieces)

def silu_slope(values):
    sigma = jax.nn.sigmoid(values)
    return sigma * (1.0 + values * (1.0 - sigma))

def project_rows(tile_rows, tile_ids, angle_ids, response):
    row_count = tile_ids.shape[0]
    angles = response.shape[0] // 64
    picked = jnp.take(tile_rows, tile_ids.reshape(-1), axis=0).reshape(row_count, -1)
    spread = jnp.dot(picked, response.T, preferred_element_type=jnp.float32).reshape(row_count, angles, 64)
    onehot = (angle_ids[:, None] == jnp.arange(angles, dtype=jnp.int32)[None, :]).astype(spread.dtype)
    return lax.optimization_barrier(jnp.sum(spread * onehot[:, :, None], axis=1))

def backproject_rows(dual_rows, angle_ids, response):
    row_count = dual_rows.shape[0]
    angles = response.shape[0] // 64
    onehot = (angle_ids[:, None] == jnp.arange(angles, dtype=jnp.int32)[None, :]).astype(dual_rows.dtype)
    expanded = (onehot[:, :, None] * dual_rows[:, None, :]).reshape(row_count, angles * 64)
    contrib = jnp.dot(expanded, response, preferred_element_type=jnp.float32)
    return contrib.reshape(row_count * (response.shape[1] // 64), 64)

def tiles_of(field_in):
    blocks = field_in.reshape(N_SLAB, CZ // 4, 4, N_VIEW, CY // 4, 4, CX // 4, 4)
    blocks = blocks.transpose(0, 3, 1, 4, 6, 2, 5, 7)
    return blocks.reshape(N_SLAB, BAND_TILES, 64)

def field_of(tile_bands):
    blocks = tile_bands.reshape(N_SLAB, N_VIEW, CZ // 4, CY // 4, CX // 4, 4, 4, 4)
    blocks = blocks.transpose(0, 2, 5, 1, 3, 6, 4, 7)
    return blocks.reshape(NZ, NY, NX)

def reference(volume, measured, dual_gain, pattern, angle, response, w1, bias1, w2, bias2, w3, upstream):
    pattern_bands = jnp.swapaxes(pattern, 0, 1)
    angle_bands = jnp.swapaxes(angle, 0, 1)

    def project(field_bf):
        tile_bands = tiles_of(field_bf)

        def one_band(operands):
            band_tiles, band_pattern, band_angle = operands
            out_rows = project_rows(band_tiles, band_pattern.reshape(-1, K_TILES), band_angle.reshape(-1), response)
            return out_rows.reshape(GROUPS, DPIX)
        return jnp.swapaxes(lax.map(one_band, (tile_bands, pattern_bands, angle_bands)), 0, 1)

    def backproject(dual_field):

        def one_band(operands):
            band_dual, band_pattern, band_angle = operands
            contrib = backproject_rows(band_dual.reshape(-1, 64), band_angle.reshape(-1), response)
            return jax.ops.segment_sum(contrib, band_pattern.reshape(-1), num_segments=BAND_TILES)
        sums = lax.map(one_band, (jnp.swapaxes(dual_field, 0, 1), pattern_bands, angle_bands))
        return field_of(sums)
    projection = project(volume.astype(jnp.bfloat16))
    dual_field = (dual_gain * (projection - measured)).astype(jnp.bfloat16)
    back_field = backproject(dual_field)
    inputs = jnp.stack([volume, back_field]).astype(jnp.bfloat16)
    inputs_pad = pad_field(inputs)
    first_pre = conv_apply(inputs_pad, w1) + bias1[:, None, None, None]
    hidden_one = jax.nn.silu(first_pre).astype(jnp.bfloat16)
    hidden_one_pad = pad_field(hidden_one)
    second_pre = conv_apply(hidden_one_pad, w2) + bias2[:, None, None, None]
    hidden_two = jax.nn.silu(second_pre).astype(jnp.bfloat16)
    hidden_two_pad = pad_field(hidden_two)
    new_volume = volume + conv_apply(hidden_two_pad, w3)[0]
    grad_scale = 1.0 / math.sqrt(VOXELS)
    upward = upstream[None]
    slope_two = (conv_transpose(pad_field(upward), w3) * silu_slope(second_pre)).astype(jnp.bfloat16)
    slope_one = (conv_transpose(pad_field(slope_two), w2) * silu_slope(first_pre)).astype(jnp.bfloat16)
    back_grad = conv_transpose(pad_field(slope_one), w1)
    echo = (dual_gain * project(back_grad[1].astype(jnp.bfloat16))).astype(jnp.bfloat16)
    grad_volume = upstream.astype(jnp.float32) + back_grad[0] + backproject(echo)
    grad_w3 = weight_grad(upward, hidden_two_pad) * grad_scale
    grad_w2 = weight_grad(slope_two, hidden_one_pad) * grad_scale
    grad_bias2 = lax.optimization_barrier(jnp.sum(slope_two.astype(jnp.float32), axis=(1, 2, 3))) * grad_scale
    grad_w1 = weight_grad(slope_one, inputs_pad) * grad_scale
    grad_bias1 = lax.optimization_barrier(jnp.sum(slope_one.astype(jnp.float32), axis=(1, 2, 3))) * grad_scale
    return (new_volume, grad_volume, grad_w1, grad_bias1, grad_w2, grad_bias2, grad_w3)
```

```python
import functools
import math

import jax
import jax.numpy as jnp
import ml_dtypes
import numpy as np
from jax import lax
from jax.experimental import pallas as pl
from jax.experimental.pallas import tpu as pltpu
from jax.sharding import PartitionSpec as P

F32 = jnp.float32
BF16 = jnp.bfloat16
MESH = pl.DeviceIdType.MESH
VIEWS = 4
RING = 8
LAYERS = 4
SLABS = RING * LAYERS
PIECE = 5
VMEM_BYTES = 50 * 1024 * 1024


def mm(a, b):
    return lax.dot_general(a, b, (((1,), (0,)), ((), ())), preferred_element_type=F32)


def mmt(a, b):
    return lax.dot_general(a, b, (((1,), (1,)), ((), ())), preferred_element_type=F32)


def iota(shape, dim):
    return lax.broadcasted_iota(jnp.int32, shape, dim)


def one(cond):
    return jnp.where(cond, 1.0, 0.0).astype(BF16)


def host_bf16(cond):
    return np.asarray(cond, np.float32).astype(ml_dtypes.bfloat16)


def tile_constants():
    row, col = np.arange(128)[:, None], np.arange(128)[None, :]
    pick_x = host_bf16(col == 4 * (row % 32) + row // 32)
    r, c = np.arange(512)[:, None], np.arange(1024)[None, :]
    xi, quarter, z, y8 = r // 128, r // 32 % 4, r // 8 % 4, r % 8
    yt, j = c // 128, c % 64
    place = host_bf16(
        (2 * quarter + y8 // 4 == yt) & (z == j // 16) & (y8 % 4 == j // 4 % 4) & (xi == j % 4)
    )
    r, c = np.arange(64)[:, None], np.arange(128)[None, :]
    pick_j = host_bf16((c < 64) & (c % 4 == r // 16) & (c // 4 == r % 16))
    r, c = np.arange(512)[:, None], np.arange(512)[None, :]
    spread_x = host_bf16((r // 32 % 4 == c // 128) & (c % 128 == 4 * (r % 32) + r // 128))
    return pick_x, place, pick_j, spread_x


def weight_constants():
    lane = np.arange(384)
    band1 = np.zeros((9, 6, 384), np.float32)
    for a in range(3):
        for b in range(3):
            for e in range(3):
                for c in range(2):
                    band1[3 * a + b, 2 * e + c, ((a * 2 + c) * 3 + e) * 16 + b] = 1.0
    band3 = np.zeros((3, 9, 256), np.float32)
    for a in range(3):
        for b in range(3):
            for e in range(3):
                band3[e, 3 * (2 - a) + (2 - b), (a * 3 + e) * 16 + b] = 1.0
    rep3 = np.zeros((3, 96, 384), np.float32)
    for e in range(3):
        rep3[e, 32 * e + lane % 32, lane] = 1.0
    fold1 = np.zeros((384, 1152), np.float32)
    for a in range(3):
        for b in range(3):
            for e in range(3):
                for c in range(2):
                    fold1[
                        ((a * 2 + c) * 3 + e) * 16 + 3 + b, 128 * (3 * a + b) + 97 + 2 * e + c
                    ] = 1.0
    fold1[288, 103] = 1.0
    fold3 = np.zeros((3, 384, 128), np.float32)
    for e in range(3):
        live = lane[lane < 320]
        fold3[e, live, 32 * e + live % 32] = 1.0
    return tuple(host_bf16(x) for x in (band1, band3, rep3, fold1, fold3))


def own_order():
    return one(iota((64, 64), 1) == 2 * (iota((64, 64), 0) % 32) + iota((64, 64), 0) // 32)


def view_choice(pattern_ref, angle_ref, member):
    order = own_order()
    ids = mm(order, pattern_ref[member].astype(F32).astype(BF16)).astype(jnp.int32)
    lanes = iota((64, 256), 1)
    choice = jnp.concatenate([one(lanes == ids[:, k : k + 1]) for k in range(16)], axis=0)
    angles = mmt(order, angle_ref[...].astype(F32).astype(BF16)).astype(jnp.int32)
    mine = jnp.sum(jnp.where(iota((64, 4), 1) == member, angles, 0), axis=1, keepdims=True)
    return choice, mine


def band_choice(pattern_ref, angle_ref, first, count):
    order = own_order()
    rows = jnp.concatenate(
        [mm(order, pattern_ref[g].astype(F32).astype(BF16)) for g in range(VIEWS)], axis=0
    )
    eye = one(iota((16, 16), 0) == iota((16, 16), 1))
    ids = mmt(eye, rows.astype(BF16)).astype(jnp.int32)
    tile = iota((count, 256), 0) + first
    even = jnp.concatenate([one(tile == ids[k : k + 1, :]) for k in range(0, 16, 2)], axis=1)
    odd = jnp.concatenate([one(tile == ids[k : k + 1, :]) for k in range(1, 16, 2)], axis=1)
    angles = mmt(order, angle_ref[...].astype(F32).astype(BF16)).astype(jnp.int32)
    column = jnp.concatenate([angles[:, g : g + 1] for g in range(VIEWS)], axis=0)
    return jnp.concatenate([even, odd], axis=0), column


def project(field_rows, choice, angles, response_ref, pick_x_ref, place_ref):
    by_x = mmt(pick_x_ref[...], field_rows).astype(BF16)
    wide = jnp.concatenate([by_x[32 * i : 32 * i + 32] for i in range(4)], axis=1)
    spread = mm(wide, place_ref[...]).astype(BF16)
    tiles = jnp.concatenate([spread[:, 128 * i : 128 * i + 128] for i in range(8)], axis=0)
    picked = mm(choice, tiles)
    low = iota((64, 128), 1) < 64
    pairs = [
        jnp.where(low, picked[128 * p : 128 * p + 64], picked[128 * p + 64 : 128 * p + 128])
        for p in range(8)
    ]
    lines = mmt(jnp.concatenate(pairs, axis=1).astype(BF16), response_ref[...])
    half = iota((64, 128), 1) // 64
    total = jnp.zeros((64, 128), F32)
    for p in range(4):
        total = total + jnp.where(angles == 2 * p + half, lines[:, 128 * p : 128 * p + 128], 0.0)
    total = total + pltpu.roll(total, 64, 1)
    return jnp.where(low[:32], total[:32], total[32:])


def backproject(rows_ref, chosen, angles, response_ref, pick_j_ref, spread_x_ref, count):
    low = iota((32, 128), 1) < 64
    parts = []
    for g in range(VIEWS):
        rows = rows_ref[g].astype(F32)
        turned = pltpu.roll(rows, 64, 1)
        parts.append(jnp.where(low, rows, turned))
        parts.append(jnp.where(low, turned, rows))
    doubled = jnp.concatenate(parts, axis=0)
    half = iota((256, 128), 1) // 64
    masked = [
        jnp.where(angles == 2 * p + half, doubled, 0.0).astype(BF16) for p in range(4)
    ]
    contrib = mm(jnp.concatenate(masked, axis=1), response_ref[...])
    high = contrib.astype(BF16)
    rest = (contrib - high.astype(F32)).astype(BF16)
    stacked = jnp.concatenate(
        [
            jnp.concatenate(
                [high[:, 128 * p : 128 * p + 128], rest[:, 128 * p : 128 * p + 128]], axis=1
            )
            for p in range(8)
        ],
        axis=0,
    )
    sums = mm(chosen, stacked)
    sums = sums[:, :128] + sums[:, 128:]
    tiles = sums[:count] + pltpu.roll(sums[count:], 64, 1)
    top = tiles.astype(BF16)
    if count == 64:
        top = jnp.concatenate([top, (tiles - top.astype(F32)).astype(BF16)], axis=0)
    by_j = mmt(pick_j_ref[...], top).astype(BF16)
    wide = jnp.concatenate([by_j[16 * i : 16 * i + 16] for i in range(4)], axis=1)
    return mm(wide, spread_x_ref[...])


def gather_view(source, slots, member, sems, start_only=True):
    copies = []
    for off in range(1, VIEWS):
        copies.append(
            pltpu.make_async_remote_copy(
                src_ref=source,
                dst_ref=slots.at[member],
                send_sem=sems.at[0, off],
                recv_sem=sems.at[1, off],
                device_id={"view": lax.rem(member + off, VIEWS)},
                device_id_type=MESH,
            )
        )
    for copy in copies:
        copy.start()
    return copies


def wait_all(copies):
    for copy in copies:
        copy.wait()


def greet(peers):
    barrier = pltpu.get_barrier_semaphore()
    for peer in peers:
        pl.semaphore_signal(barrier, inc=1, device_id=peer, device_id_type=MESH)
    pl.semaphore_wait(barrier, len(peers))


def ahead_kernel(
    volume_ref,
    upstream_ref,
    measured_ref,
    gain_ref,
    pattern_ref,
    angle_ref,
    response_ref,
    pick_x_ref,
    place_ref,
    pick_j_ref,
    spread_x_ref,
    fields_ref,
    ups,
    slots,
    rows,
    gather_sems,
    slab_sems,
):
    slab, member = lax.axis_index("slab"), lax.axis_index("view")
    above, below = lax.rem(slab + 1, SLABS), lax.rem(slab + SLABS - 1, SLABS)
    ups[...] = upstream_ref[...].astype(F32)
    slots[0, member] = volume_ref[...]
    slots[1, member] = ups[...]
    greet(
        [{"view": lax.rem(member + off, VIEWS)} for off in range(1, VIEWS)]
        + [{"slab": above}, {"slab": below}]
    )
    volume_copies = gather_view(volume_ref, slots.at[0], member, gather_sems.at[0])
    ups_copies = gather_view(ups, slots.at[1], member, gather_sems.at[1])
    choice, angles = view_choice(pattern_ref, angle_ref, member)
    wait_all(volume_copies)
    field_rows = slots[0].reshape(128, 128).astype(BF16)
    lines = project(field_rows, choice, angles, response_ref, pick_x_ref, place_ref)
    dual = (gain_ref[...] * (lines - measured_ref[...])).astype(BF16)
    rows[member] = dual
    dual_copies = gather_view(rows.at[member], rows, member, gather_sems.at[2])

    def to_slabs(field):
        copies = []
        for side, peer, start in ((0, above, 0), (1, below, 8)):
            copies.append(
                pltpu.make_async_remote_copy(
                    src_ref=fields_ref.at[field, pl.ds(4, 4)],
                    dst_ref=fields_ref.at[field, pl.ds(start, 4)],
                    send_sem=slab_sems.at[0, field, side],
                    recv_sem=slab_sems.at[1, field, side],
                    device_id={"slab": peer},
                    device_id_type=MESH,
                )
            )
        for copy in copies:
            copy.start()
        return copies

    wait_all(ups_copies)
    left, right = lax.rem(member + VIEWS - 1, VIEWS), lax.rem(member + 1, VIEWS)
    for field in range(2):
        fields_ref[field, 4:8, 4:12, :] = slots[field, member]
        fields_ref[field, 4:8, 0:4, :] = slots[field, left, :, 4:8, :]
        fields_ref[field, 4:8, 12:16, :] = slots[field, right, :, 0:4, :]
    plane_copies = to_slabs(0) + to_slabs(1)
    chosen, columns = band_choice(pattern_ref, angle_ref, 64 * member - 32, 128)
    wait_all(dual_copies)
    spread = backproject(rows, chosen, columns, response_ref, pick_j_ref, spread_x_ref, 128)
    for z in range(4):
        for yt in range(4):
            fields_ref[2, 4 + z, 4 * yt : 4 * yt + 4, :] = spread[
                4 * z : 4 * z + 4, 128 * yt : 128 * yt + 128
            ]
    back_copies = to_slabs(2)
    wait_all(plane_copies)
    wait_all(back_copies)


def shifted(value, e, lane):
    if e == 1:
        return value
    if e == 0:
        return jnp.where(lane == 0, 0.0, pltpu.roll(value, 1, 1))
    return jnp.where(lane == 127, 0.0, pltpu.roll(value, 127, 1))


def conv_kernel(
    fields_ref,
    w1_ref,
    bias1_ref,
    w2_ref,
    bias2_ref,
    w3_ref,
    band1_ref,
    band3_ref,
    rep3_ref,
    fold1_ref,
    fold3_ref,
    new_ref,
    back_ref,
    sums_ref,
    ins,
    ups,
    ups_own,
    t1,
    t3t,
    t3,
    t1t,
    w2r,
    w2t,
    pre1,
    h3,
    ct3,
    h2,
    s3,
    s2z,
    s1,
    g2,
    g3,
):
    slab, member = lax.axis_index("slab"), lax.axis_index("view")
    low_z, low_y = 4 * slab - 4, 8 * member - 4
    depth, height = 4 * SLABS, 8 * VIEWS

    base = jnp.zeros((32, 384), F32)
    for tap in range(9):
        base = base + mm(w1_ref[tap], band1_ref[tap])
    for yo in range(14):
        t1[32 * yo : 32 * yo + 32, :] = (pltpu.roll(base, yo, 1) if yo else base).astype(BF16)
    eye96 = one(iota((96, 96), 0) == iota((96, 96), 1))
    w3 = w3_ref[...]
    w3_turned = mmt(eye96, w3).astype(BF16)
    base3 = jnp.zeros((32, 256), F32)
    for e in range(3):
        base3 = base3 + mm(w3_turned[32 * (2 - e) : 32 * (2 - e) + 32], band3_ref[e])
    for yo in range(12):
        t3t[32 * yo : 32 * yo + 32, :] = pltpu.roll(base3, yo + 1, 1).astype(BF16)
    step = iota((8, 384), 1) // 32 - iota((8, 384), 0)
    for e in range(3):
        line = mm(w3, rep3_ref[e])
        for a in range(3):
            block = jnp.zeros((8, 384), F32)
            for b in range(3):
                block = block + jnp.where(step == b, line[3 * a + b : 3 * a + b + 1, :], 0.0)
            t3[8 * (3 * a + e) : 8 * (3 * a + e) + 8, :] = block
    eye6 = one(iota((8, 6), 0) == iota((8, 6), 1))
    turned = [
        mmt(eye6, jnp.concatenate([w1_ref[tap]] * 12, axis=0)) for tap in range(9)
    ]
    for a in range(3):
        for c in range(2):
            for e in range(3):
                row = 2 * (2 - e) + c
                block = jnp.zeros((8, 384), F32)
                for b in range(3):
                    tap = 3 * (2 - a) + (2 - b)
                    block = block + jnp.where(step == b, turned[tap][row : row + 1, :], 0.0)
                at = 8 * ((a * 2 + c) * 3 + e)
                t1t[at : at + 8, :] = block
    wide = mm(
        jnp.concatenate([w2_ref[tap] for tap in range(9)], axis=0),
        one(iota((96, 128), 0) == iota((96, 128), 1)),
    )
    keep = iota((128, 128), 1) // 32 == 2 - iota((128, 128), 0) // 32
    towers = []
    for tap in range(9):
        piece = wide[32 * tap : 32 * tap + 32]
        a, b = tap // 3, tap % 3
        w2r[32 * a : 32 * a + 32, 128 * b : 128 * b + 128] = piece.astype(BF16)
        towers.append(
            jnp.where(keep, jnp.concatenate([piece] * 4, axis=0), 0.0).astype(BF16)
        )
    across = mmt(
        one(iota((32, 128), 0) == iota((32, 128), 1) % 32), jnp.concatenate(towers, axis=0)
    ).astype(BF16)
    for a in range(3):
        for b in range(3):
            tap = 3 * (2 - a) + (2 - b)
            w2t[32 * a : 32 * a + 32, 128 * b : 128 * b + 128] = across[
                :, 128 * tap : 128 * tap + 128
            ]
    eye32 = iota((32, 32), 0) == iota((32, 32), 1)
    bias1 = jnp.sum(jnp.where(eye32, bias1_ref[...], 0.0), axis=1, keepdims=True)
    bias2 = jnp.sum(jnp.where(eye32, bias2_ref[...], 0.0), axis=1, keepdims=True)

    lane16 = iota((16, 128), 1)
    global_y = iota((16, 128), 0) + low_y
    inside_y = (global_y >= 0) & (global_y < height)
    lane8 = iota((8, 128), 1)

    def prepare(z, carry):
        inside = inside_y & (z + low_z >= 0) & (z + low_z < depth)
        for c, field in ((0, 0), (1, 2)):
            plane = jnp.where(inside, fields_ref[field, z], 0.0)
            plane = plane.astype(BF16).astype(F32)
            for e in range(3):
                at = (c * 3 + e) * 16
                ins[z, at : at + 16, :] = shifted(plane, e, lane16).astype(BF16)
        plane = jnp.where(inside, fields_ref[1, z], 0.0)
        for e in range(3):
            ups[z, 16 * e : 16 * e + 16, :] = shifted(plane, e, lane16).astype(BF16)
        return carry

    lax.fori_loop(0, 12, prepare, 0)
    ups_own[...] = jnp.zeros(ups_own.shape, F32)
    for z in range(4):
        plane = fields_ref[1, 4 + z, 4:12, :]
        for e in range(3):
            ups_own[2 + z, e] = shifted(plane, 2 - e, lane8)

    def pair_of(ref, z, count):
        cols = [
            jnp.concatenate([ref[z + n + a] for a in range(count)], axis=0) for n in range(2)
        ]
        return jnp.concatenate(cols, axis=1)

    def first(p, carry):
        z = 2 * p
        out = mm(t1[:, :288], pair_of(ins, z, 3))
        pre1[z] = out[:, :128]
        pre1[z + 1] = out[:, 128:]
        return carry

    lax.fori_loop(0, 5, first, 0)

    lane448 = iota((448, 128), 1)
    row_y1 = iota((448, 128), 0) // 32 + low_y + 1
    inside1 = (row_y1 >= 0) & (row_y1 < height)
    bias1_rows = jnp.concatenate([jnp.broadcast_to(bias1, (32, 128))] * 14, axis=0)

    def activate(z, carry):
        value = pre1[z] + bias1_rows
        gate = 0.5 * jnp.tanh(0.5 * value) + 0.5
        act = value * gate
        pre1[z] = gate + act * (1.0 - gate)
        inside = inside1 & (z + low_z + 1 >= 0) & (z + low_z + 1 < depth)
        act = jnp.where(inside, act, 0.0)
        for e in range(3):
            h3[z, :, 32 * e : 32 * e + 32, :] = (
                shifted(act, e, lane448).astype(BF16).reshape(14, 32, 128)
            )
        h3[z, :, 96:128, :] = jnp.ones((14, 32, 128), BF16)
        return carry

    lax.fori_loop(0, 10, activate, 0)

    def third_turned(p, carry):
        z = 2 * p
        out = mm(t3t[:, :144], pair_of(ups, z + 1, 3))
        ct3[z] = out[:, :128]
        ct3[z + 1] = out[:, 128:]
        return carry

    lax.fori_loop(0, 4, third_turned, 0)

    lane32 = iota((32, 128), 1)
    s2z[...] = jnp.zeros(s2z.shape, BF16)

    def stacked_rows(ref, z, y):
        cols = [ref[z + n, pl.ds(y, 3)].reshape(384, 128) for n in range(2)]
        return jnp.concatenate(cols, axis=1)

    def second(y, carry):
        outs = [mm(w2r[...], stacked_rows(h3, 2 * p, y)) for p in range(5)]
        parts = [outs[z // 2][:, 128 * (z % 2) : 128 * (z % 2) + 128] for z in range(10)]
        ok_y = (y + low_y + 2 >= 0) & (y + low_y + 2 < height)
        at = pl.multiple_of(32 * y, 32)
        for z in range(8):
            value = parts[z][:32] + parts[z + 1][32:64] + parts[z + 2][64:] + bias2
            gate = 0.5 * jnp.tanh(0.5 * value) + 0.5
            act = value * gate
            slope = gate + act * (1.0 - gate)
            ok = ok_y & (z + low_z + 2 >= 0) & (z + low_z + 2 < depth)
            live = jnp.where(ok, 1.0, 0.0)
            h2[z, pl.ds(at, 32), :] = (act * live).astype(BF16)
            slope = slope * ct3[z, pl.ds(at, 32), :] * live
            for e in range(3):
                s3[z, y, 32 * e : 32 * e + 32, :] = shifted(slope, e, lane32).astype(BF16)
            s3[z, y, 96:128, :] = jnp.zeros((32, 128), BF16)
        return carry

    lax.fori_loop(0, 12, second, 0)
    for z in range(2, 6):
        s2z[z] = s3[z, 2:10, 32:64, :]

    g2[...] = jnp.zeros(g2.shape, F32)

    def second_grad(y, carry):
        left = jnp.concatenate(
            [
                jnp.concatenate([s2z[z - a, y] for z in range(2, 8)], axis=1)
                for a in range(3)
            ],
            axis=0,
        )
        right = jnp.concatenate(
            [h3[z, pl.ds(y + 2, 3)].reshape(384, 128) for z in range(2, 8)], axis=1
        )
        g2[...] += mmt(left, right)
        return carry

    lax.fori_loop(0, 8, second_grad, 0)

    def second_turned(y, carry):
        outs = [mm(w2t[...], stacked_rows(s3, 2 * p, y)) for p in range(4)]
        parts = [outs[z // 2][:, 128 * (z % 2) : 128 * (z % 2) + 128] for z in range(8)]
        ok_y = (y + low_y + 3 >= 0) & (y + low_y + 3 < height)
        at = pl.multiple_of(32 * y, 32)
        from_ = pl.multiple_of(32 * y + 64, 32)
        for z in range(6):
            value = parts[z][:32] + parts[z + 1][32:64] + parts[z + 2][64:]
            ok = ok_y & (z + low_z + 3 >= 0) & (z + low_z + 3 < depth)
            live = jnp.where(ok, 1.0, 0.0)
            value = value * pre1[z + 2, pl.ds(from_, 32), :] * live
            s1[z, pl.ds(at, 32), :] = value.astype(BF16)
        return carry

    lax.fori_loop(0, 10, second_turned, 0)

    t1t_now = t1t[:, :320].astype(BF16)
    outs = [mm(t1t_now, jnp.concatenate([s1[2 * p], s1[2 * p + 1]], axis=1)) for p in range(3)]
    for c in range(2):
        for z in range(4):
            for e in range(3):
                total = jnp.zeros((8, 128), F32)
                for a in range(3):
                    zi = z + a
                    at = 8 * ((a * 2 + c) * 3 + e)
                    total = total + outs[zi // 2][
                        at : at + 8, 128 * (zi % 2) : 128 * (zi % 2) + 128
                    ]
                total = shifted(total, e, lane8)
                if e == 0:
                    back_ref[c, z] = total
                else:
                    back_ref[c, z] += total

    t3_now = t3[:, :320].astype(BF16)
    outs = [
        mm(t3_now, jnp.concatenate([h2[z, 32:352, :], h2[z + 1, 32:352, :]], axis=1))
        for z in (1, 3, 5)
    ]
    for z in range(4):
        total = fields_ref[0, 4 + z, 4:12, :]
        for e in range(3):
            part = jnp.zeros((8, 128), F32)
            for a in range(3):
                zi = z + a
                at = 8 * (3 * a + e)
                part = part + outs[zi // 2][at : at + 8, 128 * (zi % 2) : 128 * (zi % 2) + 128]
            total = total + shifted(part, e, lane8)
        new_ref[z] = total

    left = jnp.concatenate(
        [
            jnp.concatenate(
                [ups_own[z + 1 - a, e] for a in range(3) for e in range(3)], axis=0
            ).astype(BF16)
            for z in range(1, 7)
        ],
        axis=1,
    )
    right = jnp.concatenate([h2[z, 32:352, :] for z in range(1, 7)], axis=1)
    cross = mmt(left, right)
    step10 = iota((8, 320), 1) // 32 - iota((8, 320), 0)
    g3[...] = jnp.zeros(g3.shape, F32)
    for a in range(3):
        for e in range(3):
            block = cross[8 * (3 * a + e) : 8 * (3 * a + e) + 8]
            for b in range(3):
                g3[e, 3 * a + b : 3 * a + b + 1, 0:320] = jnp.sum(
                    jnp.where(step10 == b, block, 0.0), axis=0, keepdims=True
                )
    third = jnp.zeros((16, 128), F32)
    for e in range(3):
        value = g3[e]
        high = value.astype(BF16)
        rest = (value - high.astype(F32)).astype(BF16)
        third = third + mm(high, fold3_ref[e]) + mm(rest, fold3_ref[e])

    left = jnp.concatenate([s1[z, 32:288, :] for z in range(1, 5)], axis=1)
    right = jnp.concatenate(
        [
            jnp.concatenate(
                [ins[z + 3 + a] for a in range(3)] + [jnp.ones((96, 128), BF16)], axis=0
            )
            for z in range(4)
        ],
        axis=1,
    )
    cross = mmt(left, right)
    total = cross[:32]
    for yo in range(1, 8):
        total = total + pltpu.roll(cross[32 * yo : 32 * yo + 32], 384 - yo, 1)
    high = total.astype(BF16)
    rest = (total - high.astype(F32)).astype(BF16)
    first_grads = mm(high, fold1_ref[...]) + mm(rest, fold1_ref[...])

    lane_keep = iota((32, 128), 1) < 97
    for tap in range(9):
        a, b = tap // 3, tap % 3
        block = jnp.where(
            lane_keep, g2[32 * a : 32 * a + 32, 128 * b : 128 * b + 128], 0.0
        ) + first_grads[:, 128 * tap : 128 * tap + 128]
        sums_ref[4 * tap : 4 * tap + 4] = block.reshape(4, 8, 128)
    sums_ref[36:38] = third.reshape(2, 8, 128)
    sums_ref[38:40] = jnp.zeros((2, 8, 128), F32)


def behind_kernel(
    back_ref,
    upstream_ref,
    gain_ref,
    pattern_ref,
    angle_ref,
    response_ref,
    pick_x_ref,
    place_ref,
    pick_j_ref,
    spread_x_ref,
    sums_ref,
    grad_ref,
    total_ref,
    slots,
    rows,
    ring_in,
    view_in,
    layer_in,
    gather_sems,
    ring_sems,
    view_sems,
    layer_sems,
    final_sems,
):
    slab, member = lax.axis_index("slab"), lax.axis_index("view")
    place, layer = lax.rem(slab, RING), lax.div(slab, RING)
    ring_peers = [layer * RING + lax.rem(place + off, RING) for off in range(1, RING)]
    layer_peers = [
        lax.rem(layer + off, LAYERS) * RING + place for off in range(1, LAYERS)
    ]
    slots[member] = back_ref[1]
    greet(
        [{"view": lax.rem(member + off, VIEWS)} for off in range(1, VIEWS)]
        + [{"slab": peer} for peer in ring_peers]
        + [{"slab": peer} for peer in layer_peers]
    )
    field_copies = gather_view(back_ref.at[1], slots, member, gather_sems.at[0])

    def to_peers(source_of, target, axis, peers, sems):
        copies = []
        for n, peer in enumerate(peers):
            copies.append(
                pltpu.make_async_remote_copy(
                    src_ref=source_of(n),
                    dst_ref=target,
                    send_sem=sems.at[0, n],
                    recv_sem=sems.at[1, n],
                    device_id={axis: peer},
                    device_id_type=MESH,
                )
            )
        for copy in copies:
            copy.start()
        return copies

    ring_copies = to_peers(
        lambda n: sums_ref.at[pl.ds(PIECE * lax.rem(place + n + 1, RING), PIECE)],
        ring_in.at[place],
        "slab",
        ring_peers,
        ring_sems,
    )
    ring_in[place] = sums_ref[pl.ds(PIECE * place, PIECE)]
    choice, angles = view_choice(pattern_ref, angle_ref, member)
    wait_all(field_copies)
    field_rows = slots[...].reshape(128, 128).astype(BF16)
    lines = project(field_rows, choice, angles, response_ref, pick_x_ref, place_ref)
    rows[member] = (gain_ref[...] * lines).astype(BF16)
    echo_copies = gather_view(rows.at[member], rows, member, gather_sems.at[1])

    def add_up(ref, count):
        total = ref[0]
        for n in range(1, count):
            total = total + ref[n]
        return total

    wait_all(ring_copies)
    view_in[member] = add_up(ring_in, RING)
    view_copies = to_peers(
        lambda n: view_in.at[member],
        view_in.at[member],
        "view",
        [lax.rem(member + off, VIEWS) for off in range(1, VIEWS)],
        view_sems,
    )
    chosen, columns = band_choice(pattern_ref, angle_ref, 64 * member, 64)
    wait_all(view_copies)
    layer_in[layer] = add_up(view_in, VIEWS)
    layer_copies = to_peers(
        lambda n: layer_in.at[layer], layer_in.at[layer], "slab", layer_peers, layer_sems
    )
    wait_all(echo_copies)
    spread = backproject(rows, chosen, columns, response_ref, pick_j_ref, spread_x_ref, 64)
    spread = spread[:, :256] + spread[:, 256:]
    wait_all(layer_copies)
    total_ref[pl.ds(PIECE * place, PIECE)] = add_up(layer_in, LAYERS)
    final_copies = to_peers(
        lambda n: total_ref.at[pl.ds(PIECE * place, PIECE)],
        total_ref.at[pl.ds(PIECE * place, PIECE)],
        "slab",
        ring_peers,
        final_sems,
    )
    base = upstream_ref[...].astype(F32) + back_ref[0]
    for z in range(4):
        for yt in range(2):
            grad_ref[z, 4 * yt : 4 * yt + 4, :] = (
                base[z, 4 * yt : 4 * yt + 4, :]
                + spread[4 * z : 4 * z + 4, 128 * yt : 128 * yt + 128]
            )
    wait_all(final_copies)


def vmem_specs(count):
    return [pl.BlockSpec(memory_space=pltpu.VMEM)] * count


def body(volume, measured, dual_gain, pattern, angle, response, w1, bias1, w2, bias2, w3, upstream):
    measured2 = measured.reshape(32, 128)
    gain2 = dual_gain.reshape(32, 128)
    pattern3 = pattern.reshape(VIEWS, 64, 16)
    angle2 = angle.reshape(VIEWS, 64)
    moves = [jnp.asarray(x) for x in tile_constants()]
    dma = pltpu.SemaphoreType.DMA
    fields = pl.pallas_call(
        ahead_kernel,
        name="ahead",
        out_shape=jax.ShapeDtypeStruct((3, 12, 16, 128), F32),
        in_specs=vmem_specs(11),
        out_specs=vmem_specs(1)[0],
        scratch_shapes=[
            pltpu.VMEM((4, 8, 128), F32),
            pltpu.VMEM((2, VIEWS, 4, 8, 128), F32),
            pltpu.VMEM((VIEWS, 32, 128), BF16),
            dma((3, 2, VIEWS)),
            dma((2, 3, 2)),
        ],
        compiler_params=pltpu.CompilerParams(
            collective_id=0, has_side_effects=True, vmem_limit_bytes=VMEM_BYTES
        ),
    )(volume, upstream, measured2, gain2, pattern3, angle2, response, *moves)

    consts = [jnp.asarray(x) for x in weight_constants()]
    new_volume, back, sums = pl.pallas_call(
        conv_kernel,
        name="convs",
        out_shape=(
            jax.ShapeDtypeStruct((4, 8, 128), F32),
            jax.ShapeDtypeStruct((2, 4, 8, 128), F32),
            jax.ShapeDtypeStruct((PIECE * RING, 8, 128), F32),
        ),
        in_specs=vmem_specs(11),
        out_specs=tuple(vmem_specs(3)),
        scratch_shapes=[
            pltpu.VMEM((12, 96, 128), BF16),
            pltpu.VMEM((12, 48, 128), BF16),
            pltpu.VMEM((8, 3, 8, 128), F32),
            pltpu.VMEM((448, 384), BF16),
            pltpu.VMEM((384, 256), BF16),
            pltpu.VMEM((72, 384), F32),
            pltpu.VMEM((144, 384), F32),
            pltpu.VMEM((96, 384), BF16),
            pltpu.VMEM((96, 384), BF16),
            pltpu.VMEM((10, 448, 128), F32),
            pltpu.VMEM((10, 14, 128, 128), BF16),
            pltpu.VMEM((8, 384, 128), F32),
            pltpu.VMEM((8, 384, 128), BF16),
            pltpu.VMEM((8, 12, 128, 128), BF16),
            pltpu.VMEM((8, 8, 32, 128), BF16),
            pltpu.VMEM((6, 320, 128), BF16),
            pltpu.VMEM((96, 384), F32),
            pltpu.VMEM((3, 16, 384), F32),
        ],
        compiler_params=pltpu.CompilerParams(vmem_limit_bytes=VMEM_BYTES),
    )(fields, w1, bias1.reshape(1, 32), w2, bias2.reshape(1, 32), w3.reshape(9, 96), *consts)

    grad_volume, total = pl.pallas_call(
        behind_kernel,
        name="behind",
        out_shape=(
            jax.ShapeDtypeStruct((4, 8, 128), F32),
            jax.ShapeDtypeStruct((PIECE * RING, 8, 128), F32),
        ),
        in_specs=vmem_specs(11),
        out_specs=tuple(vmem_specs(2)),
        scratch_shapes=[
            pltpu.VMEM((VIEWS, 4, 8, 128), F32),
            pltpu.VMEM((VIEWS, 32, 128), BF16),
            pltpu.VMEM((RING, PIECE, 8, 128), F32),
            pltpu.VMEM((VIEWS, PIECE, 8, 128), F32),
            pltpu.VMEM((LAYERS, PIECE, 8, 128), F32),
            dma((2, 2, VIEWS)),
            dma((2, RING - 1)),
            dma((2, VIEWS - 1)),
            dma((2, LAYERS - 1)),
            dma((2, RING - 1)),
        ],
        compiler_params=pltpu.CompilerParams(
            collective_id=1, has_side_effects=True, vmem_limit_bytes=VMEM_BYTES
        ),
    )(back, upstream, gain2, pattern3, angle2, response, *moves, sums)

    scale = 1.0 / math.sqrt(volume.size * SLABS * VIEWS)
    scaled = total.reshape(PIECE * RING * 8, 128) * scale
    taps = scaled[:288].reshape(9, 32, 128)
    return (
        new_volume,
        grad_volume,
        taps[:, :, 97:103],
        taps[0, :, 103],
        taps[:, :, :96],
        taps[4, :, 96],
        scaled[288:297, :96].reshape(9, 1, 96),
    )


def solution(mesh):
    placed = (
        P("slab", "view", None),
        P("view", "slab", None),
        P("view", "slab", None),
        P(None, "slab", None, None),
        P(None, "slab", None),
        P(),
        P(),
        P(),
        P(),
        P(),
        P(),
        P("slab", "view", None),
    )
    return jax.shard_map(
        body,
        mesh=mesh,
        in_specs=placed,
        out_specs=(P("slab", "view", None), P("slab", "view", None), P(), P(), P(), P(), P()),
        check_vma=False,
    )
```

```python
import functools
import math

import jax
import jax.numpy as jnp
import ml_dtypes
import numpy as np
from jax import lax
from jax.experimental import pallas as pl
from jax.experimental.pallas import tpu as pltpu
from jax.sharding import PartitionSpec as P

F32 = jnp.float32
BF16 = jnp.bfloat16
MESH = pl.DeviceIdType.MESH
VIEWS = 4
RING = 8
LAYERS = 4
SLABS = RING * LAYERS
PIECE = 5
VMEM_BYTES = 56 * 1024 * 1024
HELD = pl.ANY


def mm(a, b):
    return lax.dot_general(a, b, (((1,), (0,)), ((), ())), preferred_element_type=F32)


def mmt(a, b):
    return lax.dot_general(a, b, (((1,), (1,)), ((), ())), preferred_element_type=F32)


def iota(shape, dim):
    return lax.broadcasted_iota(jnp.int32, shape, dim)


def one(cond):
    return jnp.where(cond, 1.0, 0.0).astype(BF16)


def host_bf16(cond):
    return np.asarray(cond, np.float32).astype(ml_dtypes.bfloat16)


def tile_constants():
    row, col = np.arange(128)[:, None], np.arange(128)[None, :]
    pick_x = host_bf16(col == 4 * (row % 32) + row // 32)
    r, c = np.arange(512)[:, None], np.arange(1024)[None, :]
    xi, quarter, z, y8 = r // 128, r // 32 % 4, r // 8 % 4, r % 8
    yt, j = c // 128, c % 64
    place = host_bf16(
        (2 * quarter + y8 // 4 == yt) & (z == j // 16) & (y8 % 4 == j // 4 % 4) & (xi == j % 4)
    )
    r, c = np.arange(64)[:, None], np.arange(128)[None, :]
    pick_j = host_bf16((c < 64) & (c % 4 == r // 16) & (c // 4 == r % 16))
    r, c = np.arange(512)[:, None], np.arange(512)[None, :]
    spread_x = host_bf16((r // 32 % 4 == c // 128) & (c % 128 == 4 * (r % 32) + r // 128))
    return pick_x, place, pick_j, spread_x


def weight_constants():
    lane = np.arange(384)
    band1 = np.zeros((2, 9, 6, 256), np.float32)
    fold1 = np.zeros((384, 1152), np.float32)
    for a in range(3):
        for b in range(3):
            for e in range(3):
                for c in range(2):
                    band1[c, 3 * a + b, 2 * e + c, (a * 3 + e) * 16 + b] = 1.0
                    fold1[
                        ((c * 3 + a) * 3 + e) * 16 + 3 + b, 128 * (3 * a + b) + 97 + 2 * e + c
                    ] = 1.0
    fold1[288, 103] = 1.0
    band3 = np.zeros((3, 9, 256), np.float32)
    for a in range(3):
        for b in range(3):
            for e in range(3):
                band3[e, 3 * (2 - a) + (2 - b), (a * 3 + e) * 16 + b] = 1.0
    rep3 = np.zeros((3, 96, 384), np.float32)
    for e in range(3):
        rep3[e, 32 * e + lane % 32, lane] = 1.0
    fold3 = np.zeros((3, 384, 128), np.float32)
    for e in range(3):
        live = lane[lane < 320]
        fold3[e, live, 32 * e + live % 32] = 1.0
    return tuple(host_bf16(x) for x in (band1, band3, rep3, fold1, fold3))


def own_order():
    return one(iota((64, 64), 1) == 2 * (iota((64, 64), 0) % 32) + iota((64, 64), 0) // 32)


def choose_tiles(pattern_ref, angle_ref, choice, chosen, first):
    order = own_order()
    lanes = iota((64, 256), 1)
    lines = []
    for g in range(VIEWS):
        held = pattern_ref[g].astype(F32).astype(BF16)
        ids = mmt(order, held).astype(jnp.int32)
        for k in range(16):
            at = 256 * k + 64 * g
            choice[at : at + 64, :] = one(lanes == ids[:, k : k + 1])
        lines.append(mmt(held, order))
    line = jnp.concatenate(lines, axis=1).astype(jnp.int32)
    tile = iota((128, 256), 0) + first
    for k in range(16):
        at = 128 * (k % 2)
        chosen[at : at + 128, 256 * (k // 2) : 256 * (k // 2) + 256] = one(
            tile == line[k : k + 1, :]
        )
    angles = mmt(order, angle_ref[...].astype(F32).astype(BF16)).astype(jnp.int32)
    return jnp.concatenate([angles[:, g : g + 1] for g in range(VIEWS)], axis=0)


def project(field_rows, choice, angles, response_ref, pick_x_ref, place_ref):
    by_x = mmt(pick_x_ref[...], field_rows).astype(BF16)
    wide = jnp.concatenate([by_x[32 * i : 32 * i + 32] for i in range(4)], axis=1)
    spread = mm(wide, place_ref[...]).astype(BF16)
    tiles = jnp.concatenate([spread[:, 128 * i : 128 * i + 128] for i in range(8)], axis=0)
    low = iota((256, 128), 1) < 64
    pairs = []
    for p in range(8):
        picked = mm(choice[512 * p : 512 * p + 512, :], tiles)
        pairs.append(jnp.where(low, picked[:256], picked[256:]).astype(BF16))
    lines = mmt(jnp.concatenate(pairs, axis=1), response_ref[...])
    half = iota((256, 128), 1) // 64
    total = jnp.zeros((256, 128), F32)
    for p in range(4):
        total = total + jnp.where(angles == 2 * p + half, lines[:, 128 * p : 128 * p + 128], 0.0)
    return total + pltpu.roll(total, 64, 1)


def doubled_rows(ref, part):
    low = iota((32, 128), 1) < 64
    parts = []
    for g in range(VIEWS):
        rows = ref[g, part]
        turned = pltpu.roll(rows, 64, 1)
        parts.append(jnp.where(low, rows, turned))
        parts.append(jnp.where(low, turned, rows))
    return jnp.concatenate(parts, axis=0)


def backproject(doubled, chosen, angles, response_ref, pick_j_ref, spread_x_ref, count):
    half = iota((256, 128), 1) // 64
    masked = [
        jnp.where(angles == 2 * p + half, doubled, 0.0).astype(BF16) for p in range(4)
    ]
    contrib = mm(jnp.concatenate(masked, axis=1), response_ref[...])
    high = contrib.astype(BF16)
    rest = (contrib - high.astype(F32)).astype(BF16)
    stacked = jnp.concatenate(
        [
            jnp.concatenate(
                [high[:, 128 * p : 128 * p + 128], rest[:, 128 * p : 128 * p + 128]], axis=1
            )
            for p in range(8)
        ],
        axis=0,
    )
    skip = (128 - count) // 2
    left = jnp.concatenate(
        [chosen[skip : skip + count, :], chosen[128 + skip : 128 + skip + count, :]], axis=0
    )
    sums = mm(left, stacked)
    sums = sums[:, :128] + sums[:, 128:]
    tiles = sums[:count] + pltpu.roll(sums[count:], 64, 1)
    top = tiles.astype(BF16)
    if count == 64:
        top = jnp.concatenate([top, (tiles - top.astype(F32)).astype(BF16)], axis=0)
    by_j = mmt(pick_j_ref[...], top).astype(BF16)
    wide = jnp.concatenate([by_j[16 * i : 16 * i + 16] for i in range(4)], axis=1)
    return mm(wide, spread_x_ref[...])


def start_copies(pairs, sems):
    copies = []
    for n, (source, target, device) in enumerate(pairs):
        copies.append(
            pltpu.make_async_remote_copy(
                src_ref=source,
                dst_ref=target,
                send_sem=sems.at[0, n],
                recv_sem=sems.at[1, n],
                device_id=device,
                device_id_type=MESH,
            )
        )
    for copy in copies:
        copy.start()
    return copies


def wait_in(copies):
    for copy in copies:
        copy.wait_recv()


def wait_out(copies):
    for copy in copies:
        copy.wait_send()


def shifted(value, e, lane):
    if e == 1:
        return value
    if e == 0:
        return jnp.where(lane == 0, 0.0, pltpu.roll(value, 1, 1))
    return jnp.where(lane == 127, 0.0, pltpu.roll(value, 127, 1))


def prepare_weights(
    w1_ref, w2_ref, w3_ref, band1_ref, band3_ref, rep3_ref, t1v, t1b, t3t, t3, t1t, w2r, w2t
):
    eye32 = one(iota((32, 32), 0) == iota((32, 32), 1))
    for c, ref in ((0, t1v), (1, t1b)):
        base = jnp.zeros((32, 256), F32)
        for tap in range(9):
            turned = mmt(eye32, w1_ref[tap]).astype(BF16)
            base = base + mm(turned, band1_ref[c, tap])
        for yo in range(12):
            ref[32 * yo : 32 * yo + 32, :] = pltpu.roll(base, yo + 1, 1).astype(BF16)
    eye96 = one(iota((96, 96), 0) == iota((96, 96), 1))
    w3 = w3_ref[...]
    w3_turned = mmt(eye96, w3).astype(BF16)
    base = jnp.zeros((32, 256), F32)
    for e in range(3):
        base = base + mm(w3_turned[32 * (2 - e) : 32 * (2 - e) + 32], band3_ref[e])
    for yo in range(10):
        t3t[32 * yo : 32 * yo + 32, :] = pltpu.roll(base, yo + 2, 1).astype(BF16)
    step = iota((8, 384), 1) // 32 - iota((8, 384), 0)
    for e in range(3):
        line = mm(w3, rep3_ref[e])
        for a in range(3):
            block = jnp.zeros((8, 384), F32)
            for b in range(3):
                block = block + jnp.where(step == b, line[3 * a + b : 3 * a + b + 1, :], 0.0)
            t3[8 * (3 * a + e) : 8 * (3 * a + e) + 8, :] = block
    rep = one(iota((32, 256), 0) == iota((32, 256), 1) % 32)
    turned = [mm(w1_ref[tap], rep) for tap in range(9)]
    row16 = iota((16, 256), 0)
    row_y = jnp.where(row16 < 8, row16, jnp.where(row16 == 8, -1, 8))
    step = iota((16, 256), 1) // 32 - row_y + 1
    step = jnp.where(row16 < 10, step, -1)
    for a in range(3):
        for c in range(2):
            for e in range(3):
                row = 2 * (2 - e) + c
                block = jnp.zeros((16, 256), F32)
                for b in range(3):
                    tap = 3 * (2 - a) + (2 - b)
                    block = block + jnp.where(step == b, turned[tap][row : row + 1, :], 0.0)
                at = 16 * ((a * 2 + c) * 3 + e)
                t1t[at : at + 16, :] = block.astype(BF16)
    places = [one(iota((96, 384), 1) == iota((96, 384), 0) + 96 * b) for b in range(3)]
    keep = iota((96, 96), 1) // 32 == 2 - iota((96, 96), 0) // 32
    same = one(iota((32, 96), 0) == iota((32, 96), 1) % 32)
    for a in range(3):
        plain = jnp.zeros((32, 384), F32)
        across = jnp.zeros((32, 384), F32)
        for b in range(3):
            plain = plain + mm(w2_ref[3 * a + b], places[b])
            tower = jnp.concatenate([w2_ref[3 * (2 - a) + (2 - b)].astype(F32)] * 3, axis=0)
            tower = jnp.where(keep, tower, 0.0).astype(BF16)
            across = across + mm(mmt(same, tower).astype(BF16), places[b])
        w2r[32 * a : 32 * a + 32, :] = plain.astype(BF16)
        w2t[32 * a : 32 * a + 32, :] = across.astype(BF16)


def pair_of(ref, z, count):
    cols = [jnp.concatenate([ref[z + n + a] for a in range(count)], axis=0) for n in range(2)]
    return jnp.concatenate(cols, axis=1)


def stacked_rows(ref, z, y):
    cols = [ref[z + n, pl.ds(y, 3)].reshape(288, 128) for n in range(2)]
    return jnp.concatenate(cols, axis=1)


def split_pairs(outs):
    return [out[:, 128 * n : 128 * n + 128] for out in outs for n in range(2)]


def step_kernel(
    volume_ref,
    upstream_ref,
    measured_ref,
    gain_ref,
    pattern_ref,
    angle_ref,
    w1_ref,
    bias1_ref,
    w2_ref,
    bias2_ref,
    w3_ref,
    pick_x_ref,
    pick_j_ref,
    band1_ref,
    band3_ref,
    response_hbm,
    place_hbm,
    spread_x_hbm,
    rep3_hbm,
    fold1_hbm,
    fold3_hbm,
    new_ref,
    grad_ref,
    total_ref,
    response_ref,
    place_ref,
    spread_x_ref,
    rep3_ref,
    fold1_ref,
    fold3_ref,
    slots,
    slots_low,
    slots_high,
    lines,
    choice,
    chosen,
    fields,
    ins,
    backs,
    ups,
    ups_own,
    t1v,
    t1b,
    t3t,
    t3,
    t1t,
    w2r,
    w2t,
    pre1,
    h3,
    ct3,
    h2,
    s3,
    s2z,
    s1,
    g2,
    g3,
    parts_own,
    parts,
    edges,
    edges_low,
    edges_high,
    sums,
    ring_in,
    view_in,
    layer_in,
    local_sems,
    volume_sems,
    line_sems,
    ups_sems,
    plane_sems,
    back_sems,
    part_sems,
    low_sems,
    high_sems,
    ring_sems,
    view_sems,
    layer_sems,
    final_sems,
):
    slab, member = lax.axis_index("slab"), lax.axis_index("view")
    above, below = lax.rem(slab + 1, SLABS), lax.rem(slab + SLABS - 1, SLABS)
    left, right = lax.rem(member + VIEWS - 1, VIEWS), lax.rem(member + 1, VIEWS)
    place, layer = lax.rem(slab, RING), lax.div(slab, RING)
    view_peers = [lax.rem(member + off, VIEWS) for off in range(1, VIEWS)]
    ring_peers = [layer * RING + lax.rem(place + off, RING) for off in range(1, RING)]
    layer_peers = [
        lax.rem(layer + off, LAYERS) * RING + place for off in range(1, LAYERS)
    ]
    depth, height = 4 * SLABS, 8 * VIEWS

    loads = [
        pltpu.make_async_copy(source, target, local_sems.at[n])
        for n, (source, target) in enumerate(
            (
                (place_hbm, place_ref),
                (response_hbm, response_ref),
                (rep3_hbm, rep3_ref),
                (spread_x_hbm, spread_x_ref),
                (fold1_hbm, fold1_ref),
                (fold3_hbm, fold3_ref),
            )
        )
    ]
    for load in loads:
        load.start()

    barrier = pltpu.get_barrier_semaphore()
    peers = [{"view": peer} for peer in view_peers]
    peers += [{"slab": peer} for peer in ring_peers + layer_peers]
    for off in range(VIEWS):
        view = lax.rem(member + off, VIEWS)
        peers += [{"slab": above, "view": view}, {"slab": below, "view": view}]
    for peer in peers:
        pl.semaphore_signal(barrier, inc=1, device_id=peer, device_id_type=MESH)
    slots[0, member] = volume_ref[...]
    slots[1, member] = upstream_ref[...].astype(F32)
    lines[member, 0] = measured_ref[...]
    lines[member, 1] = gain_ref[...]
    pl.semaphore_wait(barrier, len(peers))

    pending = []
    volume_copies = start_copies(
        [(slots.at[0, member], slots.at[0, member], {"view": p}) for p in view_peers],
        volume_sems,
    )
    line_copies = start_copies(
        [(lines.at[member], lines.at[member], {"view": p}) for p in view_peers], line_sems
    )
    ups_copies = start_copies(
        [(slots.at[1, member], slots.at[1, member], {"view": p}) for p in view_peers],
        ups_sems,
    )
    pending += volume_copies + line_copies + ups_copies

    angles = choose_tiles(pattern_ref, angle_ref, choice, chosen, 64 * member - 32)
    loads[2].wait()
    prepare_weights(
        w1_ref, w2_ref, w3_ref, band1_ref, band3_ref, rep3_ref, t1v, t1b, t3t, t3, t1t, w2r, w2t
    )
    wait_in(line_copies)
    measured_rows, gain_rows = doubled_rows(lines, 0), doubled_rows(lines, 1)
    loads[0].wait()
    loads[1].wait()
    loads[3].wait()
    wait_in(volume_copies)
    wait_in(ups_copies)
    plane_copies = start_copies(
        [
            (slots.at[:, :, pl.ds(1, 3)], slots_low, {"slab": above}),
            (slots.at[:, :, pl.ds(0, 3)], slots_high, {"slab": below}),
        ],
        plane_sems,
    )
    pending += plane_copies

    field_rows = slots[0].reshape(128, 128).astype(BF16)
    got = project(field_rows, choice, angles, response_ref, pick_x_ref, place_ref)
    dual = (gain_rows * (got - measured_rows)).astype(BF16).astype(F32)
    spread = backproject(dual, chosen, angles, response_ref, pick_j_ref, spread_x_ref, 128)
    for z in range(4):
        for yt in range(4):
            fields[2, 4 + z, 4 * yt : 4 * yt + 4, :] = spread[
                4 * z : 4 * z + 4, 128 * yt : 128 * yt + 128
            ]
    back_copies = start_copies(
        [
            (fields.at[2, pl.ds(5, 3)], fields.at[2, pl.ds(1, 3)], {"slab": above}),
            (fields.at[2, pl.ds(4, 3)], fields.at[2, pl.ds(8, 3)], {"slab": below}),
        ],
        back_sems,
    )
    pending += back_copies

    wait_in(plane_copies)
    low_z, low_y = 4 * slab - 4, 8 * member - 4
    lane16 = iota((16, 128), 1)
    global_y = iota((16, 128), 0) + low_y
    inside_y = (global_y >= 0) & (global_y < height)
    lane8 = iota((8, 128), 1)
    for field in range(2):
        for z in range(1, 11):
            if z < 4:
                source, at = slots_low, z - 1
            elif z < 8:
                source, at = slots, z - 4
            else:
                source, at = slots_high, z - 8
            fields[field, z, 4:12, :] = source[field, member, at]
            fields[field, z, 0:4, :] = source[field, left, at, 4:8, :]
            fields[field, z, 12:16, :] = source[field, right, at, 0:4, :]

    def shifts_of(field, target):
        def one_plane(z, carry):
            inside = inside_y & (z + low_z >= 0) & (z + low_z < depth)
            plane = jnp.where(inside, fields[field, z], 0.0)
            plane = plane.astype(BF16).astype(F32)
            for e in range(3):
                target[z, 16 * e : 16 * e + 16, :] = shifted(plane, e, lane16).astype(BF16)
            return carry

        lax.fori_loop(1, 11, one_plane, 0, unroll=2)

    shifts_of(0, ins)
    shifts_of(1, ups)
    ups_own[...] = jnp.zeros(ups_own.shape, F32)
    for z in range(4):
        plane = slots[1, member, z]
        for e in range(3):
            ups_own[2 + z, e] = shifted(plane, 2 - e, lane8)

    def third_turned(p, carry):
        z = 2 * p
        out = mm(t3t[:, :144], pair_of(ups, z + 2, 3))
        ct3[z] = out[:, :128]
        ct3[z + 1] = out[:, 128:]
        return carry

    lax.fori_loop(0, 3, third_turned, 0)
    eye32 = iota((32, 32), 0) == iota((32, 32), 1)
    bias1 = jnp.sum(jnp.where(eye32, bias1_ref[...], 0.0), axis=1, keepdims=True)
    bias2 = jnp.sum(jnp.where(eye32, bias2_ref[...], 0.0), axis=1, keepdims=True)
    bias1_rows = jnp.concatenate([jnp.broadcast_to(bias1, (32, 128))] * 12, axis=0)

    def first_volume(p, carry):
        z = 2 * p
        out = mm(t1v[:, :144], pair_of(ins, z + 1, 3))
        pre1[z] = out[:, :128] + bias1_rows
        pre1[z + 1] = out[:, 128:] + bias1_rows
        return carry

    lax.fori_loop(0, 4, first_volume, 0)
    s2z[...] = jnp.zeros(s2z.shape, BF16)
    g2[...] = jnp.zeros(g2.shape, F32)
    g3[...] = jnp.zeros(g3.shape, F32)

    wait_in(back_copies)
    shifts_of(2, backs)

    def first_back(p, carry):
        z = 2 * p
        out = mm(t1b[:, :144], pair_of(backs, z + 1, 3))
        pre1[z] += out[:, :128]
        pre1[z + 1] += out[:, 128:]
        return carry

    lax.fori_loop(0, 4, first_back, 0)

    lane384 = iota((384, 128), 1)
    row_y1 = iota((384, 128), 0) // 32 + low_y + 2
    inside1 = (row_y1 >= 0) & (row_y1 < height)

    def activate(z, keep_slope):
        value = pre1[z]
        gate = 0.5 * jnp.tanh(0.5 * value) + 0.5
        act = value * gate
        if keep_slope:
            pre1[z] = gate + act * (1.0 - gate)
        inside = inside1 & (z + low_z + 2 >= 0) & (z + low_z + 2 < depth)
        act = jnp.where(inside, act, 0.0)
        for e in range(3):
            h3[z, :, 32 * e : 32 * e + 32, :] = (
                shifted(act, e, lane384).astype(BF16).reshape(12, 32, 128)
            )

    def activate_outer(n, carry):
        activate(n + 4 * (n // 2), False)
        return carry

    def activate_inner(n, carry):
        activate(n + 2, True)
        return carry

    lax.fori_loop(0, 4, activate_outer, 0)
    lax.fori_loop(0, 4, activate_inner, 0)

    lane32 = iota((32, 128), 1)

    def second(y, carry):
        out = split_pairs([mm(w2r[:, :288], stacked_rows(h3, 2 * p, y)) for p in range(4)])
        ok_y = (y + low_y + 3 >= 0) & (y + low_y + 3 < height)
        at = pl.multiple_of(32 * y, 32)
        for z in range(6):
            value = out[z][:32] + out[z + 1][32:64] + out[z + 2][64:] + bias2
            gate = 0.5 * jnp.tanh(0.5 * value) + 0.5
            act = value * gate
            slope = gate + act * (1.0 - gate)
            ok = ok_y & (z + low_z + 3 >= 0) & (z + low_z + 3 < depth)
            live = jnp.where(ok, 1.0, 0.0)
            h2[z, pl.ds(at, 32), :] = (act * live).astype(BF16)
            slope = slope * ct3[z, pl.ds(at, 32), :] * live
            for e in range(3):
                s3[z, y, 32 * e : 32 * e + 32, :] = shifted(slope, e, lane32).astype(BF16)
        return carry

    lax.fori_loop(0, 10, second, 0)

    def second_turned(y, carry):
        out = split_pairs([mm(w2t[:, :288], stacked_rows(s3, 2 * p, y)) for p in range(3)])
        at = pl.multiple_of(32 * y, 32)
        from_ = pl.multiple_of(32 * y + 64, 32)
        for z in range(4):
            value = out[z][:32] + out[z + 1][32:64] + out[z + 2][64:]
            s1[z, pl.ds(at, 32), :] = (value * pre1[z + 2, pl.ds(from_, 32), :]).astype(BF16)
        return carry

    lax.fori_loop(0, 8, second_turned, 0)

    out = split_pairs([mm(t1t[...], pair_of(s1, 2 * p, 1)) for p in range(2)])
    for c in range(2):
        for z in range(-1, 5):
            total = jnp.zeros((16, 128), F32)
            for e in range(3):
                part = jnp.zeros((16, 128), F32)
                for a in range(3):
                    if 0 <= z + a - 1 < 4:
                        at = 16 * ((a * 2 + c) * 3 + e)
                        part = part + out[z + a - 1][at : at + 16]
                total = total + shifted(part, e, lane16)
            if z == -1:
                edges[0, c] = total.astype(BF16)
            elif z == 4:
                edges[1, c] = total.astype(BF16)
            else:
                parts[member, c, z] = total.astype(BF16)
                if c == 0:
                    parts_own[z] = total
    part_copies = start_copies(
        [(parts.at[member], parts.at[member], {"view": p}) for p in view_peers], part_sems
    )
    all_views = [lax.rem(member + off, VIEWS) for off in range(VIEWS)]
    low_copies = start_copies(
        [
            (edges.at[1], edges_low.at[member], {"slab": above, "view": view})
            for view in all_views
        ],
        low_sems,
    )
    high_copies = start_copies(
        [
            (edges.at[0], edges_high.at[member], {"slab": below, "view": view})
            for view in all_views
        ],
        high_sems,
    )
    pending += part_copies + low_copies + high_copies

    for z in range(4):
        s2z[z + 2] = s3[z + 1, 1:9, 32:64, :]
    ones = jnp.ones((16, 768), BF16)

    def second_grad(y, carry):
        turned = jnp.concatenate(
            [
                jnp.concatenate([s2z[z + 1 - a, y] for z in range(1, 7)], axis=1)
                for a in range(3)
            ],
            axis=0,
        )
        plain = jnp.concatenate(
            [h3[z, pl.ds(y + 1, 3)].reshape(288, 128) for z in range(1, 7)], axis=1
        )
        g2[:, :304] += mmt(turned, jnp.concatenate([plain, ones], axis=0))
        return carry

    lax.fori_loop(0, 8, second_grad, 0)

    turned = jnp.concatenate(
        [
            jnp.concatenate(
                [ups_own[z + 2 - a, e] for a in range(3) for e in range(3)], axis=0
            ).astype(BF16)
            for z in range(6)
        ],
        axis=1,
    )
    plain = jnp.concatenate([h2[z] for z in range(6)], axis=1)
    cross = mmt(turned, plain)
    step10 = iota((8, 320), 1) // 32 - iota((8, 320), 0)
    for a in range(3):
        for e in range(3):
            block = cross[8 * (3 * a + e) : 8 * (3 * a + e) + 8]
            for b in range(3):
                g3[e, 3 * a + b : 3 * a + b + 1, 0:320] = jnp.sum(
                    jnp.where(step10 == b, block, 0.0), axis=0, keepdims=True
                )
    loads[4].wait()
    loads[5].wait()
    third = jnp.zeros((16, 128), F32)
    for e in range(3):
        value = g3[e]
        high = value.astype(BF16)
        rest = (value - high.astype(F32)).astype(BF16)
        third = third + mm(high, fold3_ref[e]) + mm(rest, fold3_ref[e])

    turned = jnp.concatenate([s1[z] for z in range(4)], axis=1)
    plain = jnp.concatenate(
        [
            jnp.concatenate(
                [ins[z + 3 + a] for a in range(3)]
                + [backs[z + 3 + a] for a in range(3)]
                + [jnp.ones((96, 128), BF16)],
                axis=0,
            )
            for z in range(4)
        ],
        axis=1,
    )
    cross = mmt(turned, plain)
    total = cross[:32]
    for yo in range(1, 8):
        total = total + pltpu.roll(cross[32 * yo : 32 * yo + 32], 384 - yo, 1)
    high = total.astype(BF16)
    rest = (total - high.astype(F32)).astype(BF16)
    first_grads = mm(high, fold1_ref[...]) + mm(rest, fold1_ref[...])

    lanes = iota((32, 128), 1)
    for tap in range(9):
        a, b = tap // 3, tap % 3
        block = g2[32 * a : 32 * a + 32, :]
        if b:
            block = pltpu.roll(block, 384 - 96 * b, 1)
        block = jnp.where(lanes < (97 if b == 2 else 96), block[:, :128], 0.0)
        block = block + first_grads[:, 128 * tap : 128 * tap + 128]
        sums[4 * tap : 4 * tap + 4] = block.reshape(4, 8, 128)
    sums[36:38] = third.reshape(2, 8, 128)
    sums[38:40] = jnp.zeros((2, 8, 128), F32)

    ring_in[place] = sums[pl.ds(PIECE * place, PIECE)]
    ring_copies = start_copies(
        [
            (sums.at[pl.ds(PIECE * lax.rem(peer, RING), PIECE)], ring_in.at[place], {"slab": peer})
            for peer in ring_peers
        ],
        ring_sems,
    )
    pending += ring_copies

    t3_now = t3[:, :320].astype(BF16)
    out = split_pairs([mm(t3_now, pair_of(h2, 2 * p, 1)) for p in range(3)])
    for z in range(4):
        total = volume_ref[z]
        for e in range(3):
            part = jnp.zeros((8, 128), F32)
            for a in range(3):
                at = 8 * (3 * a + e)
                part = part + out[z + a][at : at + 8]
            total = total + shifted(part, e, lane8)
        new_ref[z] = total

    def add_up(ref, count):
        total = ref[0]
        for n in range(1, count):
            total = total + ref[n]
        return total

    wait_in(part_copies)
    wait_in(low_copies)
    wait_in(high_copies)
    has_low = jnp.where(slab > 0, 1.0, 0.0)
    has_high = jnp.where(slab < SLABS - 1, 1.0, 0.0)

    def plane_at(view, c, z):
        plane = parts[view, c, z].astype(F32)
        if z == 0:
            plane = plane + has_low * edges_low[view, c].astype(F32)
        if z == 3:
            plane = plane + has_high * edges_high[view, c].astype(F32)
        return plane

    row8 = iota((8, 128), 0)
    rows = [None] * 16
    for z in range(4):
        planes = [plane_at(view, 1, z) for view in range(VIEWS)]
        for view in range(VIEWS):
            value = planes[view][:8]
            if view > 0:
                value = value + jnp.where(row8 == 0, planes[view - 1][9:10], 0.0)
            if view < VIEWS - 1:
                value = value + jnp.where(row8 == 7, planes[view + 1][8:9], 0.0)
            rows[4 * view + z] = value
    field_rows = jnp.concatenate(rows, axis=0).astype(BF16)
    got = project(field_rows, choice, angles, response_ref, pick_x_ref, place_ref)
    wait_in(ring_copies)
    view_in[member] = add_up(ring_in, RING)
    view_copies = start_copies(
        [(view_in.at[member], view_in.at[member], {"view": p}) for p in view_peers], view_sems
    )
    echo = (gain_rows * got).astype(BF16).astype(F32)
    spread = backproject(echo, chosen, angles, response_ref, pick_j_ref, spread_x_ref, 64)
    spread = spread[:, :256] + spread[:, 256:]
    has_left = jnp.where(member > 0, 1.0, 0.0)
    has_right = jnp.where(member < VIEWS - 1, 1.0, 0.0)
    for z in range(4):
        value = parts_own[z]
        if z == 0:
            value = value + has_low * edges_low[member, 0].astype(F32)
        if z == 3:
            value = value + has_high * edges_high[member, 0].astype(F32)
        value = value[:8] + upstream_ref[z].astype(F32)
        value = value + jnp.where(row8 == 0, has_left * plane_at(left, 0, z)[9:10], 0.0)
        value = value + jnp.where(row8 == 7, has_right * plane_at(right, 0, z)[8:9], 0.0)
        for yt in range(2):
            grad_ref[z, 4 * yt : 4 * yt + 4, :] = (
                value[4 * yt : 4 * yt + 4, :]
                + spread[4 * z : 4 * z + 4, 128 * yt : 128 * yt + 128]
            )
    wait_in(view_copies)
    layer_in[layer] = add_up(view_in, VIEWS)
    layer_copies = start_copies(
        [(layer_in.at[layer], layer_in.at[layer], {"slab": p}) for p in layer_peers],
        layer_sems,
    )
    wait_out(pending)
    wait_in(layer_copies)
    mine = pl.ds(PIECE * place, PIECE)
    total_ref[mine] = add_up(layer_in, LAYERS)
    final_copies = start_copies(
        [(total_ref.at[mine], total_ref.at[mine], {"slab": p}) for p in ring_peers],
        final_sems,
    )
    wait_in(final_copies)
    wait_out(view_copies + layer_copies + final_copies)


def emit_kernel(
    scale,
    new_ref,
    grad_ref,
    total_ref,
    new_out,
    grad_out,
    w1_out,
    bias1_out,
    w2_out,
    bias2_out,
    w3_out,
):
    new_out[...] = new_ref[...]
    grad_out[...] = grad_ref[...]
    for tap in range(9):
        block = total_ref[4 * tap : 4 * tap + 4].reshape(32, 128) * scale
        w2_out[tap] = block[:, :96]
        turned = block.T
        w1_out[tap] = turned[97:103, :]
        if tap == 0:
            bias1_out[...] = turned[103:104, :]
        if tap == 5:
            bias2_out[...] = turned[96:97, :]
    third = total_ref[36:38].reshape(16, 128) * scale
    for tap in range(9):
        w3_out[tap] = third[tap : tap + 1, :96]


def vmem_specs(count):
    return [pl.BlockSpec(memory_space=pltpu.VMEM)] * count


def body(volume, measured, dual_gain, pattern, angle, response, w1, bias1, w2, bias2, w3, upstream):
    pick_x, place, pick_j, spread_x = [jnp.asarray(x) for x in tile_constants()]
    band1, band3, rep3, fold1, fold3 = [jnp.asarray(x) for x in weight_constants()]
    dma = pltpu.SemaphoreType.DMA
    pieces = PIECE * RING
    new_volume, grad_volume, total = pl.pallas_call(
        step_kernel,
        name="step",
        out_shape=(
            jax.ShapeDtypeStruct((4, 8, 128), F32),
            jax.ShapeDtypeStruct((4, 8, 128), F32),
            jax.ShapeDtypeStruct((pieces, 8, 128), F32),
        ),
        in_specs=vmem_specs(15) + [pl.BlockSpec(memory_space=HELD)] * 6,
        out_specs=tuple(vmem_specs(3)),
        scratch_shapes=[
            pltpu.VMEM((512, 1024), BF16),
            pltpu.VMEM((512, 1024), BF16),
            pltpu.VMEM((512, 512), BF16),
            pltpu.VMEM((3, 96, 384), BF16),
            pltpu.VMEM((384, 1152), BF16),
            pltpu.VMEM((3, 384, 128), BF16),
            pltpu.VMEM((2, VIEWS, 4, 8, 128), F32),
            pltpu.VMEM((2, VIEWS, 3, 8, 128), F32),
            pltpu.VMEM((2, VIEWS, 3, 8, 128), F32),
            pltpu.VMEM((VIEWS, 2, 32, 128), F32),
            pltpu.VMEM((4096, 256), BF16),
            pltpu.VMEM((256, 2048), BF16),
            pltpu.VMEM((3, 12, 16, 128), F32),
            pltpu.VMEM((12, 48, 128), BF16),
            pltpu.VMEM((12, 48, 128), BF16),
            pltpu.VMEM((12, 48, 128), BF16),
            pltpu.VMEM((8, 3, 8, 128), F32),
            pltpu.VMEM((384, 256), BF16),
            pltpu.VMEM((384, 256), BF16),
            pltpu.VMEM((320, 256), BF16),
            pltpu.VMEM((72, 384), F32),
            pltpu.VMEM((288, 256), BF16),
            pltpu.VMEM((96, 384), BF16),
            pltpu.VMEM((96, 384), BF16),
            pltpu.VMEM((8, 384, 128), F32),
            pltpu.VMEM((8, 12, 96, 128), BF16),
            pltpu.VMEM((6, 320, 128), F32),
            pltpu.VMEM((6, 320, 128), BF16),
            pltpu.VMEM((6, 10, 96, 128), BF16),
            pltpu.VMEM((8, 8, 32, 128), BF16),
            pltpu.VMEM((4, 256, 128), BF16),
            pltpu.VMEM((96, 384), F32),
            pltpu.VMEM((3, 16, 384), F32),
            pltpu.VMEM((4, 16, 128), F32),
            pltpu.VMEM((VIEWS, 2, 4, 16, 128), BF16),
            pltpu.VMEM((2, 2, 16, 128), BF16),
            pltpu.VMEM((VIEWS, 2, 16, 128), BF16),
            pltpu.VMEM((VIEWS, 2, 16, 128), BF16),
            pltpu.VMEM((pieces, 8, 128), F32),
            pltpu.VMEM((RING, PIECE, 8, 128), F32),
            pltpu.VMEM((VIEWS, PIECE, 8, 128), F32),
            pltpu.VMEM((LAYERS, PIECE, 8, 128), F32),
            dma((6,)),
            dma((2, 3)),
            dma((2, 3)),
            dma((2, 3)),
            dma((2, 2)),
            dma((2, 2)),
            dma((2, 3)),
            dma((2, 4)),
            dma((2, 4)),
            dma((2, RING - 1)),
            dma((2, 3)),
            dma((2, 3)),
            dma((2, RING - 1)),
        ],
        compiler_params=pltpu.CompilerParams(
            collective_id=0, has_side_effects=True, vmem_limit_bytes=VMEM_BYTES
        ),
    )(
        volume,
        upstream,
        measured.reshape(32, 128),
        dual_gain.reshape(32, 128),
        pattern.transpose(0, 1, 3, 2).reshape(VIEWS, 16, 64),
        angle.reshape(VIEWS, 64),
        w1.transpose(0, 2, 1),
        bias1.reshape(1, 32),
        w2,
        bias2.reshape(1, 32),
        w3.reshape(9, 96),
        pick_x,
        pick_j,
        band1,
        band3,
        response,
        place,
        spread_x,
        rep3,
        fold1,
        fold3,
    )
    scale = 1.0 / math.sqrt(volume.size * SLABS * VIEWS)
    new_volume, grad_volume, grad_w1, grad_bias1, grad_w2, grad_bias2, grad_w3 = pl.pallas_call(
        functools.partial(emit_kernel, scale),
        name="emit",
        out_shape=(
            jax.ShapeDtypeStruct((4, 8, 128), F32),
            jax.ShapeDtypeStruct((4, 8, 128), F32),
            jax.ShapeDtypeStruct((9, 6, 32), F32),
            jax.ShapeDtypeStruct((1, 32), F32),
            jax.ShapeDtypeStruct((9, 32, 96), F32),
            jax.ShapeDtypeStruct((1, 32), F32),
            jax.ShapeDtypeStruct((9, 1, 96), F32),
        ),
        in_specs=vmem_specs(3),
        out_specs=tuple(vmem_specs(7)),
    )(new_volume, grad_volume, total)
    return (
        new_volume,
        grad_volume,
        grad_w1.transpose(0, 2, 1),
        grad_bias1.reshape(32),
        grad_w2,
        grad_bias2.reshape(32),
        grad_w3,
    )


def solution(mesh):
    placed = (
        P("slab", "view", None),
        P("view", "slab", None),
        P("view", "slab", None),
        P(None, "slab", None, None),
        P(None, "slab", None),
        P(),
        P(),
        P(),
        P(),
        P(),
        P(),
        P("slab", "view", None),
    )
    return jax.shard_map(
        body,
        mesh=mesh,
        in_specs=placed,
        out_specs=(P("slab", "view", None), P("slab", "view", None), P(), P(), P(), P(), P()),
        check_vma=False,
    )
```

```python
import functools
import math

import jax
import jax.numpy as jnp
import ml_dtypes
import numpy as np
from jax import lax
from jax.experimental import pallas as pl
from jax.experimental.pallas import tpu as pltpu
from jax.sharding import PartitionSpec as P

F32 = jnp.float32
BF16 = jnp.bfloat16
MESH = pl.DeviceIdType.MESH
VIEWS = 4
RING = 8
LAYERS = 4
SLABS = RING * LAYERS
PIECE = 40
SMALL = 32
MESSAGE = SMALL + PIECE
VMEM_BYTES = 56 * 1024 * 1024
HELD = pl.ANY


def mm(a, b):
    return lax.dot_general(a, b, (((1,), (0,)), ((), ())), preferred_element_type=F32)


def mmt(a, b):
    return lax.dot_general(a, b, (((1,), (1,)), ((), ())), preferred_element_type=F32)


def iota(shape, dim):
    return lax.broadcasted_iota(jnp.int32, shape, dim)


def one(cond):
    return jnp.where(cond, 1.0, 0.0).astype(BF16)


def host_bf16(cond):
    return np.asarray(cond, np.float32).astype(ml_dtypes.bfloat16)


def tile_constants():
    row, col = np.arange(128)[:, None], np.arange(128)[None, :]
    pick_x = host_bf16(col == 4 * (row % 32) + row // 32)
    r, c = np.arange(512)[:, None], np.arange(1024)[None, :]
    xi, quarter, z, y8 = r // 128, r // 32 % 4, r // 8 % 4, r % 8
    yt, j = c // 128, c % 64
    place = host_bf16(
        (2 * quarter + y8 // 4 == yt) & (z == j // 16) & (y8 % 4 == j // 4 % 4) & (xi == j % 4)
    )
    r, c = np.arange(64)[:, None], np.arange(128)[None, :]
    pick_j = host_bf16((c < 64) & (c % 4 == r // 16) & (c // 4 == r % 16))
    r, c = np.arange(512)[:, None], np.arange(512)[None, :]
    spread_x = host_bf16((r // 32 % 4 == c // 128) & (c % 128 == 4 * (r % 32) + r // 128))
    return pick_x, place, pick_j, spread_x


def weight_constants():
    lane = np.arange(384)
    band1 = np.zeros((2, 9, 6, 256), np.float32)
    fold1 = np.zeros((384, 128), np.float32)
    for a in range(3):
        for b in range(3):
            for e in range(3):
                for c in range(2):
                    band1[c, 3 * a + b, 2 * e + c, (a * 3 + e) * 16 + b] = 1.0
                    fold1[
                        ((c * 3 + a) * 3 + e) * 16 + 3 + b, 6 * (3 * a + b) + 2 * e + c
                    ] = 1.0
    fold1[288, 54] = 1.0
    band3 = np.zeros((3, 9, 256), np.float32)
    for a in range(3):
        for b in range(3):
            for e in range(3):
                band3[e, 3 * (2 - a) + (2 - b), (a * 3 + e) * 16 + b] = 1.0
    rep3 = np.zeros((3, 96, 384), np.float32)
    for e in range(3):
        rep3[e, 32 * e + lane % 32, lane] = 1.0
    fold3 = np.zeros((3, 384, 128), np.float32)
    for e in range(3):
        live = lane[lane < 320]
        fold3[e, live, 32 * e + live % 32] = 1.0
    return tuple(host_bf16(x) for x in (band1, band3, rep3, fold1, fold3))


def own_order():
    return one(iota((64, 64), 1) == 2 * (iota((64, 64), 0) % 32) + iota((64, 64), 0) // 32)


def choose_tiles(pattern_ref, angle_ref, choice, chosen, first):
    order = own_order()
    lanes = iota((64, 256), 1)
    lines = []
    for g in range(VIEWS):
        held = pattern_ref[g].astype(F32).astype(BF16)
        ids = mmt(order, held).astype(jnp.int32)
        for k in range(16):
            at = 256 * k + 64 * g
            choice[at : at + 64, :] = one(lanes == ids[:, k : k + 1])
        lines.append(mmt(held, order))
    line = jnp.concatenate(lines, axis=1).astype(jnp.int32)
    tile = iota((128, 256), 0) + first
    for k in range(16):
        at = 128 * (k % 2)
        chosen[at : at + 128, 256 * (k // 2) : 256 * (k // 2) + 256] = one(
            tile == line[k : k + 1, :]
        )
    angles = mmt(order, angle_ref[...].astype(F32).astype(BF16)).astype(jnp.int32)
    return jnp.concatenate([angles[:, g : g + 1] for g in range(VIEWS)], axis=0)


def project(field_rows, choice, angles, response_ref, pick_x_ref, place_ref):
    by_x = mmt(pick_x_ref[...], field_rows).astype(BF16)
    wide = jnp.concatenate([by_x[32 * i : 32 * i + 32] for i in range(4)], axis=1)
    spread = mm(wide, place_ref[...]).astype(BF16)
    tiles = jnp.concatenate([spread[:, 128 * i : 128 * i + 128] for i in range(8)], axis=0)
    low = iota((256, 128), 1) < 64
    pairs = []
    for p in range(8):
        picked = mm(choice[512 * p : 512 * p + 512, :], tiles)
        pairs.append(jnp.where(low, picked[:256], picked[256:]).astype(BF16))
    lines = mmt(jnp.concatenate(pairs, axis=1), response_ref[...])
    half = iota((256, 128), 1) // 64
    total = jnp.zeros((256, 128), F32)
    for p in range(4):
        total = total + jnp.where(angles == 2 * p + half, lines[:, 128 * p : 128 * p + 128], 0.0)
    return total + pltpu.roll(total, 64, 1)


def doubled_rows(ref, part):
    low = iota((32, 128), 1) < 64
    parts = []
    for g in range(VIEWS):
        rows = ref[g, part].astype(F32)
        turned = pltpu.roll(rows, 64, 1)
        parts.append(jnp.where(low, rows, turned))
        parts.append(jnp.where(low, turned, rows))
    return jnp.concatenate(parts, axis=0)


def backproject(doubled, chosen, angles, response_ref, pick_j_ref, spread_x_ref, count):
    half = iota((256, 128), 1) // 64
    masked = [
        jnp.where(angles == 2 * p + half, doubled, 0.0).astype(BF16) for p in range(4)
    ]
    contrib = mm(jnp.concatenate(masked, axis=1), response_ref[...])
    high = contrib.astype(BF16)
    rest = (contrib - high.astype(F32)).astype(BF16)
    stacked = jnp.concatenate(
        [
            jnp.concatenate(
                [high[:, 128 * p : 128 * p + 128], rest[:, 128 * p : 128 * p + 128]], axis=1
            )
            for p in range(8)
        ],
        axis=0,
    )
    skip = (128 - count) // 2
    left = jnp.concatenate(
        [chosen[skip : skip + count, :], chosen[128 + skip : 128 + skip + count, :]], axis=0
    )
    sums = mm(left, stacked)
    sums = sums[:, :128] + sums[:, 128:]
    tiles = sums[:count] + pltpu.roll(sums[count:], 64, 1)
    top = tiles.astype(BF16)
    if count == 64:
        top = jnp.concatenate([top, (tiles - top.astype(F32)).astype(BF16)], axis=0)
    by_j = mmt(pick_j_ref[...], top).astype(BF16)
    wide = jnp.concatenate([by_j[16 * i : 16 * i + 16] for i in range(4)], axis=1)
    return mm(wide, spread_x_ref[...])


def start_copies(pairs, sems):
    copies = []
    for n, (source, target, device) in enumerate(pairs):
        copies.append(
            pltpu.make_async_remote_copy(
                src_ref=source,
                dst_ref=target,
                send_sem=sems.at[0, n],
                recv_sem=sems.at[1, n],
                device_id=device,
                device_id_type=MESH,
            )
        )
    for copy in copies:
        copy.start()
    return copies


def wait_in(copies):
    for copy in copies:
        copy.wait_recv()


def wait_out(copies):
    for copy in copies:
        copy.wait_send()


def shifted(value, e, lane):
    if e == 1:
        return value
    if e == 0:
        return jnp.where(lane == 0, 0.0, pltpu.roll(value, 1, 1))
    return jnp.where(lane == 127, 0.0, pltpu.roll(value, 127, 1))


def prepare_weights(
    w1_ref, w2_ref, w3_ref, band1_ref, band3_ref, rep3_ref, t1v, t1b, t3t, t3, t1t, w2r, w2t
):
    eye32 = one(iota((32, 32), 0) == iota((32, 32), 1))
    for c, ref in ((0, t1v), (1, t1b)):
        base = jnp.zeros((32, 256), F32)
        for tap in range(9):
            turned = mmt(eye32, w1_ref[tap]).astype(BF16)
            base = base + mm(turned, band1_ref[c, tap])
        for yo in range(12):
            ref[32 * yo : 32 * yo + 32, :] = pltpu.roll(base, yo + 1, 1).astype(BF16)
    eye96 = one(iota((96, 96), 0) == iota((96, 96), 1))
    w3 = w3_ref[...]
    w3_turned = mmt(eye96, w3).astype(BF16)
    base = jnp.zeros((32, 256), F32)
    for e in range(3):
        base = base + mm(w3_turned[32 * (2 - e) : 32 * (2 - e) + 32], band3_ref[e])
    for yo in range(10):
        t3t[32 * yo : 32 * yo + 32, :] = pltpu.roll(base, yo + 2, 1).astype(BF16)
    step = iota((8, 384), 1) // 32 - iota((8, 384), 0)
    for e in range(3):
        line = mm(w3, rep3_ref[e])
        for a in range(3):
            block = jnp.zeros((8, 384), F32)
            for b in range(3):
                block = block + jnp.where(step == b, line[3 * a + b : 3 * a + b + 1, :], 0.0)
            t3[8 * (3 * a + e) : 8 * (3 * a + e) + 8, :] = block
    rep = one(iota((32, 256), 0) == iota((32, 256), 1) % 32)
    turned = [mm(w1_ref[tap], rep) for tap in range(9)]
    row16 = iota((16, 256), 0)
    row_y = jnp.where(row16 < 8, row16, jnp.where(row16 == 8, -1, 8))
    step = iota((16, 256), 1) // 32 - row_y + 1
    step = jnp.where(row16 < 10, step, -1)
    for a in range(3):
        for c in range(2):
            for e in range(3):
                row = 2 * (2 - e) + c
                block = jnp.zeros((16, 256), F32)
                for b in range(3):
                    tap = 3 * (2 - a) + (2 - b)
                    block = block + jnp.where(step == b, turned[tap][row : row + 1, :], 0.0)
                at = 16 * ((a * 2 + c) * 3 + e)
                t1t[at : at + 16, :] = block.astype(BF16)
    places = [one(iota((96, 384), 1) == iota((96, 384), 0) + 96 * b) for b in range(3)]
    keep = iota((96, 96), 1) // 32 == 2 - iota((96, 96), 0) // 32
    same = one(iota((32, 96), 0) == iota((32, 96), 1) % 32)
    for a in range(3):
        plain = jnp.zeros((32, 384), F32)
        across = jnp.zeros((32, 384), F32)
        for b in range(3):
            plain = plain + mm(w2_ref[3 * a + b], places[b])
            tower = jnp.concatenate([w2_ref[3 * (2 - a) + (2 - b)].astype(F32)] * 3, axis=0)
            tower = jnp.where(keep, tower, 0.0).astype(BF16)
            across = across + mm(mmt(same, tower).astype(BF16), places[b])
        w2r[32 * a : 32 * a + 32, :] = plain.astype(BF16)
        w2t[32 * a : 32 * a + 32, :] = across.astype(BF16)


def pair_of(ref, z, count):
    cols = [jnp.concatenate([ref[z + n + a] for a in range(count)], axis=0) for n in range(2)]
    return jnp.concatenate(cols, axis=1)


def stacked_rows(ref, z, y):
    cols = [ref[z + n, pl.ds(y, 3)].reshape(288, 128) for n in range(2)]
    return jnp.concatenate(cols, axis=1)


def split_pairs(outs):
    return [out[:, 128 * n : 128 * n + 128] for out in outs for n in range(2)]


def step_kernel(
    volume_ref,
    upstream_ref,
    measured_ref,
    gain_ref,
    pattern_ref,
    angle_ref,
    w1_ref,
    bias1_ref,
    w2_ref,
    bias2_ref,
    w3_ref,
    pick_x_ref,
    pick_j_ref,
    band1_ref,
    band3_ref,
    response_hbm,
    place_hbm,
    spread_x_hbm,
    rep3_hbm,
    fold1_hbm,
    fold3_hbm,
    new_ref,
    grad_ref,
    final_in,
    response_ref,
    place_ref,
    spread_x_ref,
    rep3_ref,
    fold1_ref,
    fold3_ref,
    pack,
    pack_low,
    pack_high,
    choice,
    chosen,
    fields,
    ins,
    backs,
    ups,
    ups_own,
    t1v,
    t1b,
    t3t,
    t3,
    t1t,
    w2r,
    w2t,
    pre1,
    h3,
    ct3,
    h2,
    s3,
    s2z,
    s1,
    g2,
    g3,
    parts_own,
    parts,
    parts_side,
    edges,
    edges_low,
    edges_high,
    totals,
    sums,
    ring_in,
    view_in,
    layer_in,
    local_sems,
    pack_sems,
    plane_sems,
    back_sems,
    edge_sems,
    part_sems,
    side_sems,
    ring_sems,
    view_sems,
    layer_sems,
    final_sems,
):
    slab, member = lax.axis_index("slab"), lax.axis_index("view")
    above, below = lax.rem(slab + 1, SLABS), lax.rem(slab + SLABS - 1, SLABS)
    left, right = lax.rem(member + VIEWS - 1, VIEWS), lax.rem(member + 1, VIEWS)
    place, layer = lax.rem(slab, RING), lax.div(slab, RING)
    view_peers = [lax.rem(member + off, VIEWS) for off in range(1, VIEWS)]
    ring_peers = [layer * RING + lax.rem(place + off, RING) for off in range(1, RING)]
    layer_peers = [
        lax.rem(layer + off, LAYERS) * RING + place for off in range(1, LAYERS)
    ]
    depth, height = 4 * SLABS, 8 * VIEWS

    loads = [
        pltpu.make_async_copy(source, target, local_sems.at[n])
        for n, (source, target) in enumerate(
            (
                (place_hbm, place_ref),
                (response_hbm, response_ref),
                (rep3_hbm, rep3_ref),
                (spread_x_hbm, spread_x_ref),
                (fold1_hbm, fold1_ref),
                (fold3_hbm, fold3_ref),
            )
        )
    ]
    for load in loads:
        load.start()

    barrier = pltpu.get_barrier_semaphore()
    peers = [{"view": peer} for peer in view_peers]
    peers += [{"slab": peer} for peer in ring_peers + layer_peers + [above, below]]
    for peer in peers:
        pl.semaphore_signal(barrier, inc=1, device_id=peer, device_id_type=MESH)
    pack[member, 0] = volume_ref[...].reshape(32, 128).astype(BF16)
    pack[member, 1] = upstream_ref[...].astype(F32).reshape(32, 128).astype(BF16)
    pack[member, 2] = measured_ref[...].astype(BF16)
    pack[member, 3] = gain_ref[...].astype(BF16)
    pl.semaphore_wait(barrier, len(peers))

    pending = []
    pack_copies = start_copies(
        [(pack.at[member], pack.at[member], {"view": p}) for p in view_peers], pack_sems
    )
    pending += pack_copies
    angles = choose_tiles(pattern_ref, angle_ref, choice, chosen, 64 * member - 32)
    loads[2].wait()
    prepare_weights(
        w1_ref, w2_ref, w3_ref, band1_ref, band3_ref, rep3_ref, t1v, t1b, t3t, t3, t1t, w2r, w2t
    )
    loads[0].wait()
    loads[1].wait()
    loads[3].wait()
    wait_in(pack_copies)
    plane_copies = start_copies(
        [
            (pack.at[:, pl.ds(0, 2)], pack_low, {"slab": above}),
            (pack.at[:, pl.ds(0, 2)], pack_high, {"slab": below}),
        ],
        plane_sems,
    )
    pending += plane_copies

    field_rows = pack[:, 0].reshape(128, 128)
    got = project(field_rows, choice, angles, response_ref, pick_x_ref, place_ref)
    gain_rows = doubled_rows(pack, 3)
    dual = (gain_rows * (got - doubled_rows(pack, 2))).astype(BF16).astype(F32)
    spread = backproject(dual, chosen, angles, response_ref, pick_j_ref, spread_x_ref, 128)
    for z in range(4):
        for yt in range(4):
            fields[2, 4 + z, 4 * yt : 4 * yt + 4, :] = spread[
                4 * z : 4 * z + 4, 128 * yt : 128 * yt + 128
            ]
    back_copies = start_copies(
        [
            (fields.at[2, pl.ds(5, 3)], fields.at[2, pl.ds(1, 3)], {"slab": above}),
            (fields.at[2, pl.ds(4, 3)], fields.at[2, pl.ds(8, 3)], {"slab": below}),
        ],
        back_sems,
    )
    pending += back_copies

    wait_in(plane_copies)
    low_z, low_y = 4 * slab - 4, 8 * member - 4
    lane16 = iota((16, 128), 1)
    global_y = iota((16, 128), 0) + low_y
    inside_y = (global_y >= 0) & (global_y < height)
    lane8 = iota((8, 128), 1)
    for field in range(2):
        for source, first, low in ((pack_low, 1, 0), (pack, 4, 4), (pack_high, 8, 8)):
            own, before, after = (
                source[view, field].astype(F32) for view in (member, left, right)
            )
            for z in range(first, min(low + 4, 11)):
                at = 8 * (z - low)
                fields[field, z, 4:12, :] = own[at : at + 8]
                fields[field, z, 0:4, :] = before[at + 4 : at + 8]
                fields[field, z, 12:16, :] = after[at : at + 4]

    def shifts_of(field, target):
        def one_plane(z, carry):
            inside = inside_y & (z + low_z >= 0) & (z + low_z < depth)
            plane = jnp.where(inside, fields[field, z], 0.0)
            plane = plane.astype(BF16).astype(F32)
            for e in range(3):
                target[z, 16 * e : 16 * e + 16, :] = shifted(plane, e, lane16).astype(BF16)
            return carry

        lax.fori_loop(1, 11, one_plane, 0, unroll=2)

    shifts_of(0, ins)
    shifts_of(1, ups)
    ups_own[...] = jnp.zeros(ups_own.shape, F32)
    for z in range(4):
        plane = upstream_ref[z].astype(F32)
        for e in range(3):
            ups_own[2 + z, e] = shifted(plane, 2 - e, lane8)

    def third_turned(p, carry):
        z = 2 * p
        out = mm(t3t[:, :144], pair_of(ups, z + 2, 3))
        ct3[z] = out[:, :128]
        ct3[z + 1] = out[:, 128:]
        return carry

    lax.fori_loop(0, 3, third_turned, 0)
    eye32 = iota((32, 32), 0) == iota((32, 32), 1)
    bias1 = jnp.sum(jnp.where(eye32, bias1_ref[...], 0.0), axis=1, keepdims=True)
    bias2 = jnp.sum(jnp.where(eye32, bias2_ref[...], 0.0), axis=1, keepdims=True)
    bias1_rows = jnp.concatenate([jnp.broadcast_to(bias1, (32, 128))] * 12, axis=0)

    def first_volume(p, carry):
        z = 2 * p
        out = mm(t1v[:, :144], pair_of(ins, z + 1, 3))
        pre1[z] = out[:, :128] + bias1_rows
        pre1[z + 1] = out[:, 128:] + bias1_rows
        return carry

    lax.fori_loop(0, 4, first_volume, 0)
    s2z[...] = jnp.zeros(s2z.shape, BF16)
    g2[...] = jnp.zeros(g2.shape, F32)
    g3[...] = jnp.zeros(g3.shape, F32)

    wait_in(back_copies)
    shifts_of(2, backs)

    def first_back(p, carry):
        z = 2 * p
        out = mm(t1b[:, :144], pair_of(backs, z + 1, 3))
        pre1[z] += out[:, :128]
        pre1[z + 1] += out[:, 128:]
        return carry

    lax.fori_loop(0, 4, first_back, 0)

    lane384 = iota((384, 128), 1)
    row_y1 = iota((384, 128), 0) // 32 + low_y + 2
    inside1 = (row_y1 >= 0) & (row_y1 < height)

    def activate(z, keep_slope):
        value = pre1[z]
        gate = 0.5 * jnp.tanh(0.5 * value) + 0.5
        act = value * gate
        if keep_slope:
            pre1[z] = gate + act * (1.0 - gate)
        inside = inside1 & (z + low_z + 2 >= 0) & (z + low_z + 2 < depth)
        act = jnp.where(inside, act, 0.0)
        for e in range(3):
            h3[z, :, 32 * e : 32 * e + 32, :] = (
                shifted(act, e, lane384).astype(BF16).reshape(12, 32, 128)
            )

    def activate_outer(n, carry):
        activate(n + 4 * (n // 2), False)
        return carry

    def activate_inner(n, carry):
        activate(n + 2, True)
        return carry

    lax.fori_loop(0, 4, activate_outer, 0)
    lax.fori_loop(0, 4, activate_inner, 0)

    lane32 = iota((32, 128), 1)

    def second(y, carry):
        out = split_pairs([mm(w2r[:, :288], stacked_rows(h3, 2 * p, y)) for p in range(4)])
        ok_y = (y + low_y + 3 >= 0) & (y + low_y + 3 < height)
        at = pl.multiple_of(32 * y, 32)
        for z in range(6):
            value = out[z][:32] + out[z + 1][32:64] + out[z + 2][64:] + bias2
            gate = 0.5 * jnp.tanh(0.5 * value) + 0.5
            act = value * gate
            slope = gate + act * (1.0 - gate)
            ok = ok_y & (z + low_z + 3 >= 0) & (z + low_z + 3 < depth)
            live = jnp.where(ok, 1.0, 0.0)
            h2[z, pl.ds(at, 32), :] = (act * live).astype(BF16)
            slope = slope * ct3[z, pl.ds(at, 32), :] * live
            for e in range(3):
                s3[z, y, 32 * e : 32 * e + 32, :] = shifted(slope, e, lane32).astype(BF16)
        return carry

    lax.fori_loop(0, 10, second, 0)

    for z in range(4):
        s2z[z + 2] = s3[z + 1, 1:9, 32:64, :]
    ones = jnp.ones((16, 768), BF16)

    def second_grad(y, carry):
        turned = jnp.concatenate(
            [
                jnp.concatenate([s2z[z + 1 - a, y] for z in range(1, 7)], axis=1)
                for a in range(3)
            ],
            axis=0,
        )
        plain = jnp.concatenate(
            [h3[z, pl.ds(y + 1, 3)].reshape(288, 128) for z in range(1, 7)], axis=1
        )
        g2[:, :304] += mmt(turned, jnp.concatenate([plain, ones], axis=0))
        return carry

    lax.fori_loop(0, 8, second_grad, 0)

    turned = jnp.concatenate(
        [
            jnp.concatenate(
                [ups_own[z + 2 - a, e] for a in range(3) for e in range(3)], axis=0
            ).astype(BF16)
            for z in range(6)
        ],
        axis=1,
    )
    plain = jnp.concatenate([h2[z] for z in range(6)], axis=1)
    cross = mmt(turned, plain)
    step10 = iota((8, 320), 1) // 32 - iota((8, 320), 0)
    for a in range(3):
        for e in range(3):
            block = cross[8 * (3 * a + e) : 8 * (3 * a + e) + 8]
            for b in range(3):
                g3[e, 3 * a + b : 3 * a + b + 1, 0:320] = jnp.sum(
                    jnp.where(step10 == b, block, 0.0), axis=0, keepdims=True
                )
    loads[4].wait()
    loads[5].wait()
    third = jnp.zeros((16, 128), F32)
    for e in range(3):
        value = g3[e]
        high = value.astype(BF16)
        rest = (value - high.astype(F32)).astype(BF16)
        third = third + mm(high, fold3_ref[e]) + mm(rest, fold3_ref[e])

    lanes = iota((32, 128), 1)
    for tap in range(9):
        a, b = tap // 3, tap % 3
        block = g2[32 * a : 32 * a + 32, :]
        if b:
            block = pltpu.roll(block, 384 - 96 * b, 1)
        totals[32 * tap : 32 * tap + 32, :] = jnp.where(
            lanes < (97 if b == 2 else 96), block[:, :128], 0.0
        )
    totals[288:304, :] = third
    totals[304:320, :] = jnp.zeros((16, 128), F32)
    for n in range(RING):
        sums[n] = totals[PIECE * n : PIECE * n + PIECE, :].astype(BF16)
    ring_in[place] = sums[place]
    ring_copies = start_copies(
        [(sums.at[lax.rem(peer, RING)], ring_in.at[place], {"slab": peer}) for peer in ring_peers],
        ring_sems,
    )
    pending += ring_copies

    def second_turned(y, carry):
        out = split_pairs([mm(w2t[:, :288], stacked_rows(s3, 2 * p, y)) for p in range(3)])
        at = pl.multiple_of(32 * y, 32)
        from_ = pl.multiple_of(32 * y + 64, 32)
        for z in range(4):
            value = out[z][:32] + out[z + 1][32:64] + out[z + 2][64:]
            s1[z, pl.ds(at, 32), :] = (value * pre1[z + 2, pl.ds(from_, 32), :]).astype(BF16)
        return carry

    lax.fori_loop(0, 8, second_turned, 0)

    out = split_pairs([mm(t1t[...], pair_of(s1, 2 * p, 1)) for p in range(2)])
    for c in range(2):
        for z in range(-1, 5):
            total = jnp.zeros((16, 128), F32)
            for e in range(3):
                part = jnp.zeros((16, 128), F32)
                for a in range(3):
                    if 0 <= z + a - 1 < 4:
                        at = 16 * ((a * 2 + c) * 3 + e)
                        part = part + out[z + a - 1][at : at + 16]
                total = total + shifted(part, e, lane16)
            if z == -1:
                edges[0, c] = total.astype(BF16)
            elif z == 4:
                edges[1, c] = total.astype(BF16)
            else:
                parts_own[c, z] = total
    edge_copies = start_copies(
        [
            (edges.at[1], edges_low, {"slab": above}),
            (edges.at[0], edges_high, {"slab": below}),
        ],
        edge_sems,
    )
    pending += edge_copies

    turned = jnp.concatenate([s1[z] for z in range(4)], axis=1)
    plain = jnp.concatenate(
        [
            jnp.concatenate(
                [ins[z + 3 + a] for a in range(3)]
                + [backs[z + 3 + a] for a in range(3)]
                + [jnp.ones((96, 128), BF16)],
                axis=0,
            )
            for z in range(4)
        ],
        axis=1,
    )
    cross = mmt(turned, plain)
    total = cross[:32]
    for yo in range(1, 8):
        total = total + pltpu.roll(cross[32 * yo : 32 * yo + 32], 384 - yo, 1)
    high = total.astype(BF16)
    rest = (total - high.astype(F32)).astype(BF16)
    view_in[member, 0:SMALL, :] = (mm(high, fold1_ref[...]) + mm(rest, fold1_ref[...])).astype(BF16)

    wait_in(ring_copies)
    ring_total = ring_in[0].astype(F32)
    for n in range(1, RING):
        ring_total = ring_total + ring_in[n].astype(F32)
    view_in[member, SMALL:, :] = ring_total.astype(BF16)
    view_copies = start_copies(
        [(view_in.at[member], view_in.at[member], {"view": p}) for p in view_peers], view_sems
    )

    wait_in(edge_copies)
    has_low = jnp.where(slab > 0, 1.0, 0.0)
    has_high = jnp.where(slab < SLABS - 1, 1.0, 0.0)
    for c in (1, 0):
        parts_own[c, 0] += has_low * edges_low[c].astype(F32)
        parts_own[c, 3] += has_high * edges_high[c].astype(F32)
        (parts if c else parts_side)[member] = parts_own[c].astype(BF16)
    part_copies = start_copies(
        [(parts.at[member], parts.at[member], {"view": p}) for p in view_peers], part_sems
    )
    side_copies = start_copies(
        [(parts_side.at[member], parts_side.at[member], {"view": p}) for p in view_peers],
        side_sems,
    )
    pending += part_copies + side_copies

    t3_now = t3[:, :320].astype(BF16)
    out = split_pairs([mm(t3_now, pair_of(h2, 2 * p, 1)) for p in range(3)])
    for z in range(4):
        total = volume_ref[z]
        for e in range(3):
            part = jnp.zeros((8, 128), F32)
            for a in range(3):
                at = 8 * (3 * a + e)
                part = part + out[z + a][at : at + 8]
            total = total + shifted(part, e, lane8)
        new_ref[z] = total

    def sum_views():
        total = view_in[0].astype(F32)
        for n in range(1, VIEWS):
            total = total + view_in[n].astype(F32)
        return total.astype(BF16)

    wait_in(view_copies)
    layer_in[layer] = sum_views()
    layer_copies = start_copies(
        [(layer_in.at[layer], layer_in.at[layer], {"slab": p}) for p in layer_peers],
        layer_sems,
    )

    wait_in(part_copies)
    row8 = iota((8, 128), 0)
    rows = [None] * 16
    for z in range(4):
        planes = [parts[view, z].astype(F32) for view in range(VIEWS)]
        for view in range(VIEWS):
            value = planes[view][:8]
            if view > 0:
                value = value + jnp.where(row8 == 0, planes[view - 1][9:10], 0.0)
            if view < VIEWS - 1:
                value = value + jnp.where(row8 == 7, planes[view + 1][8:9], 0.0)
            rows[4 * view + z] = value
    field_rows = jnp.concatenate(rows, axis=0).astype(BF16)
    got = project(field_rows, choice, angles, response_ref, pick_x_ref, place_ref)
    wait_in(layer_copies)
    layer_total = layer_in[0].astype(F32)
    for n in range(1, LAYERS):
        layer_total = layer_total + layer_in[n].astype(F32)
    final_in[place] = layer_total.astype(BF16)
    final_copies = start_copies(
        [(final_in.at[place], final_in.at[place], {"slab": p}) for p in ring_peers],
        final_sems,
    )
    echo = (gain_rows * got).astype(BF16).astype(F32)
    spread = backproject(echo, chosen, angles, response_ref, pick_j_ref, spread_x_ref, 64)
    spread = spread[:, :256] + spread[:, 256:]
    wait_in(side_copies)
    has_left = jnp.where(member > 0, 1.0, 0.0)
    has_right = jnp.where(member < VIEWS - 1, 1.0, 0.0)
    for z in range(4):
        value = parts_own[0, z][:8] + upstream_ref[z].astype(F32)
        before = has_left * parts_side[left, z].astype(F32)[9:10]
        after = has_right * parts_side[right, z].astype(F32)[8:9]
        value = value + jnp.where(row8 == 0, before, 0.0) + jnp.where(row8 == 7, after, 0.0)
        for yt in range(2):
            grad_ref[z, 4 * yt : 4 * yt + 4, :] = (
                value[4 * yt : 4 * yt + 4, :]
                + spread[4 * z : 4 * z + 4, 128 * yt : 128 * yt + 128]
            )
    wait_out(pending)
    wait_in(final_copies)
    wait_out(view_copies + layer_copies + final_copies)


def emit_kernel(
    scale,
    new_ref,
    grad_ref,
    total_ref,
    new_out,
    grad_out,
    w1_out,
    bias1_out,
    w2_out,
    bias2_out,
    w3_out,
):
    new_out[...] = new_ref[...]
    grad_out[...] = grad_ref[...]
    whole = jnp.concatenate(
        [total_ref[n, SMALL:, :].astype(F32) for n in range(RING)], axis=0
    ) * scale
    small = total_ref[0, :SMALL, :].astype(F32)
    for n in range(1, RING):
        small = small + total_ref[n, :SMALL, :].astype(F32)
    turned = (small * scale).T
    bias1_out[...] = turned[54:55, :]
    for tap in range(9):
        block = whole[32 * tap : 32 * tap + 32]
        w2_out[tap] = block[:, :96]
        w1_out[tap] = turned[6 * tap : 6 * tap + 6, :]
        w3_out[tap] = whole[288 + tap : 289 + tap, :96]
    bias2_out[...] = whole[160:192].T[96:97, :]


def vmem_specs(count):
    return [pl.BlockSpec(memory_space=pltpu.VMEM)] * count


def body(volume, measured, dual_gain, pattern, angle, response, w1, bias1, w2, bias2, w3, upstream):
    pick_x, place, pick_j, spread_x = [jnp.asarray(x) for x in tile_constants()]
    band1, band3, rep3, fold1, fold3 = [jnp.asarray(x) for x in weight_constants()]
    dma = pltpu.SemaphoreType.DMA
    new_volume, grad_volume, total = pl.pallas_call(
        step_kernel,
        name="step",
        out_shape=(
            jax.ShapeDtypeStruct((4, 8, 128), F32),
            jax.ShapeDtypeStruct((4, 8, 128), F32),
            jax.ShapeDtypeStruct((RING, MESSAGE, 128), BF16),
        ),
        in_specs=vmem_specs(15) + [pl.BlockSpec(memory_space=HELD)] * 6,
        out_specs=tuple(vmem_specs(3)),
        scratch_shapes=[
            pltpu.VMEM((512, 1024), BF16),
            pltpu.VMEM((512, 1024), BF16),
            pltpu.VMEM((512, 512), BF16),
            pltpu.VMEM((3, 96, 384), BF16),
            pltpu.VMEM((384, 128), BF16),
            pltpu.VMEM((3, 384, 128), BF16),
            pltpu.VMEM((VIEWS, 4, 32, 128), BF16),
            pltpu.VMEM((VIEWS, 2, 32, 128), BF16),
            pltpu.VMEM((VIEWS, 2, 32, 128), BF16),
            pltpu.VMEM((4096, 256), BF16),
            pltpu.VMEM((256, 2048), BF16),
            pltpu.VMEM((3, 12, 16, 128), F32),
            pltpu.VMEM((12, 48, 128), BF16),
            pltpu.VMEM((12, 48, 128), BF16),
            pltpu.VMEM((12, 48, 128), BF16),
            pltpu.VMEM((8, 3, 8, 128), F32),
            pltpu.VMEM((384, 256), BF16),
            pltpu.VMEM((384, 256), BF16),
            pltpu.VMEM((320, 256), BF16),
            pltpu.VMEM((72, 384), F32),
            pltpu.VMEM((288, 256), BF16),
            pltpu.VMEM((96, 384), BF16),
            pltpu.VMEM((96, 384), BF16),
            pltpu.VMEM((8, 384, 128), F32),
            pltpu.VMEM((8, 12, 96, 128), BF16),
            pltpu.VMEM((6, 320, 128), F32),
            pltpu.VMEM((6, 320, 128), BF16),
            pltpu.VMEM((6, 10, 96, 128), BF16),
            pltpu.VMEM((8, 8, 32, 128), BF16),
            pltpu.VMEM((4, 256, 128), BF16),
            pltpu.VMEM((96, 384), F32),
            pltpu.VMEM((3, 16, 384), F32),
            pltpu.VMEM((2, 4, 16, 128), F32),
            pltpu.VMEM((VIEWS, 4, 16, 128), BF16),
            pltpu.VMEM((VIEWS, 4, 16, 128), BF16),
            pltpu.VMEM((2, 2, 16, 128), BF16),
            pltpu.VMEM((2, 16, 128), BF16),
            pltpu.VMEM((2, 16, 128), BF16),
            pltpu.VMEM((RING * PIECE, 128), F32),
            pltpu.VMEM((RING, PIECE, 128), BF16),
            pltpu.VMEM((RING, PIECE, 128), BF16),
            pltpu.VMEM((VIEWS, MESSAGE, 128), BF16),
            pltpu.VMEM((LAYERS, MESSAGE, 128), BF16),
            dma((6,)),
            dma((2, 3)),
            dma((2, 2)),
            dma((2, 2)),
            dma((2, 2)),
            dma((2, 3)),
            dma((2, 3)),
            dma((2, RING - 1)),
            dma((2, 3)),
            dma((2, 3)),
            dma((2, RING - 1)),
        ],
        compiler_params=pltpu.CompilerParams(
            collective_id=0, has_side_effects=True, vmem_limit_bytes=VMEM_BYTES
        ),
    )(
        volume,
        upstream,
        measured.reshape(32, 128),
        dual_gain.reshape(32, 128),
        pattern.transpose(0, 1, 3, 2).reshape(VIEWS, 16, 64),
        angle.reshape(VIEWS, 64),
        w1.transpose(0, 2, 1),
        bias1.reshape(1, 32),
        w2,
        bias2.reshape(1, 32),
        w3.reshape(9, 96),
        pick_x,
        pick_j,
        band1,
        band3,
        response,
        place,
        spread_x,
        rep3,
        fold1,
        fold3,
    )
    scale = 1.0 / math.sqrt(volume.size * SLABS * VIEWS)
    new_volume, grad_volume, grad_w1, grad_bias1, grad_w2, grad_bias2, grad_w3 = pl.pallas_call(
        functools.partial(emit_kernel, scale),
        name="emit",
        out_shape=(
            jax.ShapeDtypeStruct((4, 8, 128), F32),
            jax.ShapeDtypeStruct((4, 8, 128), F32),
            jax.ShapeDtypeStruct((9, 6, 32), F32),
            jax.ShapeDtypeStruct((1, 32), F32),
            jax.ShapeDtypeStruct((9, 32, 96), F32),
            jax.ShapeDtypeStruct((1, 32), F32),
            jax.ShapeDtypeStruct((9, 1, 96), F32),
        ),
        in_specs=vmem_specs(3),
        out_specs=tuple(vmem_specs(7)),
    )(new_volume, grad_volume, total)
    return (
        new_volume,
        grad_volume,
        grad_w1.transpose(0, 2, 1),
        grad_bias1.reshape(32),
        grad_w2,
        grad_bias2.reshape(32),
        grad_w3,
    )


def solution(mesh):
    placed = (
        P("slab", "view", None),
        P("view", "slab", None),
        P("view", "slab", None),
        P(None, "slab", None, None),
        P(None, "slab", None),
        P(),
        P(),
        P(),
        P(),
        P(),
        P(),
        P("slab", "view", None),
    )
    return jax.shard_map(
        body,
        mesh=mesh,
        in_specs=placed,
        out_specs=(P("slab", "view", None), P("slab", "view", None), P(), P(), P(), P(), P()),
        check_vma=False,
    )
```

```python
import functools
import math

import jax
import jax.numpy as jnp
import ml_dtypes
import numpy as np
from jax import lax
from jax.experimental import pallas as pl
from jax.experimental.pallas import tpu as pltpu
from jax.sharding import PartitionSpec as P

F32 = jnp.float32
BF16 = jnp.bfloat16
MESH = pl.DeviceIdType.MESH
VIEWS = 4
RING = 8
LAYERS = 4
SLABS = RING * LAYERS
PIECE = 40
SMALL = 32
MESSAGE = SMALL + PIECE
VMEM_BYTES = 56 * 1024 * 1024
HELD = pl.ANY


def mm(a, b):
    return lax.dot_general(a, b, (((1,), (0,)), ((), ())), preferred_element_type=F32)


def mmt(a, b):
    return lax.dot_general(a, b, (((1,), (1,)), ((), ())), preferred_element_type=F32)


def iota(shape, dim):
    return lax.broadcasted_iota(jnp.int32, shape, dim)


def one(cond):
    return jnp.where(cond, 1.0, 0.0).astype(BF16)


def host_bf16(cond):
    return np.asarray(cond, np.float32).astype(ml_dtypes.bfloat16)


def tile_constants():
    row, col = np.arange(128)[:, None], np.arange(128)[None, :]
    pick_x = host_bf16(col == 4 * (row % 32) + row // 32)
    r, c = np.arange(512)[:, None], np.arange(1024)[None, :]
    xi, quarter, z, y8 = r // 128, r // 32 % 4, r // 8 % 4, r % 8
    yt, j = c // 128, c % 64
    place = host_bf16(
        (2 * quarter + y8 // 4 == yt) & (z == j // 16) & (y8 % 4 == j // 4 % 4) & (xi == j % 4)
    )
    r, c = np.arange(64)[:, None], np.arange(128)[None, :]
    pick_j = host_bf16((c < 64) & (c % 4 == r // 16) & (c // 4 == r % 16))
    r, c = np.arange(512)[:, None], np.arange(512)[None, :]
    spread_x = host_bf16((r // 32 % 4 == c // 128) & (c % 128 == 4 * (r % 32) + r // 128))
    return pick_x, place, pick_j, spread_x


def weight_constants():
    lane = np.arange(384)
    band1 = np.zeros((2, 9, 6, 256), np.float32)
    fold1 = np.zeros((384, 128), np.float32)
    for a in range(3):
        for b in range(3):
            for e in range(3):
                for c in range(2):
                    band1[c, 3 * a + b, 2 * e + c, (a * 3 + e) * 16 + b] = 1.0
                    fold1[
                        ((c * 3 + a) * 3 + e) * 16 + 3 + b, 6 * (3 * a + b) + 2 * e + c
                    ] = 1.0
    fold1[288, 54] = 1.0
    band3 = np.zeros((3, 9, 256), np.float32)
    for a in range(3):
        for b in range(3):
            for e in range(3):
                band3[e, 3 * (2 - a) + (2 - b), (a * 3 + e) * 16 + b] = 1.0
    rep3 = np.zeros((3, 96, 384), np.float32)
    for e in range(3):
        rep3[e, 32 * e + lane % 32, lane] = 1.0
    fold3 = np.zeros((3, 384, 128), np.float32)
    for e in range(3):
        live = lane[lane < 320]
        fold3[e, live, 32 * e + live % 32] = 1.0
    return tuple(host_bf16(x) for x in (band1, band3, rep3, fold1, fold3))


def own_order():
    return one(iota((64, 64), 1) == 2 * (iota((64, 64), 0) % 32) + iota((64, 64), 0) // 32)


def choose_tiles(pattern_ref, angle_ref, choice, chosen, first):
    order = own_order()
    lanes = iota((64, 256), 1)
    lines = []
    for g in range(VIEWS):
        held = pattern_ref[g].astype(F32).astype(BF16)
        ids = mmt(order, held).astype(jnp.int32)
        for k in range(16):
            at = 256 * k + 64 * g
            choice[at : at + 64, :] = one(lanes == ids[:, k : k + 1])
        lines.append(mmt(held, order))
    line = jnp.concatenate(lines, axis=1).astype(jnp.int32)
    tile = iota((128, 256), 0) + first
    for k in range(16):
        at = 128 * (k % 2)
        chosen[at : at + 128, 256 * (k // 2) : 256 * (k // 2) + 256] = one(
            tile == line[k : k + 1, :]
        )
    angles = mmt(order, angle_ref[...].astype(F32).astype(BF16)).astype(jnp.int32)
    return jnp.concatenate([angles[:, g : g + 1] for g in range(VIEWS)], axis=0)


def project(field_rows, choice, angles, response_ref, pick_x_ref, place_ref):
    by_x = mmt(pick_x_ref[...], field_rows).astype(BF16)
    wide = jnp.concatenate([by_x[32 * i : 32 * i + 32] for i in range(4)], axis=1)
    spread = mm(wide, place_ref[...]).astype(BF16)
    tiles = jnp.concatenate([spread[:, 128 * i : 128 * i + 128] for i in range(8)], axis=0)
    low = iota((256, 128), 1) < 64
    pairs = []
    for p in range(8):
        picked = mm(choice[512 * p : 512 * p + 512, :], tiles)
        pairs.append(jnp.where(low, picked[:256], picked[256:]).astype(BF16))
    lines = mmt(jnp.concatenate(pairs, axis=1), response_ref[...])
    half = iota((256, 128), 1) // 64
    total = jnp.zeros((256, 128), F32)
    for p in range(4):
        total = total + jnp.where(angles == 2 * p + half, lines[:, 128 * p : 128 * p + 128], 0.0)
    return total + pltpu.roll(total, 64, 1)


def doubled_rows(ref, part):
    low = iota((32, 128), 1) < 64
    parts = []
    for g in range(VIEWS):
        rows = ref[g, part].astype(F32)
        turned = pltpu.roll(rows, 64, 1)
        parts.append(jnp.where(low, rows, turned))
        parts.append(jnp.where(low, turned, rows))
    return jnp.concatenate(parts, axis=0)


def backproject(doubled, chosen, angles, response_ref, pick_j_ref, spread_x_ref, count):
    half = iota((256, 128), 1) // 64
    masked = [
        jnp.where(angles == 2 * p + half, doubled, 0.0).astype(BF16) for p in range(4)
    ]
    contrib = mm(jnp.concatenate(masked, axis=1), response_ref[...])
    high = contrib.astype(BF16)
    rest = (contrib - high.astype(F32)).astype(BF16)
    stacked = jnp.concatenate(
        [
            jnp.concatenate(
                [high[:, 128 * p : 128 * p + 128], rest[:, 128 * p : 128 * p + 128]], axis=1
            )
            for p in range(8)
        ],
        axis=0,
    )
    skip = (128 - count) // 2
    left = jnp.concatenate(
        [chosen[skip : skip + count, :], chosen[128 + skip : 128 + skip + count, :]], axis=0
    )
    sums = mm(left, stacked)
    sums = sums[:, :128] + sums[:, 128:]
    tiles = sums[:count] + pltpu.roll(sums[count:], 64, 1)
    top = tiles.astype(BF16)
    if count == 64:
        top = jnp.concatenate([top, (tiles - top.astype(F32)).astype(BF16)], axis=0)
    by_j = mmt(pick_j_ref[...], top).astype(BF16)
    wide = jnp.concatenate([by_j[16 * i : 16 * i + 16] for i in range(4)], axis=1)
    return mm(wide, spread_x_ref[...])


def start_copies(pairs, sems):
    copies = []
    for n, (source, target, device) in enumerate(pairs):
        copies.append(
            pltpu.make_async_remote_copy(
                src_ref=source,
                dst_ref=target,
                send_sem=sems.at[0, n],
                recv_sem=sems.at[1, n],
                device_id=device,
                device_id_type=MESH,
            )
        )
    for copy in copies:
        copy.start()
    return copies


def wait_in(copies):
    for copy in copies:
        copy.wait_recv()


def wait_out(copies):
    for copy in copies:
        copy.wait_send()


def shifted(value, e, lane):
    if e == 1:
        return value
    if e == 0:
        return jnp.where(lane == 0, 0.0, pltpu.roll(value, 1, 1))
    return jnp.where(lane == 127, 0.0, pltpu.roll(value, 127, 1))


def prepare_weights(
    w1_ref, w2_ref, w3_ref, band1_ref, band3_ref, rep3_ref, t1v, t1b, t3t, t3, t1t, w2r, w2t
):
    eye32 = one(iota((32, 32), 0) == iota((32, 32), 1))
    for c, ref in ((0, t1v), (1, t1b)):
        base = jnp.zeros((32, 256), F32)
        for tap in range(9):
            turned = mmt(eye32, w1_ref[tap]).astype(BF16)
            base = base + mm(turned, band1_ref[c, tap])
        for yo in range(12):
            ref[32 * yo : 32 * yo + 32, :] = pltpu.roll(base, yo + 1, 1).astype(BF16)
    eye96 = one(iota((96, 96), 0) == iota((96, 96), 1))
    w3 = w3_ref[...]
    w3_turned = mmt(eye96, w3).astype(BF16)
    base = jnp.zeros((32, 256), F32)
    for e in range(3):
        base = base + mm(w3_turned[32 * (2 - e) : 32 * (2 - e) + 32], band3_ref[e])
    for yo in range(10):
        t3t[32 * yo : 32 * yo + 32, :] = pltpu.roll(base, yo + 2, 1).astype(BF16)
    step = iota((8, 384), 1) // 32 - iota((8, 384), 0)
    for e in range(3):
        line = mm(w3, rep3_ref[e])
        for a in range(3):
            block = jnp.zeros((8, 384), F32)
            for b in range(3):
                block = block + jnp.where(step == b, line[3 * a + b : 3 * a + b + 1, :], 0.0)
            t3[8 * (3 * a + e) : 8 * (3 * a + e) + 8, :] = block
    rep = one(iota((32, 256), 0) == iota((32, 256), 1) % 32)
    turned = [mm(w1_ref[tap], rep) for tap in range(9)]
    row16 = iota((16, 256), 0)
    row_y = jnp.where(row16 < 8, row16, jnp.where(row16 == 8, -1, 8))
    step = iota((16, 256), 1) // 32 - row_y + 1
    step = jnp.where(row16 < 10, step, -1)
    for a in range(3):
        for c in range(2):
            for e in range(3):
                row = 2 * (2 - e) + c
                block = jnp.zeros((16, 256), F32)
                for b in range(3):
                    tap = 3 * (2 - a) + (2 - b)
                    block = block + jnp.where(step == b, turned[tap][row : row + 1, :], 0.0)
                at = 16 * ((a * 2 + c) * 3 + e)
                t1t[at : at + 16, :] = block.astype(BF16)
    places = [one(iota((96, 384), 1) == iota((96, 384), 0) + 96 * b) for b in range(3)]
    keep = iota((96, 96), 1) // 32 == 2 - iota((96, 96), 0) // 32
    same = one(iota((32, 96), 0) == iota((32, 96), 1) % 32)
    for a in range(3):
        plain = jnp.zeros((32, 384), F32)
        across = jnp.zeros((32, 384), F32)
        for b in range(3):
            plain = plain + mm(w2_ref[3 * a + b], places[b])
            tower = jnp.concatenate([w2_ref[3 * (2 - a) + (2 - b)].astype(F32)] * 3, axis=0)
            tower = jnp.where(keep, tower, 0.0).astype(BF16)
            across = across + mm(mmt(same, tower).astype(BF16), places[b])
        w2r[32 * a : 32 * a + 32, :] = plain.astype(BF16)
        w2t[32 * a : 32 * a + 32, :] = across.astype(BF16)


def pair_of(ref, z, count):
    cols = [jnp.concatenate([ref[z + n + a] for a in range(count)], axis=0) for n in range(2)]
    return jnp.concatenate(cols, axis=1)


def stacked_rows(ref, z, y):
    cols = [ref[z + n, pl.ds(y, 3)].reshape(288, 128) for n in range(2)]
    return jnp.concatenate(cols, axis=1)


def split_pairs(outs):
    return [out[:, 128 * n : 128 * n + 128] for out in outs for n in range(2)]


def step_kernel(
    volume_hbm,
    upstream_hbm,
    measured_hbm,
    gain_hbm,
    pattern_hbm,
    angle_hbm,
    w1_hbm,
    bias1_hbm,
    w2_hbm,
    bias2_hbm,
    w3_hbm,
    pick_x_hbm,
    pick_j_hbm,
    band1_hbm,
    band3_hbm,
    response_hbm,
    place_hbm,
    spread_x_hbm,
    rep3_hbm,
    fold1_hbm,
    fold3_hbm,
    new_ref,
    grad_ref,
    final_in,
    volume_ref,
    upstream_ref,
    measured_ref,
    gain_ref,
    pattern_ref,
    angle_ref,
    w1_ref,
    bias1_ref,
    w2_ref,
    bias2_ref,
    w3_ref,
    pick_x_ref,
    pick_j_ref,
    band1_ref,
    band3_ref,
    response_ref,
    place_ref,
    spread_x_ref,
    rep3_ref,
    fold1_ref,
    fold3_ref,
    pack,
    pack_low,
    pack_high,
    choice,
    chosen,
    fields,
    ins,
    backs,
    ups,
    ups_own,
    t1v,
    t1b,
    t3t,
    t3,
    t1t,
    w2r,
    w2t,
    pre1,
    h3,
    ct3,
    h2,
    s3,
    s2z,
    s1,
    g2,
    g3,
    parts_own,
    parts,
    parts_side,
    edges,
    edges_low,
    edges_high,
    totals,
    sums,
    ring_in,
    view_in,
    layer_in,
    local_sems,
    pack_sems,
    plane_sems,
    back_sems,
    edge_sems,
    part_sems,
    side_sems,
    ring_sems,
    view_sems,
    layer_sems,
    final_sems,
):
    slab, member = lax.axis_index("slab"), lax.axis_index("view")
    above, below = lax.rem(slab + 1, SLABS), lax.rem(slab + SLABS - 1, SLABS)
    left, right = lax.rem(member + VIEWS - 1, VIEWS), lax.rem(member + 1, VIEWS)
    place, layer = lax.rem(slab, RING), lax.div(slab, RING)
    view_peers = [
        VIEWS - 1 - member,
        lax.rem(member + 2, VIEWS),
        member + 1 - 2 * lax.rem(member, 2),
    ]
    ring_peers = [layer * RING + lax.rem(place + off, RING) for off in range(1, RING)]
    layer_peers = [
        lax.rem(layer + off, LAYERS) * RING + place for off in range(1, LAYERS)
    ]
    depth, height = 4 * SLABS, 8 * VIEWS

    barrier = pltpu.get_barrier_semaphore()
    peers = [{"view": peer} for peer in view_peers]
    peers += [{"slab": peer} for peer in ring_peers + layer_peers + [above, below]]
    for peer in peers:
        pl.semaphore_signal(barrier, inc=1, device_id=peer, device_id_type=MESH)

    loads = {}
    for n, (name, source, target) in enumerate(
        (
            ("volume", volume_hbm, volume_ref),
            ("upstream", upstream_hbm, upstream_ref),
            ("measured", measured_hbm, measured_ref),
            ("gain", gain_hbm, gain_ref),
            ("pattern", pattern_hbm, pattern_ref),
            ("angle", angle_hbm, angle_ref),
            ("w1", w1_hbm, w1_ref),
            ("w2", w2_hbm, w2_ref),
            ("w3", w3_hbm, w3_ref),
            ("band1", band1_hbm, band1_ref),
            ("band3", band3_hbm, band3_ref),
            ("rep3", rep3_hbm, rep3_ref),
            ("pick_x", pick_x_hbm, pick_x_ref),
            ("place", place_hbm, place_ref),
            ("response", response_hbm, response_ref),
            ("pick_j", pick_j_hbm, pick_j_ref),
            ("spread_x", spread_x_hbm, spread_x_ref),
            ("bias1", bias1_hbm, bias1_ref),
            ("bias2", bias2_hbm, bias2_ref),
            ("fold3", fold3_hbm, fold3_ref),
            ("fold1", fold1_hbm, fold1_ref),
        )
    ):
        loads[name] = pltpu.make_async_copy(source, target, local_sems.at[n])
        loads[name].start()

    def loaded(*which):
        for name in which:
            loads[name].wait()

    loaded("volume", "upstream", "measured", "gain")
    pack[member, 0] = volume_ref[...].reshape(32, 128).astype(BF16)
    pack[member, 1] = upstream_ref[...].astype(F32).reshape(32, 128).astype(BF16)
    pack[member, 2] = measured_ref[...].astype(BF16)
    pack[member, 3] = gain_ref[...].astype(BF16)
    pl.semaphore_wait(barrier, len(peers))

    pending = []
    pack_copies = start_copies(
        [(pack.at[member], pack.at[member], {"view": p}) for p in view_peers], pack_sems
    )
    pending += pack_copies
    loaded("pattern", "angle")
    angles = choose_tiles(pattern_ref, angle_ref, choice, chosen, 64 * member - 32)
    loaded("w1", "w2", "w3", "band1", "band3", "rep3")
    prepare_weights(
        w1_ref, w2_ref, w3_ref, band1_ref, band3_ref, rep3_ref, t1v, t1b, t3t, t3, t1t, w2r, w2t
    )
    loaded("pick_x", "place", "response", "pick_j", "spread_x", "bias1", "bias2")
    wait_in(pack_copies)
    plane_copies = start_copies(
        [
            (pack.at[:, pl.ds(0, 2)], pack_low, {"slab": above}),
            (pack.at[:, pl.ds(0, 2)], pack_high, {"slab": below}),
        ],
        plane_sems,
    )
    pending += plane_copies

    field_rows = pack[:, 0].reshape(128, 128)
    got = project(field_rows, choice, angles, response_ref, pick_x_ref, place_ref)
    gain_rows = doubled_rows(pack, 3)
    dual = (gain_rows * (got - doubled_rows(pack, 2))).astype(BF16).astype(F32)
    spread = backproject(dual, chosen, angles, response_ref, pick_j_ref, spread_x_ref, 128)
    for z in range(4):
        for yt in range(4):
            fields[2, 4 + z, 4 * yt : 4 * yt + 4, :] = spread[
                4 * z : 4 * z + 4, 128 * yt : 128 * yt + 128
            ]
    back_copies = start_copies(
        [
            (fields.at[2, pl.ds(5, 3)], fields.at[2, pl.ds(1, 3)], {"slab": above}),
            (fields.at[2, pl.ds(4, 3)], fields.at[2, pl.ds(8, 3)], {"slab": below}),
        ],
        back_sems,
    )
    pending += back_copies

    wait_in(plane_copies)
    low_z, low_y = 4 * slab - 4, 8 * member - 4
    lane16 = iota((16, 128), 1)
    global_y = iota((16, 128), 0) + low_y
    inside_y = (global_y >= 0) & (global_y < height)
    lane8 = iota((8, 128), 1)
    for field in range(2):
        for source, first, low in ((pack_low, 1, 0), (pack, 4, 4), (pack_high, 8, 8)):
            own, before, after = (
                source[view, field].astype(F32) for view in (member, left, right)
            )
            for z in range(first, min(low + 4, 11)):
                at = 8 * (z - low)
                fields[field, z, 4:12, :] = own[at : at + 8]
                fields[field, z, 0:4, :] = before[at + 4 : at + 8]
                fields[field, z, 12:16, :] = after[at : at + 4]

    def shifts_of(field, target):
        def one_plane(z, carry):
            inside = inside_y & (z + low_z >= 0) & (z + low_z < depth)
            plane = jnp.where(inside, fields[field, z], 0.0)
            plane = plane.astype(BF16).astype(F32)
            for e in range(3):
                target[z, 16 * e : 16 * e + 16, :] = shifted(plane, e, lane16).astype(BF16)
            return carry

        lax.fori_loop(1, 11, one_plane, 0, unroll=10)

    shifts_of(0, ins)
    shifts_of(1, ups)
    ups_own[...] = jnp.zeros(ups_own.shape, F32)
    for z in range(4):
        plane = upstream_ref[z].astype(F32)
        for e in range(3):
            ups_own[2 + z, e] = shifted(plane, 2 - e, lane8)

    def third_turned(p, carry):
        z = 2 * p
        out = mm(t3t[:, :144], pair_of(ups, z + 2, 3))
        ct3[z] = out[:, :128]
        ct3[z + 1] = out[:, 128:]
        return carry

    lax.fori_loop(0, 3, third_turned, 0, unroll=3)
    eye32 = iota((32, 32), 0) == iota((32, 32), 1)
    bias1 = jnp.sum(jnp.where(eye32, bias1_ref[...], 0.0), axis=1, keepdims=True)
    bias2 = jnp.sum(jnp.where(eye32, bias2_ref[...], 0.0), axis=1, keepdims=True)
    bias1_rows = jnp.concatenate([jnp.broadcast_to(bias1, (32, 128))] * 12, axis=0)

    def first_volume(p, carry):
        z = 2 * p
        out = mm(t1v[:, :144], pair_of(ins, z + 1, 3))
        pre1[z] = out[:, :128] + bias1_rows
        pre1[z + 1] = out[:, 128:] + bias1_rows
        return carry

    lax.fori_loop(0, 4, first_volume, 0, unroll=4)
    s2z[...] = jnp.zeros(s2z.shape, BF16)
    g2[...] = jnp.zeros(g2.shape, F32)
    g3[...] = jnp.zeros(g3.shape, F32)

    wait_in(back_copies)
    shifts_of(2, backs)

    def first_back(p, carry):
        z = 2 * p
        out = mm(t1b[:, :144], pair_of(backs, z + 1, 3))
        pre1[z] += out[:, :128]
        pre1[z + 1] += out[:, 128:]
        return carry

    lax.fori_loop(0, 4, first_back, 0, unroll=4)

    lane384 = iota((384, 128), 1)
    row_y1 = iota((384, 128), 0) // 32 + low_y + 2
    inside1 = (row_y1 >= 0) & (row_y1 < height)

    def activate(z, keep_slope):
        value = pre1[z]
        gate = 0.5 * jnp.tanh(0.5 * value) + 0.5
        act = value * gate
        if keep_slope:
            pre1[z] = gate + act * (1.0 - gate)
        inside = inside1 & (z + low_z + 2 >= 0) & (z + low_z + 2 < depth)
        act = jnp.where(inside, act, 0.0)
        for e in range(3):
            h3[z, :, 32 * e : 32 * e + 32, :] = (
                shifted(act, e, lane384).astype(BF16).reshape(12, 32, 128)
            )

    def activate_outer(n, carry):
        activate(n + 4 * (n // 2), False)
        return carry

    def activate_inner(n, carry):
        activate(n + 2, True)
        return carry

    lax.fori_loop(0, 4, activate_outer, 0, unroll=4)
    lax.fori_loop(0, 4, activate_inner, 0, unroll=4)

    lane32 = iota((32, 128), 1)

    def second(y, carry):
        out = split_pairs([mm(w2r[:, :288], stacked_rows(h3, 2 * p, y)) for p in range(4)])
        ok_y = (y + low_y + 3 >= 0) & (y + low_y + 3 < height)
        at = pl.multiple_of(32 * y, 32)
        for z in range(6):
            value = out[z][:32] + out[z + 1][32:64] + out[z + 2][64:] + bias2
            gate = 0.5 * jnp.tanh(0.5 * value) + 0.5
            act = value * gate
            slope = gate + act * (1.0 - gate)
            ok = ok_y & (z + low_z + 3 >= 0) & (z + low_z + 3 < depth)
            live = jnp.where(ok, 1.0, 0.0)
            h2[z, pl.ds(at, 32), :] = (act * live).astype(BF16)
            slope = slope * ct3[z, pl.ds(at, 32), :] * live
            for e in range(3):
                s3[z, y, 32 * e : 32 * e + 32, :] = shifted(slope, e, lane32).astype(BF16)
        return carry

    lax.fori_loop(0, 10, second, 0, unroll=10)

    for z in range(4):
        s2z[z + 2] = s3[z + 1, 1:9, 32:64, :]
    ones = jnp.ones((16, 768), BF16)

    def second_grad(y, carry):
        turned = jnp.concatenate(
            [
                jnp.concatenate([s2z[z + 1 - a, y] for z in range(1, 7)], axis=1)
                for a in range(3)
            ],
            axis=0,
        )
        plain = jnp.concatenate(
            [h3[z, pl.ds(y + 1, 3)].reshape(288, 128) for z in range(1, 7)], axis=1
        )
        g2[:, :304] += mmt(turned, jnp.concatenate([plain, ones], axis=0))
        return carry

    lax.fori_loop(0, 8, second_grad, 0, unroll=8)

    turned = jnp.concatenate(
        [
            jnp.concatenate(
                [ups_own[z + 2 - a, e] for a in range(3) for e in range(3)], axis=0
            ).astype(BF16)
            for z in range(6)
        ],
        axis=1,
    )
    plain = jnp.concatenate([h2[z] for z in range(6)], axis=1)
    cross = mmt(turned, plain)
    step10 = iota((8, 320), 1) // 32 - iota((8, 320), 0)
    for a in range(3):
        for e in range(3):
            block = cross[8 * (3 * a + e) : 8 * (3 * a + e) + 8]
            for b in range(3):
                g3[e, 3 * a + b : 3 * a + b + 1, 0:320] = jnp.sum(
                    jnp.where(step10 == b, block, 0.0), axis=0, keepdims=True
                )
    loaded("fold1", "fold3")
    third = jnp.zeros((16, 128), F32)
    for e in range(3):
        value = g3[e]
        high = value.astype(BF16)
        rest = (value - high.astype(F32)).astype(BF16)
        third = third + mm(high, fold3_ref[e]) + mm(rest, fold3_ref[e])

    lanes = iota((32, 128), 1)
    for tap in range(9):
        a, b = tap // 3, tap % 3
        block = g2[32 * a : 32 * a + 32, :]
        if b:
            block = pltpu.roll(block, 384 - 96 * b, 1)
        totals[32 * tap : 32 * tap + 32, :] = jnp.where(
            lanes < (97 if b == 2 else 96), block[:, :128], 0.0
        )
    totals[288:304, :] = third
    totals[304:320, :] = jnp.zeros((16, 128), F32)
    for n in range(RING):
        sums[n] = totals[PIECE * n : PIECE * n + PIECE, :].astype(BF16)
    ring_in[place] = sums[place]
    ring_copies = start_copies(
        [(sums.at[lax.rem(peer, RING)], ring_in.at[place], {"slab": peer}) for peer in ring_peers],
        ring_sems,
    )
    pending += ring_copies

    def second_turned(y, carry):
        out = split_pairs([mm(w2t[:, :288], stacked_rows(s3, 2 * p, y)) for p in range(3)])
        at = pl.multiple_of(32 * y, 32)
        from_ = pl.multiple_of(32 * y + 64, 32)
        for z in range(4):
            value = out[z][:32] + out[z + 1][32:64] + out[z + 2][64:]
            s1[z, pl.ds(at, 32), :] = (value * pre1[z + 2, pl.ds(from_, 32), :]).astype(BF16)
        return carry

    lax.fori_loop(0, 8, second_turned, 0, unroll=8)

    out = split_pairs([mm(t1t[...], pair_of(s1, 2 * p, 1)) for p in range(2)])
    for c in range(2):
        for z in range(-1, 5):
            total = jnp.zeros((16, 128), F32)
            for e in range(3):
                part = jnp.zeros((16, 128), F32)
                for a in range(3):
                    if 0 <= z + a - 1 < 4:
                        at = 16 * ((a * 2 + c) * 3 + e)
                        part = part + out[z + a - 1][at : at + 16]
                total = total + shifted(part, e, lane16)
            if z == -1:
                edges[0, c] = total.astype(BF16)
            elif z == 4:
                edges[1, c] = total.astype(BF16)
            else:
                parts_own[c, z] = total
    edge_copies = start_copies(
        [
            (edges.at[1], edges_low, {"slab": above}),
            (edges.at[0], edges_high, {"slab": below}),
        ],
        edge_sems,
    )
    pending += edge_copies

    turned = jnp.concatenate([s1[z] for z in range(4)], axis=1)
    plain = jnp.concatenate(
        [
            jnp.concatenate(
                [ins[z + 3 + a] for a in range(3)]
                + [backs[z + 3 + a] for a in range(3)]
                + [jnp.ones((96, 128), BF16)],
                axis=0,
            )
            for z in range(4)
        ],
        axis=1,
    )
    cross = mmt(turned, plain)
    total = cross[:32]
    for yo in range(1, 8):
        total = total + pltpu.roll(cross[32 * yo : 32 * yo + 32], 384 - yo, 1)
    high = total.astype(BF16)
    rest = (total - high.astype(F32)).astype(BF16)
    view_in[member, 0:SMALL, :] = (mm(high, fold1_ref[...]) + mm(rest, fold1_ref[...])).astype(BF16)

    wait_in(ring_copies)
    ring_total = ring_in[0].astype(F32)
    for n in range(1, RING):
        ring_total = ring_total + ring_in[n].astype(F32)
    view_in[member, SMALL:, :] = ring_total.astype(BF16)
    view_copies = start_copies(
        [(view_in.at[member], view_in.at[member], {"view": p}) for p in view_peers], view_sems
    )

    wait_in(edge_copies)
    has_low = jnp.where(slab > 0, 1.0, 0.0)
    has_high = jnp.where(slab < SLABS - 1, 1.0, 0.0)
    for c in (1, 0):
        parts_own[c, 0] += has_low * edges_low[c].astype(F32)
        parts_own[c, 3] += has_high * edges_high[c].astype(F32)
        (parts if c else parts_side)[member] = parts_own[c].astype(BF16)
    part_copies = start_copies(
        [(parts.at[member], parts.at[member], {"view": p}) for p in view_peers], part_sems
    )
    side_copies = start_copies(
        [(parts_side.at[member], parts_side.at[member], {"view": p}) for p in view_peers],
        side_sems,
    )
    pending += part_copies + side_copies

    t3_now = t3[:, :320].astype(BF16)
    out = split_pairs([mm(t3_now, pair_of(h2, 2 * p, 1)) for p in range(3)])
    for z in range(4):
        total = volume_ref[z]
        for e in range(3):
            part = jnp.zeros((8, 128), F32)
            for a in range(3):
                at = 8 * (3 * a + e)
                part = part + out[z + a][at : at + 8]
            total = total + shifted(part, e, lane8)
        new_ref[z] = total

    def sum_views():
        total = view_in[0].astype(F32)
        for n in range(1, VIEWS):
            total = total + view_in[n].astype(F32)
        return total.astype(BF16)

    wait_in(view_copies)
    layer_in[layer] = sum_views()
    layer_copies = start_copies(
        [(layer_in.at[layer], layer_in.at[layer], {"slab": p}) for p in layer_peers],
        layer_sems,
    )

    wait_in(part_copies)
    row8 = iota((8, 128), 0)
    rows = [None] * 16
    for z in range(4):
        planes = [parts[view, z].astype(F32) for view in range(VIEWS)]
        for view in range(VIEWS):
            value = planes[view][:8]
            if view > 0:
                value = value + jnp.where(row8 == 0, planes[view - 1][9:10], 0.0)
            if view < VIEWS - 1:
                value = value + jnp.where(row8 == 7, planes[view + 1][8:9], 0.0)
            rows[4 * view + z] = value
    field_rows = jnp.concatenate(rows, axis=0).astype(BF16)
    got = project(field_rows, choice, angles, response_ref, pick_x_ref, place_ref)
    wait_in(layer_copies)
    layer_total = layer_in[0].astype(F32)
    for n in range(1, LAYERS):
        layer_total = layer_total + layer_in[n].astype(F32)
    final_in[place] = layer_total.astype(BF16)
    final_copies = start_copies(
        [(final_in.at[place], final_in.at[place], {"slab": p}) for p in ring_peers],
        final_sems,
    )
    echo = (gain_rows * got).astype(BF16).astype(F32)
    spread = backproject(echo, chosen, angles, response_ref, pick_j_ref, spread_x_ref, 64)
    spread = spread[:, :256] + spread[:, 256:]
    wait_in(side_copies)
    has_left = jnp.where(member > 0, 1.0, 0.0)
    has_right = jnp.where(member < VIEWS - 1, 1.0, 0.0)
    for z in range(4):
        value = parts_own[0, z][:8] + upstream_ref[z].astype(F32)
        before = has_left * parts_side[left, z].astype(F32)[9:10]
        after = has_right * parts_side[right, z].astype(F32)[8:9]
        value = value + jnp.where(row8 == 0, before, 0.0) + jnp.where(row8 == 7, after, 0.0)
        for yt in range(2):
            grad_ref[z, 4 * yt : 4 * yt + 4, :] = (
                value[4 * yt : 4 * yt + 4, :]
                + spread[4 * z : 4 * z + 4, 128 * yt : 128 * yt + 128]
            )
    wait_out(pending)
    wait_in(final_copies)
    wait_out(view_copies + layer_copies + final_copies)


def emit_kernel(
    scale,
    new_ref,
    grad_ref,
    total_ref,
    new_out,
    grad_out,
    w1_out,
    bias1_out,
    w2_out,
    bias2_out,
    w3_out,
):
    new_out[...] = new_ref[...]
    grad_out[...] = grad_ref[...]
    whole = jnp.concatenate(
        [total_ref[n, SMALL:, :].astype(F32) for n in range(RING)], axis=0
    ) * scale
    small = total_ref[0, :SMALL, :].astype(F32)
    for n in range(1, RING):
        small = small + total_ref[n, :SMALL, :].astype(F32)
    turned = (small * scale).T
    bias1_out[...] = turned[54:55, :]
    for tap in range(9):
        block = whole[32 * tap : 32 * tap + 32]
        w2_out[tap] = block[:, :96]
        w1_out[tap] = turned[6 * tap : 6 * tap + 6, :]
        w3_out[tap] = whole[288 + tap : 289 + tap, :96]
    bias2_out[...] = whole[160:192].T[96:97, :]


def vmem_specs(count):
    return [pl.BlockSpec(memory_space=pltpu.VMEM)] * count


def body(volume, measured, dual_gain, pattern, angle, response, w1, bias1, w2, bias2, w3, upstream):
    pick_x, place, pick_j, spread_x = [jnp.asarray(x) for x in tile_constants()]
    band1, band3, rep3, fold1, fold3 = [jnp.asarray(x) for x in weight_constants()]
    dma = pltpu.SemaphoreType.DMA
    new_volume, grad_volume, total = pl.pallas_call(
        step_kernel,
        name="step",
        out_shape=(
            jax.ShapeDtypeStruct((4, 8, 128), F32),
            jax.ShapeDtypeStruct((4, 8, 128), F32),
            jax.ShapeDtypeStruct((RING, MESSAGE, 128), BF16),
        ),
        in_specs=[pl.BlockSpec(memory_space=HELD)] * 21,
        out_specs=tuple(vmem_specs(3)),
        scratch_shapes=[
            pltpu.VMEM((4, 8, 128), F32),
            pltpu.VMEM((4, 8, 128), BF16),
            pltpu.VMEM((32, 128), F32),
            pltpu.VMEM((32, 128), F32),
            pltpu.VMEM((VIEWS, 16, 64), jnp.int32),
            pltpu.VMEM((VIEWS, 64), jnp.int32),
            pltpu.VMEM((9, 6, 32), BF16),
            pltpu.VMEM((1, 32), F32),
            pltpu.VMEM((9, 32, 96), BF16),
            pltpu.VMEM((1, 32), F32),
            pltpu.VMEM((9, 96), BF16),
            pltpu.VMEM((128, 128), BF16),
            pltpu.VMEM((64, 128), BF16),
            pltpu.VMEM((2, 9, 6, 256), BF16),
            pltpu.VMEM((3, 9, 256), BF16),
            pltpu.VMEM((512, 1024), BF16),
            pltpu.VMEM((512, 1024), BF16),
            pltpu.VMEM((512, 512), BF16),
            pltpu.VMEM((3, 96, 384), BF16),
            pltpu.VMEM((384, 128), BF16),
            pltpu.VMEM((3, 384, 128), BF16),
            pltpu.VMEM((VIEWS, 4, 32, 128), BF16),
            pltpu.VMEM((VIEWS, 2, 32, 128), BF16),
            pltpu.VMEM((VIEWS, 2, 32, 128), BF16),
            pltpu.VMEM((4096, 256), BF16),
            pltpu.VMEM((256, 2048), BF16),
            pltpu.VMEM((3, 12, 16, 128), F32),
            pltpu.VMEM((12, 48, 128), BF16),
            pltpu.VMEM((12, 48, 128), BF16),
            pltpu.VMEM((12, 48, 128), BF16),
            pltpu.VMEM((8, 3, 8, 128), F32),
            pltpu.VMEM((384, 256), BF16),
            pltpu.VMEM((384, 256), BF16),
            pltpu.VMEM((320, 256), BF16),
            pltpu.VMEM((72, 384), F32),
            pltpu.VMEM((288, 256), BF16),
            pltpu.VMEM((96, 384), BF16),
            pltpu.VMEM((96, 384), BF16),
            pltpu.VMEM((8, 384, 128), F32),
            pltpu.VMEM((8, 12, 96, 128), BF16),
            pltpu.VMEM((6, 320, 128), F32),
            pltpu.VMEM((6, 320, 128), BF16),
            pltpu.VMEM((6, 10, 96, 128), BF16),
            pltpu.VMEM((8, 8, 32, 128), BF16),
            pltpu.VMEM((4, 256, 128), BF16),
            pltpu.VMEM((96, 384), F32),
            pltpu.VMEM((3, 16, 384), F32),
            pltpu.VMEM((2, 4, 16, 128), F32),
            pltpu.VMEM((VIEWS, 4, 16, 128), BF16),
            pltpu.VMEM((VIEWS, 4, 16, 128), BF16),
            pltpu.VMEM((2, 2, 16, 128), BF16),
            pltpu.VMEM((2, 16, 128), BF16),
            pltpu.VMEM((2, 16, 128), BF16),
            pltpu.VMEM((RING * PIECE, 128), F32),
            pltpu.VMEM((RING, PIECE, 128), BF16),
            pltpu.VMEM((RING, PIECE, 128), BF16),
            pltpu.VMEM((VIEWS, MESSAGE, 128), BF16),
            pltpu.VMEM((LAYERS, MESSAGE, 128), BF16),
            dma((21,)),
            dma((2, 3)),
            dma((2, 2)),
            dma((2, 2)),
            dma((2, 2)),
            dma((2, 3)),
            dma((2, 3)),
            dma((2, RING - 1)),
            dma((2, 3)),
            dma((2, 3)),
            dma((2, RING - 1)),
        ],
        compiler_params=pltpu.CompilerParams(
            collective_id=0, has_side_effects=True, vmem_limit_bytes=VMEM_BYTES
        ),
    )(
        volume,
        upstream,
        measured.reshape(32, 128),
        dual_gain.reshape(32, 128),
        pattern.transpose(0, 1, 3, 2).reshape(VIEWS, 16, 64),
        angle.reshape(VIEWS, 64),
        w1.transpose(0, 2, 1),
        bias1.reshape(1, 32),
        w2,
        bias2.reshape(1, 32),
        w3.reshape(9, 96),
        pick_x,
        pick_j,
        band1,
        band3,
        response,
        place,
        spread_x,
        rep3,
        fold1,
        fold3,
    )
    scale = 1.0 / math.sqrt(volume.size * SLABS * VIEWS)
    new_volume, grad_volume, grad_w1, grad_bias1, grad_w2, grad_bias2, grad_w3 = pl.pallas_call(
        functools.partial(emit_kernel, scale),
        name="emit",
        out_shape=(
            jax.ShapeDtypeStruct((4, 8, 128), F32),
            jax.ShapeDtypeStruct((4, 8, 128), F32),
            jax.ShapeDtypeStruct((9, 6, 32), F32),
            jax.ShapeDtypeStruct((1, 32), F32),
            jax.ShapeDtypeStruct((9, 32, 96), F32),
            jax.ShapeDtypeStruct((1, 32), F32),
            jax.ShapeDtypeStruct((9, 1, 96), F32),
        ),
        in_specs=vmem_specs(3),
        out_specs=tuple(vmem_specs(7)),
    )(new_volume, grad_volume, total)
    return (
        new_volume,
        grad_volume,
        grad_w1.transpose(0, 2, 1),
        grad_bias1.reshape(32),
        grad_w2,
        grad_bias2.reshape(32),
        grad_w3,
    )


def solution(mesh):
    placed = (
        P("slab", "view", None),
        P("view", "slab", None),
        P("view", "slab", None),
        P(None, "slab", None, None),
        P(None, "slab", None),
        P(),
        P(),
        P(),
        P(),
        P(),
        P(),
        P("slab", "view", None),
    )
    return jax.shard_map(
        body,
        mesh=mesh,
        in_specs=placed,
        out_specs=(P("slab", "view", None), P("slab", "view", None), P(), P(), P(), P(), P()),
        check_vma=False,
    )
```

```python
import functools
import math

import jax
import jax.numpy as jnp
import ml_dtypes
import numpy as np
from jax import lax
from jax.experimental import pallas as pl
from jax.experimental.pallas import tpu as pltpu
from jax.sharding import PartitionSpec as P

F32 = jnp.float32
BF16 = jnp.bfloat16
MESH = pl.DeviceIdType.MESH
VIEWS = 4
RING = 8
LAYERS = 4
SLABS = RING * LAYERS
PIECE = 40
SMALL = 16
MESSAGE = SMALL + PIECE
VMEM_BYTES = 56 * 1024 * 1024
HELD = pl.ANY


def mm(a, b):
    return lax.dot_general(a, b, (((1,), (0,)), ((), ())), preferred_element_type=F32)


def mmt(a, b):
    return lax.dot_general(a, b, (((1,), (1,)), ((), ())), preferred_element_type=F32)


def iota(shape, dim):
    return lax.broadcasted_iota(jnp.int32, shape, dim)


def one(cond):
    return jnp.where(cond, 1.0, 0.0).astype(BF16)


def host_bf16(cond):
    return np.asarray(cond, np.float32).astype(ml_dtypes.bfloat16)


def tile_constants():
    row, col = np.arange(128)[:, None], np.arange(128)[None, :]
    pick_x = host_bf16(col == 4 * (row % 32) + row // 32)
    r, c = np.arange(512)[:, None], np.arange(1024)[None, :]
    xi, quarter, z, y8 = r // 128, r // 32 % 4, r // 8 % 4, r % 8
    yt, j = c // 128, c % 64
    place = host_bf16(
        (2 * quarter + y8 // 4 == yt) & (z == j // 16) & (y8 % 4 == j // 4 % 4) & (xi == j % 4)
    )
    r, c = np.arange(64)[:, None], np.arange(128)[None, :]
    pick_j = host_bf16((c < 64) & (c % 4 == r // 16) & (c // 4 == r % 16))
    r, c = np.arange(512)[:, None], np.arange(512)[None, :]
    spread_x = host_bf16((r // 32 % 4 == c // 128) & (c % 128 == 4 * (r % 32) + r // 128))
    return pick_x, place, pick_j, spread_x


def weight_constants():
    lane = np.arange(384)
    band1 = np.zeros((2, 9, 6, 256), np.float32)
    fold1 = np.zeros((384, 128), np.float32)
    for a in range(3):
        for b in range(3):
            for e in range(3):
                for c in range(2):
                    band1[c, 3 * a + b, 2 * e + c, (a * 3 + e) * 16 + b] = 1.0
                    fold1[
                        ((c * 3 + a) * 3 + e) * 16 + 3 + b, 6 * (3 * a + b) + 2 * e + c
                    ] = 1.0
    fold1[288, 54] = 1.0
    band3 = np.zeros((3, 9, 256), np.float32)
    for a in range(3):
        for b in range(3):
            for e in range(3):
                band3[e, 3 * (2 - a) + (2 - b), (a * 3 + e) * 16 + b] = 1.0
    rep3 = np.zeros((3, 96, 384), np.float32)
    for e in range(3):
        rep3[e, 32 * e + lane % 32, lane] = 1.0
    fold3 = np.zeros((3, 384, 128), np.float32)
    for e in range(3):
        live = lane[lane < 320]
        fold3[e, live, 32 * e + live % 32] = 1.0
    return tuple(host_bf16(x) for x in (band1, band3, rep3, fold1, fold3))


def own_order():
    return one(iota((64, 64), 1) == 2 * (iota((64, 64), 0) % 32) + iota((64, 64), 0) // 32)


def choose_tiles(pattern_ref, angle_ref, choice, chosen, first):
    order = own_order()
    lanes = iota((64, 256), 1)
    lines = []
    for g in range(VIEWS):
        held = pattern_ref[g].astype(F32).astype(BF16)
        ids = mmt(order, held).astype(jnp.int32)
        for k in range(16):
            at = 256 * (k // 2) + 64 * g
            side = 256 * (k % 2)
            choice[at : at + 64, side : side + 256] = one(lanes == ids[:, k : k + 1])
        lines.append(mmt(held, order))
    line = jnp.concatenate(lines, axis=1).astype(jnp.int32)
    tile = iota((128, 256), 0) + first
    for k in range(16):
        at = 128 * (k % 2)
        chosen[at : at + 128, 256 * (k // 2) : 256 * (k // 2) + 256] = one(
            tile == line[k : k + 1, :]
        )
    angles = mmt(order, angle_ref[...].astype(F32).astype(BF16)).astype(jnp.int32)
    return jnp.concatenate([angles[:, g : g + 1] for g in range(VIEWS)], axis=0)


def project(field_rows, choice, angles, response_turned, pick_x_ref, place_ref):
    by_x = mmt(pick_x_ref[...], field_rows).astype(BF16)
    wide = jnp.concatenate([by_x[32 * i : 32 * i + 32] for i in range(4)], axis=1)
    spread = mm(wide, place_ref[...]).astype(BF16)
    tiles = jnp.concatenate([spread[:, 128 * i : 128 * i + 128] for i in range(8)], axis=0)
    zero = jnp.zeros((256, 128), F32)
    wide_tiles = tiles.astype(F32)
    low = iota((256, 128), 1) < 64
    both = jnp.concatenate(
        [jnp.where(low, wide_tiles, zero), jnp.where(low, zero, wide_tiles)], axis=0
    ).astype(BF16)
    pairs = [mm(choice[256 * p : 256 * p + 256, :], both).astype(BF16) for p in range(8)]
    lines = mm(jnp.concatenate(pairs, axis=1), response_turned[...])
    half = iota((256, 128), 1) // 64
    total = jnp.zeros((256, 128), F32)
    for p in range(4):
        total = total + jnp.where(angles == 2 * p + half, lines[:, 128 * p : 128 * p + 128], 0.0)
    return total + pltpu.roll(total, 64, 1)


def doubled_rows(ref, part):
    low = iota((32, 128), 1) < 64
    parts = []
    for g in range(VIEWS):
        rows = ref[g, part].astype(F32)
        turned = pltpu.roll(rows, 64, 1)
        parts.append(jnp.where(low, rows, turned))
        parts.append(jnp.where(low, turned, rows))
    return jnp.concatenate(parts, axis=0)


def backproject(doubled, chosen, angles, response_ref, pick_j_ref, spread_x_ref, count):
    half = iota((256, 128), 1) // 64
    masked = [
        jnp.where(angles == 2 * p + half, doubled, 0.0).astype(BF16) for p in range(4)
    ]
    contrib = mm(jnp.concatenate(masked, axis=1), response_ref[...])
    high = contrib.astype(BF16)
    blocks = [high[:, 128 * p : 128 * p + 128] for p in range(8)]
    if count == 64:
        rest = (contrib - high.astype(F32)).astype(BF16)
        blocks = [
            jnp.concatenate([block, rest[:, 128 * p : 128 * p + 128]], axis=1)
            for p, block in enumerate(blocks)
        ]
    stacked = jnp.concatenate(blocks, axis=0)
    skip = (128 - count) // 2
    left = jnp.concatenate(
        [chosen[skip : skip + count, :], chosen[128 + skip : 128 + skip + count, :]], axis=0
    )
    sums = mm(left, stacked)
    if count == 64:
        sums = sums[:, :128] + sums[:, 128:]
    tiles = sums[:count] + pltpu.roll(sums[count:], 64, 1)
    top = tiles.astype(BF16)
    if count == 64:
        top = jnp.concatenate([top, (tiles - top.astype(F32)).astype(BF16)], axis=0)
    by_j = mmt(pick_j_ref[...], top).astype(BF16)
    wide = jnp.concatenate([by_j[16 * i : 16 * i + 16] for i in range(4)], axis=1)
    return mm(wide, spread_x_ref[...])


def start_copies(pairs, sems):
    copies = []
    for n, (source, target, device) in enumerate(pairs):
        copies.append(
            pltpu.make_async_remote_copy(
                src_ref=source,
                dst_ref=target,
                send_sem=sems.at[0, n],
                recv_sem=sems.at[1, n],
                device_id=device,
                device_id_type=MESH,
            )
        )
    for copy in copies:
        copy.start()
    return copies


def wait_in(copies):
    for copy in copies:
        copy.wait_recv()


def wait_out(copies):
    for copy in copies:
        copy.wait_send()


def shifted(value, e, lane):
    if e == 1:
        return value
    if e == 0:
        return jnp.where(lane == 0, 0.0, pltpu.roll(value, 1, 1))
    return jnp.where(lane == 127, 0.0, pltpu.roll(value, 127, 1))


def prepare_weights(
    w1_ref, w2_ref, w3_ref, band1_ref, band3_ref, rep3_ref, t1v, t1b, t3t, t3, t1t, w2r, w2t
):
    eye32 = one(iota((32, 32), 0) == iota((32, 32), 1))
    for c, ref in ((0, t1v), (1, t1b)):
        base = jnp.zeros((32, 256), F32)
        for tap in range(9):
            turned = mmt(eye32, w1_ref[tap]).astype(BF16)
            base = base + mm(turned, band1_ref[c, tap])
        for yo in range(12):
            ref[32 * yo : 32 * yo + 32, :] = pltpu.roll(base, yo + 1, 1).astype(BF16)
    eye96 = one(iota((96, 96), 0) == iota((96, 96), 1))
    w3 = w3_ref[...]
    w3_turned = mmt(eye96, w3).astype(BF16)
    base = jnp.zeros((32, 256), F32)
    for e in range(3):
        base = base + mm(w3_turned[32 * (2 - e) : 32 * (2 - e) + 32], band3_ref[e])
    for yo in range(10):
        t3t[32 * yo : 32 * yo + 32, :] = pltpu.roll(base, yo + 2, 1).astype(BF16)
    step = iota((8, 384), 1) // 32 - iota((8, 384), 0)
    for e in range(3):
        line = mm(w3, rep3_ref[e])
        for a in range(3):
            block = jnp.zeros((8, 384), F32)
            for b in range(3):
                block = block + jnp.where(step == b, line[3 * a + b : 3 * a + b + 1, :], 0.0)
            t3[8 * (3 * a + e) : 8 * (3 * a + e) + 8, :] = block
    rep = one(iota((32, 256), 0) == iota((32, 256), 1) % 32)
    turned = [mm(w1_ref[tap], rep) for tap in range(9)]
    row16 = iota((16, 256), 0)
    row_y = jnp.where(row16 < 8, row16, jnp.where(row16 == 8, -1, 8))
    step = iota((16, 256), 1) // 32 - row_y + 1
    step = jnp.where(row16 < 10, step, -1)
    for a in range(3):
        for c in range(2):
            for e in range(3):
                row = 2 * (2 - e) + c
                block = jnp.zeros((16, 256), F32)
                for b in range(3):
                    tap = 3 * (2 - a) + (2 - b)
                    block = block + jnp.where(step == b, turned[tap][row : row + 1, :], 0.0)
                at = 16 * ((a * 2 + c) * 3 + e)
                t1t[at : at + 16, :] = block.astype(BF16)
    places = [one(iota((96, 384), 1) == iota((96, 384), 0) + 96 * b) for b in range(3)]
    keep = iota((96, 96), 1) // 32 == 2 - iota((96, 96), 0) // 32
    same = one(iota((32, 96), 0) == iota((32, 96), 1) % 32)
    for a in range(3):
        plain = jnp.zeros((32, 384), F32)
        across = jnp.zeros((32, 384), F32)
        for b in range(3):
            plain = plain + mm(w2_ref[3 * a + b], places[b])
            tower = jnp.concatenate([w2_ref[3 * (2 - a) + (2 - b)].astype(F32)] * 3, axis=0)
            tower = jnp.where(keep, tower, 0.0).astype(BF16)
            across = across + mm(mmt(same, tower).astype(BF16), places[b])
        w2r[32 * a : 32 * a + 32, :] = plain.astype(BF16)
        w2t[32 * a : 32 * a + 32, :] = across.astype(BF16)


def pair_of(ref, z, count):
    cols = [jnp.concatenate([ref[z + n + a] for a in range(count)], axis=0) for n in range(2)]
    return jnp.concatenate(cols, axis=1)


def stacked_rows(ref, z, y):
    cols = [ref[z + n, pl.ds(y, 3)].reshape(288, 128) for n in range(2)]
    return jnp.concatenate(cols, axis=1)


def split_pairs(outs):
    return [out[:, 128 * n : 128 * n + 128] for out in outs for n in range(2)]


def step_kernel(
    volume_hbm,
    upstream_hbm,
    measured_hbm,
    gain_hbm,
    pattern_hbm,
    angle_hbm,
    w1_hbm,
    bias1_hbm,
    w2_hbm,
    bias2_hbm,
    w3_hbm,
    pick_x_hbm,
    pick_j_hbm,
    band1_hbm,
    band3_hbm,
    response_hbm,
    place_hbm,
    spread_x_hbm,
    rep3_hbm,
    fold1_hbm,
    fold3_hbm,
    new_ref,
    grad_ref,
    final_in,
    volume_ref,
    upstream_ref,
    measured_ref,
    gain_ref,
    pattern_ref,
    angle_ref,
    w1_ref,
    bias1_ref,
    w2_ref,
    bias2_ref,
    w3_ref,
    pick_x_ref,
    pick_j_ref,
    band1_ref,
    band3_ref,
    response_ref,
    place_ref,
    spread_x_ref,
    rep3_ref,
    fold1_ref,
    fold3_ref,
    pack,
    pack_low,
    pack_high,
    choice,
    chosen,
    fields,
    ins,
    backs,
    ups,
    ups_own,
    t1v,
    t1b,
    t3t,
    t3,
    t1t,
    w2r,
    w2t,
    pre1,
    h3,
    ct3,
    h2,
    s3,
    s2z,
    s1,
    g2,
    g3,
    parts_own,
    parts,
    edge_rows,
    response_turned,
    edges,
    edges_low,
    edges_high,
    totals,
    sums,
    ring_in,
    view_in,
    layer_in,
    local_sems,
    pack_sems,
    plane_sems,
    back_sems,
    edge_sems,
    part_sems,
    ring_sems,
    view_sems,
    layer_sems,
    final_sems,
):
    slab, member = lax.axis_index("slab"), lax.axis_index("view")
    above, below = lax.rem(slab + 1, SLABS), lax.rem(slab + SLABS - 1, SLABS)
    left, right = lax.rem(member + VIEWS - 1, VIEWS), lax.rem(member + 1, VIEWS)
    place, layer = lax.rem(slab, RING), lax.div(slab, RING)
    view_peers = [
        VIEWS - 1 - member,
        lax.rem(member + 2, VIEWS),
        member + 1 - 2 * lax.rem(member, 2),
    ]
    ring_peers = [layer * RING + lax.rem(place + off, RING) for off in range(1, RING)]
    layer_peers = [
        lax.rem(layer + off, LAYERS) * RING + place for off in range(1, LAYERS)
    ]
    depth, height = 4 * SLABS, 8 * VIEWS

    barrier = pltpu.get_barrier_semaphore()
    peers = [{"view": peer} for peer in view_peers]
    peers += [{"slab": peer} for peer in ring_peers + layer_peers + [above, below]]
    for peer in peers:
        pl.semaphore_signal(barrier, inc=1, device_id=peer, device_id_type=MESH)

    loads = {}
    for n, (name, source, target) in enumerate(
        (
            ("volume", volume_hbm, volume_ref),
            ("upstream", upstream_hbm, upstream_ref),
            ("measured", measured_hbm, measured_ref),
            ("gain", gain_hbm, gain_ref),
            ("pattern", pattern_hbm, pattern_ref),
            ("angle", angle_hbm, angle_ref),
            ("w1", w1_hbm, w1_ref),
            ("w2", w2_hbm, w2_ref),
            ("w3", w3_hbm, w3_ref),
            ("band1", band1_hbm, band1_ref),
            ("band3", band3_hbm, band3_ref),
            ("rep3", rep3_hbm, rep3_ref),
            ("pick_x", pick_x_hbm, pick_x_ref),
            ("place", place_hbm, place_ref),
            ("response", response_hbm, response_ref),
            ("pick_j", pick_j_hbm, pick_j_ref),
            ("spread_x", spread_x_hbm, spread_x_ref),
            ("bias1", bias1_hbm, bias1_ref),
            ("bias2", bias2_hbm, bias2_ref),
            ("fold3", fold3_hbm, fold3_ref),
            ("fold1", fold1_hbm, fold1_ref),
        )
    ):
        loads[name] = pltpu.make_async_copy(source, target, local_sems.at[n])
        loads[name].start()

    def loaded(*which):
        for name in which:
            loads[name].wait()

    loaded("volume", "upstream", "measured", "gain")
    pack[member, 0] = volume_ref[...].reshape(32, 128).astype(BF16)
    pack[member, 1] = upstream_ref[...].astype(F32).reshape(32, 128).astype(BF16)
    pack[member, 2] = measured_ref[...].astype(BF16)
    pack[member, 3] = gain_ref[...].astype(BF16)
    pl.semaphore_wait(barrier, len(peers))

    pending = []
    pack_copies = start_copies(
        [(pack.at[member], pack.at[member], {"view": p}) for p in view_peers], pack_sems
    )
    pending += pack_copies
    loaded("pattern", "angle")
    angles = choose_tiles(pattern_ref, angle_ref, choice, chosen, 64 * member - 32)
    loaded("w1", "w2", "w3", "band1", "band3", "rep3")
    prepare_weights(
        w1_ref, w2_ref, w3_ref, band1_ref, band3_ref, rep3_ref, t1v, t1b, t3t, t3, t1t, w2r, w2t
    )
    loaded("pick_x", "place", "response", "pick_j", "spread_x", "bias1", "bias2")
    response_turned[...] = response_ref[...].T
    wait_in(pack_copies)
    plane_copies = start_copies(
        [
            (pack.at[:, pl.ds(0, 2)], pack_low, {"slab": above}),
            (pack.at[:, pl.ds(0, 2)], pack_high, {"slab": below}),
        ],
        plane_sems,
    )
    pending += plane_copies

    field_rows = pack[:, 0].reshape(128, 128)
    got = project(field_rows, choice, angles, response_turned, pick_x_ref, place_ref)
    gain_rows = doubled_rows(pack, 3)
    dual = (gain_rows * (got - doubled_rows(pack, 2))).astype(BF16).astype(F32)
    spread = backproject(dual, chosen, angles, response_ref, pick_j_ref, spread_x_ref, 128)
    for z in range(4):
        for yt in range(4):
            fields[2, 4 + z, 4 * yt : 4 * yt + 4, :] = spread[
                4 * z : 4 * z + 4, 128 * yt : 128 * yt + 128
            ]
    back_copies = start_copies(
        [
            (fields.at[2, pl.ds(5, 3)], fields.at[2, pl.ds(1, 3)], {"slab": above}),
            (fields.at[2, pl.ds(4, 3)], fields.at[2, pl.ds(8, 3)], {"slab": below}),
        ],
        back_sems,
    )
    pending += back_copies

    wait_in(plane_copies)
    low_z, low_y = 4 * slab - 4, 8 * member - 4
    lane16 = iota((16, 128), 1)
    global_y = iota((16, 128), 0) + low_y
    inside_y = (global_y >= 0) & (global_y < height)
    lane8 = iota((8, 128), 1)
    for field in range(2):
        for source, first, low in ((pack_low, 1, 0), (pack, 4, 4), (pack_high, 8, 8)):
            own, before, after = (
                source[view, field].astype(F32) for view in (member, left, right)
            )
            for z in range(first, min(low + 4, 11)):
                at = 8 * (z - low)
                fields[field, z, 4:12, :] = own[at : at + 8]
                fields[field, z, 0:4, :] = before[at + 4 : at + 8]
                fields[field, z, 12:16, :] = after[at : at + 4]

    def shifts_of(field, target):
        def one_plane(z, carry):
            inside = inside_y & (z + low_z >= 0) & (z + low_z < depth)
            plane = jnp.where(inside, fields[field, z], 0.0)
            plane = plane.astype(BF16).astype(F32)
            for e in range(3):
                target[z, 16 * e : 16 * e + 16, :] = shifted(plane, e, lane16).astype(BF16)
            return carry

        lax.fori_loop(1, 11, one_plane, 0, unroll=10)

    shifts_of(0, ins)
    shifts_of(1, ups)
    ups_own[...] = jnp.zeros(ups_own.shape, F32)
    for z in range(4):
        plane = upstream_ref[z].astype(F32)
        for e in range(3):
            ups_own[2 + z, e] = shifted(plane, 2 - e, lane8)

    def third_turned(p, carry):
        z = 2 * p
        out = mm(t3t[:, :144], pair_of(ups, z + 2, 3))
        ct3[z] = out[:, :128]
        ct3[z + 1] = out[:, 128:]
        return carry

    lax.fori_loop(0, 3, third_turned, 0, unroll=3)
    eye32 = iota((32, 32), 0) == iota((32, 32), 1)
    bias1 = jnp.sum(jnp.where(eye32, bias1_ref[...], 0.0), axis=1, keepdims=True)
    bias2 = jnp.sum(jnp.where(eye32, bias2_ref[...], 0.0), axis=1, keepdims=True)
    bias1_rows = jnp.concatenate([jnp.broadcast_to(bias1, (32, 128))] * 12, axis=0)

    def first_volume(p, carry):
        z = 2 * p
        out = mm(t1v[:, :144], pair_of(ins, z + 1, 3))
        pre1[z] = out[:, :128] + bias1_rows
        pre1[z + 1] = out[:, 128:] + bias1_rows
        return carry

    lax.fori_loop(0, 4, first_volume, 0, unroll=4)
    s2z[...] = jnp.zeros(s2z.shape, BF16)
    g2[...] = jnp.zeros(g2.shape, F32)
    g3[...] = jnp.zeros(g3.shape, F32)

    wait_in(back_copies)
    shifts_of(2, backs)

    def first_back(p, carry):
        z = 2 * p
        out = mm(t1b[:, :144], pair_of(backs, z + 1, 3))
        pre1[z] += out[:, :128]
        pre1[z + 1] += out[:, 128:]
        return carry

    lax.fori_loop(0, 4, first_back, 0, unroll=4)

    lane384 = iota((384, 128), 1)
    row_y1 = iota((384, 128), 0) // 32 + low_y + 2
    inside1 = (row_y1 >= 0) & (row_y1 < height)

    def activate(z, keep_slope):
        value = pre1[z]
        gate = 0.5 * jnp.tanh(0.5 * value) + 0.5
        act = value * gate
        if keep_slope:
            pre1[z] = gate + act * (1.0 - gate)
        inside = inside1 & (z + low_z + 2 >= 0) & (z + low_z + 2 < depth)
        act = jnp.where(inside, act, 0.0)
        for e in range(3):
            h3[z, :, 32 * e : 32 * e + 32, :] = (
                shifted(act, e, lane384).astype(BF16).reshape(12, 32, 128)
            )

    def activate_outer(n, carry):
        activate(n + 4 * (n // 2), False)
        return carry

    def activate_inner(n, carry):
        activate(n + 2, True)
        return carry

    lax.fori_loop(0, 4, activate_outer, 0, unroll=4)
    lax.fori_loop(0, 4, activate_inner, 0, unroll=4)

    lane32 = iota((32, 128), 1)

    def second(y, carry):
        out = split_pairs([mm(w2r[:, :288], stacked_rows(h3, 2 * p, y)) for p in range(4)])
        ok_y = (y + low_y + 3 >= 0) & (y + low_y + 3 < height)
        at = pl.multiple_of(32 * y, 32)
        for z in range(6):
            value = out[z][:32] + out[z + 1][32:64] + out[z + 2][64:] + bias2
            gate = 0.5 * jnp.tanh(0.5 * value) + 0.5
            act = value * gate
            slope = gate + act * (1.0 - gate)
            ok = ok_y & (z + low_z + 3 >= 0) & (z + low_z + 3 < depth)
            live = jnp.where(ok, 1.0, 0.0)
            h2[z, pl.ds(at, 32), :] = (act * live).astype(BF16)
            slope = slope * ct3[z, pl.ds(at, 32), :] * live
            for e in range(3):
                s3[z, y, 32 * e : 32 * e + 32, :] = shifted(slope, e, lane32).astype(BF16)
        return carry

    lax.fori_loop(0, 10, second, 0, unroll=10)

    for z in range(4):
        s2z[z + 2] = s3[z + 1, 1:9, 32:64, :]
    ones = jnp.ones((16, 768), BF16)

    def second_grad(y, carry):
        turned = jnp.concatenate(
            [
                jnp.concatenate([s2z[z + 1 - a, y] for z in range(1, 7)], axis=1)
                for a in range(3)
            ],
            axis=0,
        )
        plain = jnp.concatenate(
            [h3[z, pl.ds(y + 1, 3)].reshape(288, 128) for z in range(1, 7)], axis=1
        )
        g2[:, :304] += mmt(turned, jnp.concatenate([plain, ones], axis=0))
        return carry

    lax.fori_loop(0, 8, second_grad, 0, unroll=8)

    turned = jnp.concatenate(
        [
            jnp.concatenate(
                [ups_own[z + 2 - a, e] for a in range(3) for e in range(3)], axis=0
            ).astype(BF16)
            for z in range(6)
        ],
        axis=1,
    )
    plain = jnp.concatenate([h2[z] for z in range(6)], axis=1)
    cross = mmt(turned, plain)
    step10 = iota((8, 320), 1) // 32 - iota((8, 320), 0)
    for a in range(3):
        for e in range(3):
            block = cross[8 * (3 * a + e) : 8 * (3 * a + e) + 8]
            for b in range(3):
                g3[e, 3 * a + b : 3 * a + b + 1, 0:320] = jnp.sum(
                    jnp.where(step10 == b, block, 0.0), axis=0, keepdims=True
                )
    loaded("fold1", "fold3")
    third = jnp.zeros((16, 128), F32)
    for e in range(3):
        value = g3[e]
        high = value.astype(BF16)
        rest = (value - high.astype(F32)).astype(BF16)
        third = third + mm(high, fold3_ref[e]) + mm(rest, fold3_ref[e])

    lanes = iota((32, 128), 1)
    for tap in range(9):
        a, b = tap // 3, tap % 3
        block = g2[32 * a : 32 * a + 32, :]
        if b:
            block = pltpu.roll(block, 384 - 96 * b, 1)
        totals[32 * tap : 32 * tap + 32, :] = jnp.where(
            lanes < (97 if b == 2 else 96), block[:, :128], 0.0
        )
    totals[288:304, :] = third
    totals[304:320, :] = jnp.zeros((16, 128), F32)
    for n in range(RING):
        sums[n] = totals[PIECE * n : PIECE * n + PIECE, :].astype(BF16)
    ring_in[place] = sums[place]
    ring_copies = start_copies(
        [(sums.at[lax.rem(peer, RING)], ring_in.at[place], {"slab": peer}) for peer in ring_peers],
        ring_sems,
    )
    pending += ring_copies

    def second_turned(y, carry):
        out = split_pairs([mm(w2t[:, :288], stacked_rows(s3, 2 * p, y)) for p in range(3)])
        at = pl.multiple_of(32 * y, 32)
        from_ = pl.multiple_of(32 * y + 64, 32)
        for z in range(4):
            value = out[z][:32] + out[z + 1][32:64] + out[z + 2][64:]
            s1[z, pl.ds(at, 32), :] = (value * pre1[z + 2, pl.ds(from_, 32), :]).astype(BF16)
        return carry

    lax.fori_loop(0, 8, second_turned, 0, unroll=8)

    out = split_pairs([mm(t1t[...], pair_of(s1, 2 * p, 1)) for p in range(2)])
    for c in range(2):
        for z in range(-1, 5):
            total = jnp.zeros((16, 128), F32)
            for e in range(3):
                part = jnp.zeros((16, 128), F32)
                for a in range(3):
                    if 0 <= z + a - 1 < 4:
                        at = 16 * ((a * 2 + c) * 3 + e)
                        part = part + out[z + a - 1][at : at + 16]
                total = total + shifted(part, e, lane16)
            if z == -1:
                edges[0, c] = total.astype(BF16)
            elif z == 4:
                edges[1, c] = total.astype(BF16)
            else:
                parts_own[c, z] = total
    edge_copies = start_copies(
        [
            (edges.at[1], edges_low, {"slab": above}),
            (edges.at[0], edges_high, {"slab": below}),
        ],
        edge_sems,
    )
    pending += edge_copies

    turned = jnp.concatenate([s1[z] for z in range(4)], axis=1)
    plain = jnp.concatenate(
        [
            jnp.concatenate(
                [ins[z + 3 + a] for a in range(3)]
                + [backs[z + 3 + a] for a in range(3)]
                + [jnp.ones((96, 128), BF16)],
                axis=0,
            )
            for z in range(4)
        ],
        axis=1,
    )
    cross = mmt(turned, plain)
    total = cross[:32]
    for yo in range(1, 8):
        total = total + pltpu.roll(cross[32 * yo : 32 * yo + 32], 384 - yo, 1)
    high = total.astype(BF16)
    rest = (total - high.astype(F32)).astype(BF16)
    first_grads = mm(high, fold1_ref[...]) + mm(rest, fold1_ref[...])
    view_in[member, 0:SMALL, :] = jnp.where(
        iota((16, 128), 1) < 64, first_grads[:16], pltpu.roll(first_grads[16:], 64, 1)
    ).astype(BF16)

    wait_in(ring_copies)
    ring_total = ring_in[0].astype(F32)
    for n in range(1, RING):
        ring_total = ring_total + ring_in[n].astype(F32)
    view_in[member, SMALL:, :] = ring_total.astype(BF16)
    view_copies = start_copies(
        [(view_in.at[member], view_in.at[member], {"view": p}) for p in view_peers], view_sems
    )

    wait_in(edge_copies)
    has_low = jnp.where(slab > 0, 1.0, 0.0)
    has_high = jnp.where(slab < SLABS - 1, 1.0, 0.0)
    for c in (1, 0):
        parts_own[c, 0] += has_low * edges_low[c].astype(F32)
        parts_own[c, 3] += has_high * edges_high[c].astype(F32)
        for z in range(4):
            at = 8 * (1 - c) + 2 * z
            edge_rows[at : at + 2, :] = parts_own[c, z, 8:10, :]
    parts[member, 0:32, :] = jnp.concatenate(
        [parts_own[1, z, 0:8, :] for z in range(4)], axis=0
    ).astype(BF16)
    parts[member, 32:48, :] = edge_rows[...].astype(BF16)
    part_copies = start_copies(
        [(parts.at[member], parts.at[member], {"view": p}) for p in view_peers], part_sems
    )
    pending += part_copies

    t3_now = t3[:, :320].astype(BF16)
    out = split_pairs([mm(t3_now, pair_of(h2, 2 * p, 1)) for p in range(3)])
    for z in range(4):
        total = volume_ref[z]
        for e in range(3):
            part = jnp.zeros((8, 128), F32)
            for a in range(3):
                at = 8 * (3 * a + e)
                part = part + out[z + a][at : at + 8]
            total = total + shifted(part, e, lane8)
        new_ref[z] = total

    def sum_views():
        total = view_in[0].astype(F32)
        for n in range(1, VIEWS):
            total = total + view_in[n].astype(F32)
        return total.astype(BF16)

    wait_in(view_copies)
    layer_in[layer] = sum_views()
    layer_copies = start_copies(
        [(layer_in.at[layer], layer_in.at[layer], {"slab": p}) for p in layer_peers],
        layer_sems,
    )

    wait_in(part_copies)
    row8 = iota((8, 128), 0)
    rows = [None] * 16
    planes = [parts[view].astype(F32) for view in range(VIEWS)]
    for z in range(4):
        for view in range(VIEWS):
            value = planes[view][8 * z : 8 * z + 8]
            if view > 0:
                edge = planes[view - 1][33 + 2 * z : 34 + 2 * z]
                value = value + jnp.where(row8 == 0, edge, 0.0)
            if view < VIEWS - 1:
                edge = planes[view + 1][32 + 2 * z : 33 + 2 * z]
                value = value + jnp.where(row8 == 7, edge, 0.0)
            rows[4 * view + z] = value
    field_rows = jnp.concatenate(rows, axis=0).astype(BF16)
    got = project(field_rows, choice, angles, response_turned, pick_x_ref, place_ref)
    wait_in(layer_copies)
    layer_total = layer_in[0].astype(F32)
    for n in range(1, LAYERS):
        layer_total = layer_total + layer_in[n].astype(F32)
    final_in[place] = layer_total.astype(BF16)
    final_copies = start_copies(
        [(final_in.at[place], final_in.at[place], {"slab": p}) for p in ring_peers],
        final_sems,
    )
    echo = (gain_rows * got).astype(BF16).astype(F32)
    spread = backproject(echo, chosen, angles, response_ref, pick_j_ref, spread_x_ref, 64)
    spread = spread[:, :256] + spread[:, 256:]
    has_left = jnp.where(member > 0, 1.0, 0.0)
    has_right = jnp.where(member < VIEWS - 1, 1.0, 0.0)
    before = has_left * parts[left, 32:48, :].astype(F32)
    after = has_right * parts[right, 32:48, :].astype(F32)
    for z in range(4):
        value = parts_own[0, z][:8] + upstream_ref[z].astype(F32)
        value = value + jnp.where(row8 == 0, before[9 + 2 * z : 10 + 2 * z], 0.0)
        value = value + jnp.where(row8 == 7, after[8 + 2 * z : 9 + 2 * z], 0.0)
        for yt in range(2):
            grad_ref[z, 4 * yt : 4 * yt + 4, :] = (
                value[4 * yt : 4 * yt + 4, :]
                + spread[4 * z : 4 * z + 4, 128 * yt : 128 * yt + 128]
            )
    wait_out(pending)
    wait_in(final_copies)
    wait_out(view_copies + layer_copies + final_copies)


def emit_kernel(
    scale,
    new_ref,
    grad_ref,
    total_ref,
    new_out,
    grad_out,
    w1_out,
    bias1_out,
    w2_out,
    bias2_out,
    w3_out,
):
    new_out[...] = new_ref[...]
    grad_out[...] = grad_ref[...]
    whole = jnp.concatenate(
        [total_ref[n, SMALL:, :].astype(F32) for n in range(RING)], axis=0
    ) * scale
    small = total_ref[0, :SMALL, :].astype(F32)
    for n in range(1, RING):
        small = small + total_ref[n, :SMALL, :].astype(F32)
    small = jnp.concatenate([small, pltpu.roll(small, 64, 1)], axis=0)
    turned = (small * scale).T
    bias1_out[...] = turned[54:55, :]
    for tap in range(9):
        block = whole[32 * tap : 32 * tap + 32]
        w2_out[tap] = block[:, :96]
        w1_out[tap] = turned[6 * tap : 6 * tap + 6, :]
        w3_out[tap] = whole[288 + tap : 289 + tap, :96]
    bias2_out[...] = whole[160:192].T[96:97, :]


def vmem_specs(count):
    return [pl.BlockSpec(memory_space=pltpu.VMEM)] * count


def body(volume, measured, dual_gain, pattern, angle, response, w1, bias1, w2, bias2, w3, upstream):
    pick_x, place, pick_j, spread_x = [jnp.asarray(x) for x in tile_constants()]
    band1, band3, rep3, fold1, fold3 = [jnp.asarray(x) for x in weight_constants()]
    dma = pltpu.SemaphoreType.DMA
    new_volume, grad_volume, total = pl.pallas_call(
        step_kernel,
        name="step",
        out_shape=(
            jax.ShapeDtypeStruct((4, 8, 128), F32),
            jax.ShapeDtypeStruct((4, 8, 128), F32),
            jax.ShapeDtypeStruct((RING, MESSAGE, 128), BF16),
        ),
        in_specs=[pl.BlockSpec(memory_space=HELD)] * 21,
        out_specs=tuple(vmem_specs(3)),
        scratch_shapes=[
            pltpu.VMEM((4, 8, 128), F32),
            pltpu.VMEM((4, 8, 128), BF16),
            pltpu.VMEM((32, 128), F32),
            pltpu.VMEM((32, 128), F32),
            pltpu.VMEM((VIEWS, 16, 64), jnp.int32),
            pltpu.VMEM((VIEWS, 64), jnp.int32),
            pltpu.VMEM((9, 6, 32), BF16),
            pltpu.VMEM((1, 32), F32),
            pltpu.VMEM((9, 32, 96), BF16),
            pltpu.VMEM((1, 32), F32),
            pltpu.VMEM((9, 96), BF16),
            pltpu.VMEM((128, 128), BF16),
            pltpu.VMEM((64, 128), BF16),
            pltpu.VMEM((2, 9, 6, 256), BF16),
            pltpu.VMEM((3, 9, 256), BF16),
            pltpu.VMEM((512, 1024), BF16),
            pltpu.VMEM((512, 1024), BF16),
            pltpu.VMEM((512, 512), BF16),
            pltpu.VMEM((3, 96, 384), BF16),
            pltpu.VMEM((384, 128), BF16),
            pltpu.VMEM((3, 384, 128), BF16),
            pltpu.VMEM((VIEWS, 4, 32, 128), BF16),
            pltpu.VMEM((VIEWS, 2, 32, 128), BF16),
            pltpu.VMEM((VIEWS, 2, 32, 128), BF16),
            pltpu.VMEM((2048, 512), BF16),
            pltpu.VMEM((256, 2048), BF16),
            pltpu.VMEM((3, 12, 16, 128), F32),
            pltpu.VMEM((12, 48, 128), BF16),
            pltpu.VMEM((12, 48, 128), BF16),
            pltpu.VMEM((12, 48, 128), BF16),
            pltpu.VMEM((8, 3, 8, 128), F32),
            pltpu.VMEM((384, 256), BF16),
            pltpu.VMEM((384, 256), BF16),
            pltpu.VMEM((320, 256), BF16),
            pltpu.VMEM((72, 384), F32),
            pltpu.VMEM((288, 256), BF16),
            pltpu.VMEM((96, 384), BF16),
            pltpu.VMEM((96, 384), BF16),
            pltpu.VMEM((8, 384, 128), F32),
            pltpu.VMEM((8, 12, 96, 128), BF16),
            pltpu.VMEM((6, 320, 128), F32),
            pltpu.VMEM((6, 320, 128), BF16),
            pltpu.VMEM((6, 10, 96, 128), BF16),
            pltpu.VMEM((8, 8, 32, 128), BF16),
            pltpu.VMEM((4, 256, 128), BF16),
            pltpu.VMEM((96, 384), F32),
            pltpu.VMEM((3, 16, 384), F32),
            pltpu.VMEM((2, 4, 16, 128), F32),
            pltpu.VMEM((VIEWS, 48, 128), BF16),
            pltpu.VMEM((16, 128), F32),
            pltpu.VMEM((1024, 512), BF16),
            pltpu.VMEM((2, 2, 16, 128), BF16),
            pltpu.VMEM((2, 16, 128), BF16),
            pltpu.VMEM((2, 16, 128), BF16),
            pltpu.VMEM((RING * PIECE, 128), F32),
            pltpu.VMEM((RING, PIECE, 128), BF16),
            pltpu.VMEM((RING, PIECE, 128), BF16),
            pltpu.VMEM((VIEWS, MESSAGE, 128), BF16),
            pltpu.VMEM((LAYERS, MESSAGE, 128), BF16),
            dma((21,)),
            dma((2, 3)),
            dma((2, 2)),
            dma((2, 2)),
            dma((2, 2)),
            dma((2, 3)),
            dma((2, RING - 1)),
            dma((2, 3)),
            dma((2, 3)),
            dma((2, RING - 1)),
        ],
        compiler_params=pltpu.CompilerParams(
            collective_id=0, has_side_effects=True, vmem_limit_bytes=VMEM_BYTES
        ),
    )(
        volume,
        upstream,
        measured.reshape(32, 128),
        dual_gain.reshape(32, 128),
        pattern.transpose(0, 1, 3, 2).reshape(VIEWS, 16, 64),
        angle.reshape(VIEWS, 64),
        w1.transpose(0, 2, 1),
        bias1.reshape(1, 32),
        w2,
        bias2.reshape(1, 32),
        w3.reshape(9, 96),
        pick_x,
        pick_j,
        band1,
        band3,
        response,
        place,
        spread_x,
        rep3,
        fold1,
        fold3,
    )
    scale = 1.0 / math.sqrt(volume.size * SLABS * VIEWS)
    new_volume, grad_volume, grad_w1, grad_bias1, grad_w2, grad_bias2, grad_w3 = pl.pallas_call(
        functools.partial(emit_kernel, scale),
        name="emit",
        out_shape=(
            jax.ShapeDtypeStruct((4, 8, 128), F32),
            jax.ShapeDtypeStruct((4, 8, 128), F32),
            jax.ShapeDtypeStruct((9, 6, 32), F32),
            jax.ShapeDtypeStruct((1, 32), F32),
            jax.ShapeDtypeStruct((9, 32, 96), F32),
            jax.ShapeDtypeStruct((1, 32), F32),
            jax.ShapeDtypeStruct((9, 1, 96), F32),
        ),
        in_specs=vmem_specs(3),
        out_specs=tuple(vmem_specs(7)),
    )(new_volume, grad_volume, total)
    return (
        new_volume,
        grad_volume,
        grad_w1.transpose(0, 2, 1),
        grad_bias1.reshape(32),
        grad_w2,
        grad_bias2.reshape(32),
        grad_w3,
    )


def solution(mesh):
    placed = (
        P("slab", "view", None),
        P("view", "slab", None),
        P("view", "slab", None),
        P(None, "slab", None, None),
        P(None, "slab", None),
        P(),
        P(),
        P(),
        P(),
        P(),
        P(),
        P("slab", "view", None),
    )
    return jax.shard_map(
        body,
        mesh=mesh,
        in_specs=placed,
        out_specs=(P("slab", "view", None), P("slab", "view", None), P(), P(), P(), P(), P()),
        check_vma=False,
    )
```

```python
import functools
import math

import jax
import jax.numpy as jnp
import ml_dtypes
import numpy as np
from jax import lax
from jax.experimental import pallas as pl
from jax.experimental.pallas import tpu as pltpu
from jax.sharding import PartitionSpec as P

F32 = jnp.float32
BF16 = jnp.bfloat16
MESH = pl.DeviceIdType.MESH
VIEWS = 4
RING = 8
LAYERS = 4
SLABS = RING * LAYERS
PIECE = 40
SMALL = 16
MESSAGE = SMALL + PIECE
VMEM_BYTES = 56 * 1024 * 1024
HELD = pl.ANY


def mm(a, b):
    return lax.dot_general(a, b, (((1,), (0,)), ((), ())), preferred_element_type=F32)


def mmt(a, b):
    return lax.dot_general(a, b, (((1,), (1,)), ((), ())), preferred_element_type=F32)


def iota(shape, dim):
    return lax.broadcasted_iota(jnp.int32, shape, dim)


def one(cond):
    return jnp.where(cond, 1.0, 0.0).astype(BF16)


def host_bf16(cond):
    return np.asarray(cond, np.float32).astype(ml_dtypes.bfloat16)


def tile_constants():
    row, col = np.arange(128)[:, None], np.arange(128)[None, :]
    pick_x = host_bf16(col == 4 * (row % 32) + row // 32)
    r, c = np.arange(512)[:, None], np.arange(1024)[None, :]
    xi, quarter, z, y8 = r // 128, r // 32 % 4, r // 8 % 4, r % 8
    yt, j = c // 128, c % 64
    place = host_bf16(
        (2 * quarter + y8 // 4 == yt) & (z == j // 16) & (y8 % 4 == j // 4 % 4) & (xi == j % 4)
    )
    r, c = np.arange(64)[:, None], np.arange(128)[None, :]
    pick_j = host_bf16((c < 64) & (c % 4 == r // 16) & (c // 4 == r % 16))
    r, c = np.arange(512)[:, None], np.arange(512)[None, :]
    spread_x = host_bf16((r // 32 % 4 == c // 128) & (c % 128 == 4 * (r % 32) + r // 128))
    return pick_x, place, pick_j, spread_x


def weight_constants():
    lane = np.arange(384)
    band1 = np.zeros((2, 9, 6, 256), np.float32)
    fold1 = np.zeros((384, 128), np.float32)
    for a in range(3):
        for b in range(3):
            for e in range(3):
                for c in range(2):
                    band1[c, 3 * a + b, 2 * e + c, (a * 3 + e) * 16 + b] = 1.0
                    fold1[
                        ((c * 3 + a) * 3 + e) * 16 + 3 + b, 6 * (3 * a + b) + 2 * e + c
                    ] = 1.0
    fold1[288, 54] = 1.0
    band3 = np.zeros((3, 9, 256), np.float32)
    for a in range(3):
        for b in range(3):
            for e in range(3):
                band3[e, 3 * (2 - a) + (2 - b), (a * 3 + e) * 16 + b] = 1.0
    rep3 = np.zeros((3, 96, 384), np.float32)
    for e in range(3):
        rep3[e, 32 * e + lane % 32, lane] = 1.0
    fold3 = np.zeros((3, 384, 128), np.float32)
    for e in range(3):
        live = lane[lane < 320]
        fold3[e, live, 32 * e + live % 32] = 1.0
    return tuple(host_bf16(x) for x in (band1, band3, rep3, fold1, fold3))


def own_order():
    return one(iota((64, 64), 1) == 2 * (iota((64, 64), 0) % 32) + iota((64, 64), 0) // 32)


def choose_tiles(pattern_ref, angle_ref, choice, chosen, first):
    order = own_order()
    lanes = iota((64, 256), 1)
    lines = []
    for g in range(VIEWS):
        held = pattern_ref[g].astype(F32).astype(BF16)
        ids = mmt(order, held).astype(jnp.int32)
        for k in range(16):
            at = 256 * (k // 2) + 64 * g
            side = 256 * (k % 2)
            choice[at : at + 64, side : side + 256] = one(lanes == ids[:, k : k + 1])
        lines.append(mmt(held, order))
    line = jnp.concatenate(lines, axis=1).astype(jnp.int32)
    tile = iota((128, 256), 0) + first
    for k in range(16):
        at = 128 * (k % 2)
        chosen[at : at + 128, 256 * (k // 2) : 256 * (k // 2) + 256] = one(
            tile == line[k : k + 1, :]
        )
    angles = mmt(order, angle_ref[...].astype(F32).astype(BF16)).astype(jnp.int32)
    return jnp.concatenate([angles[:, g : g + 1] for g in range(VIEWS)], axis=0)


def project(field_rows, choice, angles, response_turned, pick_x_ref, place_ref):
    by_x = mmt(pick_x_ref[...], field_rows).astype(BF16)
    wide = jnp.concatenate([by_x[32 * i : 32 * i + 32] for i in range(4)], axis=1)
    spread = mm(wide, place_ref[...]).astype(BF16)
    tiles = jnp.concatenate([spread[:, 128 * i : 128 * i + 128] for i in range(8)], axis=0)
    zero = jnp.zeros((256, 128), F32)
    wide_tiles = tiles.astype(F32)
    low = iota((256, 128), 1) < 64
    both = jnp.concatenate(
        [jnp.where(low, wide_tiles, zero), jnp.where(low, zero, wide_tiles)], axis=0
    ).astype(BF16)
    pairs = [mm(choice[256 * p : 256 * p + 256, :], both).astype(BF16) for p in range(8)]
    lines = mm(jnp.concatenate(pairs, axis=1), response_turned[...])
    half = iota((256, 128), 1) // 64
    total = jnp.zeros((256, 128), F32)
    for p in range(4):
        total = total + jnp.where(angles == 2 * p + half, lines[:, 128 * p : 128 * p + 128], 0.0)
    return total + pltpu.roll(total, 64, 1)


def doubled_rows(ref, part):
    low = iota((32, 128), 1) < 64
    parts = []
    for g in range(VIEWS):
        rows = ref[g, part].astype(F32)
        turned = pltpu.roll(rows, 64, 1)
        parts.append(jnp.where(low, rows, turned))
        parts.append(jnp.where(low, turned, rows))
    return jnp.concatenate(parts, axis=0)


def backproject(doubled, chosen, angles, response_ref, pick_j_ref, spread_x_ref, count):
    half = iota((256, 128), 1) // 64
    masked = [
        jnp.where(angles == 2 * p + half, doubled, 0.0).astype(BF16) for p in range(4)
    ]
    contrib = mm(jnp.concatenate(masked, axis=1), response_ref[...])
    high = contrib.astype(BF16)
    blocks = [high[:, 128 * p : 128 * p + 128] for p in range(8)]
    if count == 64:
        rest = (contrib - high.astype(F32)).astype(BF16)
        blocks = [
            jnp.concatenate([block, rest[:, 128 * p : 128 * p + 128]], axis=1)
            for p, block in enumerate(blocks)
        ]
    stacked = jnp.concatenate(blocks, axis=0)
    skip = (128 - count) // 2
    left = jnp.concatenate(
        [chosen[skip : skip + count, :], chosen[128 + skip : 128 + skip + count, :]], axis=0
    )
    sums = mm(left, stacked)
    if count == 64:
        sums = sums[:, :128] + sums[:, 128:]
    tiles = sums[:count] + pltpu.roll(sums[count:], 64, 1)
    top = tiles.astype(BF16)
    if count == 64:
        top = jnp.concatenate([top, (tiles - top.astype(F32)).astype(BF16)], axis=0)
    by_j = mmt(pick_j_ref[...], top).astype(BF16)
    wide = jnp.concatenate([by_j[16 * i : 16 * i + 16] for i in range(4)], axis=1)
    return mm(wide, spread_x_ref[...])


def start_copies(pairs, sems):
    copies = []
    for n, (source, target, device) in enumerate(pairs):
        copies.append(
            pltpu.make_async_remote_copy(
                src_ref=source,
                dst_ref=target,
                send_sem=sems.at[0, n],
                recv_sem=sems.at[1, n],
                device_id=device,
                device_id_type=MESH,
            )
        )
    for copy in copies:
        copy.start()
    return copies


def wait_in(copies):
    for copy in copies:
        copy.wait_recv()


def wait_out(copies):
    for copy in copies:
        copy.wait_send()


def shifted(value, e, lane):
    if e == 1:
        return value
    if e == 0:
        return jnp.where(lane == 0, 0.0, pltpu.roll(value, 1, 1))
    return jnp.where(lane == 127, 0.0, pltpu.roll(value, 127, 1))


def prepare_weights(
    w1_ref, w2_ref, w3_ref, band1_ref, band3_ref, rep3_ref, t1v, t1b, t3t, t3, t1t, w2r, w2t
):
    eye32 = one(iota((32, 32), 0) == iota((32, 32), 1))
    for c, ref in ((0, t1v), (1, t1b)):
        base = jnp.zeros((32, 256), F32)
        for tap in range(9):
            turned = mmt(eye32, w1_ref[tap]).astype(BF16)
            base = base + mm(turned, band1_ref[c, tap])
        for yo in range(12):
            ref[32 * yo : 32 * yo + 32, :] = pltpu.roll(base, yo + 1, 1).astype(BF16)
    eye96 = one(iota((96, 96), 0) == iota((96, 96), 1))
    w3 = w3_ref[...]
    w3_turned = mmt(eye96, w3).astype(BF16)
    base = jnp.zeros((32, 256), F32)
    for e in range(3):
        base = base + mm(w3_turned[32 * (2 - e) : 32 * (2 - e) + 32], band3_ref[e])
    for yo in range(10):
        t3t[32 * yo : 32 * yo + 32, :] = pltpu.roll(base, yo + 2, 1).astype(BF16)
    step = iota((8, 384), 1) // 32 - iota((8, 384), 0)
    for e in range(3):
        line = mm(w3, rep3_ref[e])
        for a in range(3):
            block = jnp.zeros((8, 384), F32)
            for b in range(3):
                block = block + jnp.where(step == b, line[3 * a + b : 3 * a + b + 1, :], 0.0)
            t3[8 * (3 * a + e) : 8 * (3 * a + e) + 8, :] = block
    rep = one(iota((32, 256), 0) == iota((32, 256), 1) % 32)
    turned = [mm(w1_ref[tap], rep) for tap in range(9)]
    row16 = iota((16, 256), 0)
    row_y = jnp.where(row16 < 8, row16, jnp.where(row16 == 8, -1, 8))
    step = iota((16, 256), 1) // 32 - row_y + 1
    step = jnp.where(row16 < 10, step, -1)
    for a in range(3):
        for c in range(2):
            for e in range(3):
                row = 2 * (2 - e) + c
                block = jnp.zeros((16, 256), F32)
                for b in range(3):
                    tap = 3 * (2 - a) + (2 - b)
                    block = block + jnp.where(step == b, turned[tap][row : row + 1, :], 0.0)
                at = 16 * ((a * 2 + c) * 3 + e)
                t1t[at : at + 16, :] = block.astype(BF16)
    places = [one(iota((96, 384), 1) == iota((96, 384), 0) + 96 * b) for b in range(3)]
    keep = iota((96, 96), 1) // 32 == 2 - iota((96, 96), 0) // 32
    same = one(iota((32, 96), 0) == iota((32, 96), 1) % 32)
    for a in range(3):
        plain = jnp.zeros((32, 384), F32)
        across = jnp.zeros((32, 384), F32)
        for b in range(3):
            plain = plain + mm(w2_ref[3 * a + b], places[b])
            tower = jnp.concatenate([w2_ref[3 * (2 - a) + (2 - b)].astype(F32)] * 3, axis=0)
            tower = jnp.where(keep, tower, 0.0).astype(BF16)
            across = across + mm(mmt(same, tower).astype(BF16), places[b])
        w2r[32 * a : 32 * a + 32, :] = plain.astype(BF16)
        w2t[32 * a : 32 * a + 32, :] = across.astype(BF16)


def pair_of(ref, z, count):
    cols = [jnp.concatenate([ref[z + n + a] for a in range(count)], axis=0) for n in range(2)]
    return jnp.concatenate(cols, axis=1)


def stacked_rows(ref, z, y):
    cols = [ref[z + n, pl.ds(y, 3)].reshape(288, 128) for n in range(2)]
    return jnp.concatenate(cols, axis=1)


def split_pairs(outs):
    return [out[:, 128 * n : 128 * n + 128] for out in outs for n in range(2)]


def step_kernel(
    volume_hbm,
    upstream_hbm,
    measured_hbm,
    gain_hbm,
    pattern_hbm,
    angle_hbm,
    w1_hbm,
    bias1_hbm,
    w2_hbm,
    bias2_hbm,
    w3_hbm,
    pick_x_hbm,
    pick_j_hbm,
    band1_hbm,
    band3_hbm,
    response_hbm,
    place_hbm,
    spread_x_hbm,
    rep3_hbm,
    fold1_hbm,
    fold3_hbm,
    new_ref,
    grad_ref,
    final_in,
    volume_ref,
    upstream_ref,
    measured_ref,
    gain_ref,
    pattern_ref,
    angle_ref,
    w1_ref,
    bias1_ref,
    w2_ref,
    bias2_ref,
    w3_ref,
    pick_x_ref,
    pick_j_ref,
    band1_ref,
    band3_ref,
    response_ref,
    place_ref,
    spread_x_ref,
    rep3_ref,
    fold1_ref,
    fold3_ref,
    pack,
    pack_low,
    pack_high,
    choice,
    chosen,
    fields,
    back_planes,
    ins,
    backs,
    ups,
    ups_own,
    t1v,
    t1b,
    t3t,
    t3,
    t1t,
    w2r,
    w2t,
    pre1,
    h3,
    ct3,
    h2,
    s3,
    s2z,
    s1,
    g2,
    g3,
    parts_own,
    parts,
    edge_rows,
    response_turned,
    edges,
    edges_low,
    edges_high,
    totals,
    sums,
    ring_in,
    view_in,
    layer_in,
    local_sems,
    pack_sems,
    plane_sems,
    back_sems,
    edge_sems,
    part_sems,
    ring_sems,
    view_sems,
    layer_sems,
    final_sems,
):
    slab, member = lax.axis_index("slab"), lax.axis_index("view")
    above, below = lax.rem(slab + 1, SLABS), lax.rem(slab + SLABS - 1, SLABS)
    left, right = lax.rem(member + VIEWS - 1, VIEWS), lax.rem(member + 1, VIEWS)
    place, layer = lax.rem(slab, RING), lax.div(slab, RING)
    view_peers = [
        VIEWS - 1 - member,
        lax.rem(member + 2, VIEWS),
        member + 1 - 2 * lax.rem(member, 2),
    ]
    ring_peers = [layer * RING + lax.rem(place + off, RING) for off in range(1, RING)]
    layer_peers = [
        lax.rem(layer + off, LAYERS) * RING + place for off in range(1, LAYERS)
    ]
    depth, height = 4 * SLABS, 8 * VIEWS

    barrier = pltpu.get_barrier_semaphore()
    peers = [{"view": peer} for peer in view_peers]
    peers += [{"slab": peer} for peer in ring_peers + layer_peers + [above, below]]
    for peer in peers:
        pl.semaphore_signal(barrier, inc=1, device_id=peer, device_id_type=MESH)

    loads = {}
    for n, (name, source, target) in enumerate(
        (
            ("volume", volume_hbm, volume_ref),
            ("upstream", upstream_hbm, upstream_ref),
            ("measured", measured_hbm, measured_ref),
            ("gain", gain_hbm, gain_ref),
            ("pattern", pattern_hbm, pattern_ref),
            ("angle", angle_hbm, angle_ref),
            ("w1", w1_hbm, w1_ref),
            ("w2", w2_hbm, w2_ref),
            ("w3", w3_hbm, w3_ref),
            ("band1", band1_hbm, band1_ref),
            ("band3", band3_hbm, band3_ref),
            ("rep3", rep3_hbm, rep3_ref),
            ("pick_x", pick_x_hbm, pick_x_ref),
            ("place", place_hbm, place_ref),
            ("response", response_hbm, response_ref),
            ("pick_j", pick_j_hbm, pick_j_ref),
            ("spread_x", spread_x_hbm, spread_x_ref),
            ("bias1", bias1_hbm, bias1_ref),
            ("bias2", bias2_hbm, bias2_ref),
            ("fold3", fold3_hbm, fold3_ref),
            ("fold1", fold1_hbm, fold1_ref),
        )
    ):
        loads[name] = pltpu.make_async_copy(source, target, local_sems.at[n])
        loads[name].start()

    def loaded(*which):
        for name in which:
            loads[name].wait()

    loaded("volume", "upstream", "measured", "gain")
    pack[member, 0] = volume_ref[...].reshape(32, 128).astype(BF16)
    pack[member, 1] = upstream_ref[...].astype(F32).reshape(32, 128).astype(BF16)
    pack[member, 2] = measured_ref[...].astype(BF16)
    pack[member, 3] = gain_ref[...].astype(BF16)
    pl.semaphore_wait(barrier, len(peers))

    pending = []
    pack_copies = start_copies(
        [(pack.at[member], pack.at[member], {"view": p}) for p in view_peers], pack_sems
    )
    pending += pack_copies
    loaded("pattern", "angle")
    angles = choose_tiles(pattern_ref, angle_ref, choice, chosen, 64 * member - 32)
    loaded("w1", "w2", "w3", "band1", "band3", "rep3")
    prepare_weights(
        w1_ref, w2_ref, w3_ref, band1_ref, band3_ref, rep3_ref, t1v, t1b, t3t, t3, t1t, w2r, w2t
    )
    loaded("pick_x", "place", "response", "pick_j", "spread_x", "bias1", "bias2")
    response_turned[...] = response_ref[...].T
    wait_in(pack_copies)
    plane_copies = start_copies(
        [
            (pack.at[:, pl.ds(0, 2)], pack_low, {"slab": above}),
            (pack.at[:, pl.ds(0, 2)], pack_high, {"slab": below}),
        ],
        plane_sems,
    )
    pending += plane_copies

    field_rows = pack[:, 0].reshape(128, 128)
    got = project(field_rows, choice, angles, response_turned, pick_x_ref, place_ref)
    gain_rows = doubled_rows(pack, 3)
    dual = (gain_rows * (got - doubled_rows(pack, 2))).astype(BF16).astype(F32)
    spread = backproject(dual, chosen, angles, response_ref, pick_j_ref, spread_x_ref, 128)
    for z in range(4):
        plane = [spread[4 * z : 4 * z + 4, 128 * yt : 128 * yt + 128] for yt in range(4)]
        back_planes[4 + z] = jnp.concatenate(plane, axis=0).astype(BF16)
    back_copies = start_copies(
        [
            (back_planes.at[pl.ds(5, 3)], back_planes.at[pl.ds(1, 3)], {"slab": above}),
            (back_planes.at[pl.ds(4, 3)], back_planes.at[pl.ds(8, 3)], {"slab": below}),
        ],
        back_sems,
    )
    pending += back_copies

    wait_in(plane_copies)
    low_z, low_y = 4 * slab - 4, 8 * member - 4
    lane16 = iota((16, 128), 1)
    global_y = iota((16, 128), 0) + low_y
    inside_y = (global_y >= 0) & (global_y < height)
    lane8 = iota((8, 128), 1)
    for field in range(2):
        for source, first, low in ((pack_low, 1, 0), (pack, 4, 4), (pack_high, 8, 8)):
            own, before, after = (
                source[view, field].astype(F32) for view in (member, left, right)
            )
            for z in range(first, min(low + 4, 11)):
                at = 8 * (z - low)
                fields[field, z, 4:12, :] = own[at : at + 8]
                fields[field, z, 0:4, :] = before[at + 4 : at + 8]
                fields[field, z, 12:16, :] = after[at : at + 4]

    def shifts_of(field, target):
        def one_plane(z, carry):
            inside = inside_y & (z + low_z >= 0) & (z + low_z < depth)
            held = back_planes[z].astype(F32) if field == 2 else fields[field, z]
            plane = jnp.where(inside, held, 0.0)
            plane = plane.astype(BF16).astype(F32)
            for e in range(3):
                target[z, 16 * e : 16 * e + 16, :] = shifted(plane, e, lane16).astype(BF16)
            return carry

        lax.fori_loop(1, 11, one_plane, 0, unroll=10)

    shifts_of(0, ins)
    shifts_of(1, ups)
    ups_own[...] = jnp.zeros(ups_own.shape, F32)
    for z in range(4):
        plane = upstream_ref[z].astype(F32)
        for e in range(3):
            ups_own[2 + z, e] = shifted(plane, 2 - e, lane8)

    def third_turned(p, carry):
        z = 2 * p
        out = mm(t3t[:, :144], pair_of(ups, z + 2, 3))
        ct3[z] = out[:, :128]
        ct3[z + 1] = out[:, 128:]
        return carry

    lax.fori_loop(0, 3, third_turned, 0, unroll=3)
    eye32 = iota((32, 32), 0) == iota((32, 32), 1)
    bias1 = jnp.sum(jnp.where(eye32, bias1_ref[...], 0.0), axis=1, keepdims=True)
    bias2 = jnp.sum(jnp.where(eye32, bias2_ref[...], 0.0), axis=1, keepdims=True)
    bias1_rows = jnp.concatenate([jnp.broadcast_to(bias1, (32, 128))] * 12, axis=0)

    def first_volume(p, carry):
        z = 2 * p
        out = mm(t1v[:, :144], pair_of(ins, z + 1, 3))
        pre1[z] = out[:, :128] + bias1_rows
        pre1[z + 1] = out[:, 128:] + bias1_rows
        return carry

    lax.fori_loop(0, 4, first_volume, 0, unroll=4)
    s2z[...] = jnp.zeros(s2z.shape, BF16)
    g2[...] = jnp.zeros(g2.shape, F32)
    g3[...] = jnp.zeros(g3.shape, F32)

    wait_in(back_copies)
    shifts_of(2, backs)

    def first_back(p, carry):
        z = 2 * p
        out = mm(t1b[:, :144], pair_of(backs, z + 1, 3))
        pre1[z] += out[:, :128]
        pre1[z + 1] += out[:, 128:]
        return carry

    lax.fori_loop(0, 4, first_back, 0, unroll=4)

    lane384 = iota((384, 128), 1)
    row_y1 = iota((384, 128), 0) // 32 + low_y + 2
    inside1 = (row_y1 >= 0) & (row_y1 < height)

    def activate(z, keep_slope):
        value = pre1[z]
        gate = 0.5 * jnp.tanh(0.5 * value) + 0.5
        act = value * gate
        if keep_slope:
            pre1[z] = gate + act * (1.0 - gate)
        inside = inside1 & (z + low_z + 2 >= 0) & (z + low_z + 2 < depth)
        act = jnp.where(inside, act, 0.0)
        for e in range(3):
            h3[z, :, 32 * e : 32 * e + 32, :] = (
                shifted(act, e, lane384).astype(BF16).reshape(12, 32, 128)
            )

    def activate_outer(n, carry):
        activate(n + 4 * (n // 2), False)
        return carry

    def activate_inner(n, carry):
        activate(n + 2, True)
        return carry

    lax.fori_loop(0, 4, activate_outer, 0, unroll=4)
    lax.fori_loop(0, 4, activate_inner, 0, unroll=4)

    lane32 = iota((32, 128), 1)

    def second(y, carry):
        out = split_pairs([mm(w2r[:, :288], stacked_rows(h3, 2 * p, y)) for p in range(4)])
        ok_y = (y + low_y + 3 >= 0) & (y + low_y + 3 < height)
        at = pl.multiple_of(32 * y, 32)
        for z in range(6):
            value = out[z][:32] + out[z + 1][32:64] + out[z + 2][64:] + bias2
            gate = 0.5 * jnp.tanh(0.5 * value) + 0.5
            act = value * gate
            slope = gate + act * (1.0 - gate)
            ok = ok_y & (z + low_z + 3 >= 0) & (z + low_z + 3 < depth)
            live = jnp.where(ok, 1.0, 0.0)
            h2[z, pl.ds(at, 32), :] = (act * live).astype(BF16)
            slope = slope * ct3[z, pl.ds(at, 32), :] * live
            for e in range(3):
                s3[z, y, 32 * e : 32 * e + 32, :] = shifted(slope, e, lane32).astype(BF16)
        return carry

    lax.fori_loop(0, 10, second, 0, unroll=10)

    for z in range(4):
        s2z[z + 2] = s3[z + 1, 1:9, 32:64, :]
    ones = jnp.ones((16, 768), BF16)

    def second_grad(y, carry):
        turned = jnp.concatenate(
            [
                jnp.concatenate([s2z[z + 1 - a, y] for z in range(1, 7)], axis=1)
                for a in range(3)
            ],
            axis=0,
        )
        plain = jnp.concatenate(
            [h3[z, pl.ds(y + 1, 3)].reshape(288, 128) for z in range(1, 7)], axis=1
        )
        g2[:, :304] += mmt(turned, jnp.concatenate([plain, ones], axis=0))
        return carry

    lax.fori_loop(0, 8, second_grad, 0, unroll=8)

    turned = jnp.concatenate(
        [
            jnp.concatenate(
                [ups_own[z + 2 - a, e] for a in range(3) for e in range(3)], axis=0
            ).astype(BF16)
            for z in range(6)
        ],
        axis=1,
    )
    plain = jnp.concatenate([h2[z] for z in range(6)], axis=1)
    cross = mmt(turned, plain)
    step10 = iota((8, 320), 1) // 32 - iota((8, 320), 0)
    for a in range(3):
        for e in range(3):
            block = cross[8 * (3 * a + e) : 8 * (3 * a + e) + 8]
            for b in range(3):
                g3[e, 3 * a + b : 3 * a + b + 1, 0:320] = jnp.sum(
                    jnp.where(step10 == b, block, 0.0), axis=0, keepdims=True
                )
    loaded("fold1", "fold3")
    third = jnp.zeros((16, 128), F32)
    for e in range(3):
        value = g3[e]
        high = value.astype(BF16)
        rest = (value - high.astype(F32)).astype(BF16)
        third = third + mm(high, fold3_ref[e]) + mm(rest, fold3_ref[e])

    lanes = iota((32, 128), 1)
    for tap in range(9):
        a, b = tap // 3, tap % 3
        block = g2[32 * a : 32 * a + 32, :]
        if b:
            block = pltpu.roll(block, 384 - 96 * b, 1)
        totals[32 * tap : 32 * tap + 32, :] = jnp.where(
            lanes < (97 if b == 2 else 96), block[:, :128], 0.0
        )
    totals[288:304, :] = third
    totals[304:320, :] = jnp.zeros((16, 128), F32)
    for n in range(RING):
        sums[n] = totals[PIECE * n : PIECE * n + PIECE, :].astype(BF16)
    ring_in[place] = sums[place]
    ring_copies = start_copies(
        [(sums.at[lax.rem(peer, RING)], ring_in.at[place], {"slab": peer}) for peer in ring_peers],
        ring_sems,
    )
    pending += ring_copies

    def second_turned(y, carry):
        out = split_pairs([mm(w2t[:, :288], stacked_rows(s3, 2 * p, y)) for p in range(3)])
        at = pl.multiple_of(32 * y, 32)
        from_ = pl.multiple_of(32 * y + 64, 32)
        for z in range(4):
            value = out[z][:32] + out[z + 1][32:64] + out[z + 2][64:]
            s1[z, pl.ds(at, 32), :] = (value * pre1[z + 2, pl.ds(from_, 32), :]).astype(BF16)
        return carry

    lax.fori_loop(0, 8, second_turned, 0, unroll=8)

    out = split_pairs([mm(t1t[...], pair_of(s1, 2 * p, 1)) for p in range(2)])
    for c in range(2):
        for z in range(-1, 5):
            total = jnp.zeros((16, 128), F32)
            for e in range(3):
                part = jnp.zeros((16, 128), F32)
                for a in range(3):
                    if 0 <= z + a - 1 < 4:
                        at = 16 * ((a * 2 + c) * 3 + e)
                        part = part + out[z + a - 1][at : at + 16]
                total = total + shifted(part, e, lane16)
            if z == -1:
                edges[0, c] = total.astype(BF16)
            elif z == 4:
                edges[1, c] = total.astype(BF16)
            else:
                parts_own[c, z] = total
    edge_copies = start_copies(
        [
            (edges.at[1], edges_low, {"slab": above}),
            (edges.at[0], edges_high, {"slab": below}),
        ],
        edge_sems,
    )
    pending += edge_copies

    turned = jnp.concatenate([s1[z] for z in range(4)], axis=1)
    plain = jnp.concatenate(
        [
            jnp.concatenate(
                [ins[z + 3 + a] for a in range(3)]
                + [backs[z + 3 + a] for a in range(3)]
                + [jnp.ones((96, 128), BF16)],
                axis=0,
            )
            for z in range(4)
        ],
        axis=1,
    )
    cross = mmt(turned, plain)
    total = cross[:32]
    for yo in range(1, 8):
        total = total + pltpu.roll(cross[32 * yo : 32 * yo + 32], 384 - yo, 1)
    high = total.astype(BF16)
    rest = (total - high.astype(F32)).astype(BF16)
    first_grads = mm(high, fold1_ref[...]) + mm(rest, fold1_ref[...])
    view_in[member, 0:SMALL, :] = jnp.where(
        iota((16, 128), 1) < 64, first_grads[:16], pltpu.roll(first_grads[16:], 64, 1)
    ).astype(BF16)

    wait_in(ring_copies)
    ring_total = ring_in[0].astype(F32)
    for n in range(1, RING):
        ring_total = ring_total + ring_in[n].astype(F32)
    view_in[member, SMALL:, :] = ring_total.astype(BF16)
    view_copies = start_copies(
        [(view_in.at[member], view_in.at[member], {"view": p}) for p in view_peers], view_sems
    )

    wait_in(edge_copies)
    has_low = jnp.where(slab > 0, 1.0, 0.0)
    has_high = jnp.where(slab < SLABS - 1, 1.0, 0.0)
    for c in (1, 0):
        parts_own[c, 0] += has_low * edges_low[c].astype(F32)
        parts_own[c, 3] += has_high * edges_high[c].astype(F32)
        for z in range(4):
            at = 8 * (1 - c) + 2 * z
            edge_rows[at : at + 2, :] = parts_own[c, z, 8:10, :]
    parts[member, 0:32, :] = jnp.concatenate(
        [parts_own[1, z, 0:8, :] for z in range(4)], axis=0
    ).astype(BF16)
    parts[member, 32:48, :] = edge_rows[...].astype(BF16)
    part_copies = start_copies(
        [(parts.at[member], parts.at[member], {"view": p}) for p in view_peers], part_sems
    )
    pending += part_copies

    t3_now = t3[:, :320].astype(BF16)
    out = split_pairs([mm(t3_now, pair_of(h2, 2 * p, 1)) for p in range(3)])
    for z in range(4):
        total = volume_ref[z]
        for e in range(3):
            part = jnp.zeros((8, 128), F32)
            for a in range(3):
                at = 8 * (3 * a + e)
                part = part + out[z + a][at : at + 8]
            total = total + shifted(part, e, lane8)
        new_ref[z] = total

    def sum_views():
        total = view_in[0].astype(F32)
        for n in range(1, VIEWS):
            total = total + view_in[n].astype(F32)
        return total.astype(BF16)

    wait_in(view_copies)
    layer_in[layer] = sum_views()
    layer_copies = start_copies(
        [(layer_in.at[layer], layer_in.at[layer], {"slab": p}) for p in layer_peers],
        layer_sems,
    )

    wait_in(part_copies)
    row8 = iota((8, 128), 0)
    rows = [None] * 16
    planes = [parts[view].astype(F32) for view in range(VIEWS)]
    for z in range(4):
        for view in range(VIEWS):
            value = planes[view][8 * z : 8 * z + 8]
            if view > 0:
                edge = planes[view - 1][33 + 2 * z : 34 + 2 * z]
                value = value + jnp.where(row8 == 0, edge, 0.0)
            if view < VIEWS - 1:
                edge = planes[view + 1][32 + 2 * z : 33 + 2 * z]
                value = value + jnp.where(row8 == 7, edge, 0.0)
            rows[4 * view + z] = value
    field_rows = jnp.concatenate(rows, axis=0).astype(BF16)
    got = project(field_rows, choice, angles, response_turned, pick_x_ref, place_ref)
    wait_in(layer_copies)
    layer_total = layer_in[0].astype(F32)
    for n in range(1, LAYERS):
        layer_total = layer_total + layer_in[n].astype(F32)
    final_in[place] = layer_total.astype(BF16)
    final_copies = start_copies(
        [(final_in.at[place], final_in.at[place], {"slab": p}) for p in ring_peers],
        final_sems,
    )
    echo = (gain_rows * got).astype(BF16).astype(F32)
    spread = backproject(echo, chosen, angles, response_ref, pick_j_ref, spread_x_ref, 64)
    spread = spread[:, :256] + spread[:, 256:]
    has_left = jnp.where(member > 0, 1.0, 0.0)
    has_right = jnp.where(member < VIEWS - 1, 1.0, 0.0)
    before = has_left * parts[left, 32:48, :].astype(F32)
    after = has_right * parts[right, 32:48, :].astype(F32)
    for z in range(4):
        value = parts_own[0, z][:8] + upstream_ref[z].astype(F32)
        value = value + jnp.where(row8 == 0, before[9 + 2 * z : 10 + 2 * z], 0.0)
        value = value + jnp.where(row8 == 7, after[8 + 2 * z : 9 + 2 * z], 0.0)
        for yt in range(2):
            grad_ref[z, 4 * yt : 4 * yt + 4, :] = (
                value[4 * yt : 4 * yt + 4, :]
                + spread[4 * z : 4 * z + 4, 128 * yt : 128 * yt + 128]
            )
    wait_out(pending)
    wait_in(final_copies)
    wait_out(view_copies + layer_copies + final_copies)


def emit_kernel(
    scale,
    new_ref,
    grad_ref,
    total_ref,
    new_out,
    grad_out,
    w1_out,
    bias1_out,
    w2_out,
    bias2_out,
    w3_out,
):
    new_out[...] = new_ref[...]
    grad_out[...] = grad_ref[...]
    whole = jnp.concatenate(
        [total_ref[n, SMALL:, :].astype(F32) for n in range(RING)], axis=0
    ) * scale
    small = total_ref[0, :SMALL, :].astype(F32)
    for n in range(1, RING):
        small = small + total_ref[n, :SMALL, :].astype(F32)
    small = jnp.concatenate([small, pltpu.roll(small, 64, 1)], axis=0)
    turned = (small * scale).T
    bias1_out[...] = turned[54:55, :]
    for tap in range(9):
        block = whole[32 * tap : 32 * tap + 32]
        w2_out[tap] = block[:, :96]
        w1_out[tap] = turned[6 * tap : 6 * tap + 6, :]
        w3_out[tap] = whole[288 + tap : 289 + tap, :96]
    bias2_out[...] = whole[160:192].T[96:97, :]


def vmem_specs(count):
    return [pl.BlockSpec(memory_space=pltpu.VMEM)] * count


def body(volume, measured, dual_gain, pattern, angle, response, w1, bias1, w2, bias2, w3, upstream):
    pick_x, place, pick_j, spread_x = [jnp.asarray(x) for x in tile_constants()]
    band1, band3, rep3, fold1, fold3 = [jnp.asarray(x) for x in weight_constants()]
    dma = pltpu.SemaphoreType.DMA
    new_volume, grad_volume, total = pl.pallas_call(
        step_kernel,
        name="step",
        out_shape=(
            jax.ShapeDtypeStruct((4, 8, 128), F32),
            jax.ShapeDtypeStruct((4, 8, 128), F32),
            jax.ShapeDtypeStruct((RING, MESSAGE, 128), BF16),
        ),
        in_specs=[pl.BlockSpec(memory_space=HELD)] * 21,
        out_specs=tuple(vmem_specs(3)),
        scratch_shapes=[
            pltpu.VMEM((4, 8, 128), F32),
            pltpu.VMEM((4, 8, 128), BF16),
            pltpu.VMEM((32, 128), F32),
            pltpu.VMEM((32, 128), F32),
            pltpu.VMEM((VIEWS, 16, 64), jnp.int32),
            pltpu.VMEM((VIEWS, 64), jnp.int32),
            pltpu.VMEM((9, 6, 32), BF16),
            pltpu.VMEM((1, 32), F32),
            pltpu.VMEM((9, 32, 96), BF16),
            pltpu.VMEM((1, 32), F32),
            pltpu.VMEM((9, 96), BF16),
            pltpu.VMEM((128, 128), BF16),
            pltpu.VMEM((64, 128), BF16),
            pltpu.VMEM((2, 9, 6, 256), BF16),
            pltpu.VMEM((3, 9, 256), BF16),
            pltpu.VMEM((512, 1024), BF16),
            pltpu.VMEM((512, 1024), BF16),
            pltpu.VMEM((512, 512), BF16),
            pltpu.VMEM((3, 96, 384), BF16),
            pltpu.VMEM((384, 128), BF16),
            pltpu.VMEM((3, 384, 128), BF16),
            pltpu.VMEM((VIEWS, 4, 32, 128), BF16),
            pltpu.VMEM((VIEWS, 2, 32, 128), BF16),
            pltpu.VMEM((VIEWS, 2, 32, 128), BF16),
            pltpu.VMEM((2048, 512), BF16),
            pltpu.VMEM((256, 2048), BF16),
            pltpu.VMEM((2, 12, 16, 128), F32),
            pltpu.VMEM((12, 16, 128), BF16),
            pltpu.VMEM((12, 48, 128), BF16),
            pltpu.VMEM((12, 48, 128), BF16),
            pltpu.VMEM((12, 48, 128), BF16),
            pltpu.VMEM((8, 3, 8, 128), F32),
            pltpu.VMEM((384, 256), BF16),
            pltpu.VMEM((384, 256), BF16),
            pltpu.VMEM((320, 256), BF16),
            pltpu.VMEM((72, 384), F32),
            pltpu.VMEM((288, 256), BF16),
            pltpu.VMEM((96, 384), BF16),
            pltpu.VMEM((96, 384), BF16),
            pltpu.VMEM((8, 384, 128), F32),
            pltpu.VMEM((8, 12, 96, 128), BF16),
            pltpu.VMEM((6, 320, 128), F32),
            pltpu.VMEM((6, 320, 128), BF16),
            pltpu.VMEM((6, 10, 96, 128), BF16),
            pltpu.VMEM((8, 8, 32, 128), BF16),
            pltpu.VMEM((4, 256, 128), BF16),
            pltpu.VMEM((96, 384), F32),
            pltpu.VMEM((3, 16, 384), F32),
            pltpu.VMEM((2, 4, 16, 128), F32),
            pltpu.VMEM((VIEWS, 48, 128), BF16),
            pltpu.VMEM((16, 128), F32),
            pltpu.VMEM((1024, 512), BF16),
            pltpu.VMEM((2, 2, 16, 128), BF16),
            pltpu.VMEM((2, 16, 128), BF16),
            pltpu.VMEM((2, 16, 128), BF16),
            pltpu.VMEM((RING * PIECE, 128), F32),
            pltpu.VMEM((RING, PIECE, 128), BF16),
            pltpu.VMEM((RING, PIECE, 128), BF16),
            pltpu.VMEM((VIEWS, MESSAGE, 128), BF16),
            pltpu.VMEM((LAYERS, MESSAGE, 128), BF16),
            dma((21,)),
            dma((2, 3)),
            dma((2, 2)),
            dma((2, 2)),
            dma((2, 2)),
            dma((2, 3)),
            dma((2, RING - 1)),
            dma((2, 3)),
            dma((2, 3)),
            dma((2, RING - 1)),
        ],
        compiler_params=pltpu.CompilerParams(
            collective_id=0, has_side_effects=True, vmem_limit_bytes=VMEM_BYTES
        ),
    )(
        volume,
        upstream,
        measured.reshape(32, 128),
        dual_gain.reshape(32, 128),
        pattern.transpose(0, 1, 3, 2).reshape(VIEWS, 16, 64),
        angle.reshape(VIEWS, 64),
        w1.transpose(0, 2, 1),
        bias1.reshape(1, 32),
        w2,
        bias2.reshape(1, 32),
        w3.reshape(9, 96),
        pick_x,
        pick_j,
        band1,
        band3,
        response,
        place,
        spread_x,
        rep3,
        fold1,
        fold3,
    )
    scale = 1.0 / math.sqrt(volume.size * SLABS * VIEWS)
    new_volume, grad_volume, grad_w1, grad_bias1, grad_w2, grad_bias2, grad_w3 = pl.pallas_call(
        functools.partial(emit_kernel, scale),
        name="emit",
        out_shape=(
            jax.ShapeDtypeStruct((4, 8, 128), F32),
            jax.ShapeDtypeStruct((4, 8, 128), F32),
            jax.ShapeDtypeStruct((9, 6, 32), F32),
            jax.ShapeDtypeStruct((1, 32), F32),
            jax.ShapeDtypeStruct((9, 32, 96), F32),
            jax.ShapeDtypeStruct((1, 32), F32),
            jax.ShapeDtypeStruct((9, 1, 96), F32),
        ),
        in_specs=vmem_specs(3),
        out_specs=tuple(vmem_specs(7)),
    )(new_volume, grad_volume, total)
    return (
        new_volume,
        grad_volume,
        grad_w1.transpose(0, 2, 1),
        grad_bias1.reshape(32),
        grad_w2,
        grad_bias2.reshape(32),
        grad_w3,
    )


def solution(mesh):
    placed = (
        P("slab", "view", None),
        P("view", "slab", None),
        P("view", "slab", None),
        P(None, "slab", None, None),
        P(None, "slab", None),
        P(),
        P(),
        P(),
        P(),
        P(),
        P(),
        P("slab", "view", None),
    )
    return jax.shard_map(
        body,
        mesh=mesh,
        in_specs=placed,
        out_specs=(P("slab", "view", None), P("slab", "view", None), P(), P(), P(), P(), P()),
        check_vma=False,
    )
```
